256 devices in a mesh: row: 8 (over x_lo, y), col: 32 (over z, x_hi, core).
Axes of the slice: x: 4 (x_hi: 2, x_lo: 2; x = x_hi * 2 + x_lo), y: 4, z: 8, core: 2. Of those that a mesh axis runs over, the one named last changes fastest.
Arguments:
- state: float32 [2, 2048, 4096], P(None, 'row', 'col'), may hold values from -6 to 6
- cotangent: float32 [2, 2048, 4096], P(None, 'row', 'col'), may hold values from -6 to 6
- first_kernel: bfloat16 [18, 32], replicated, may hold values from -1.5 to 1.5
- first_bias: float32 [32], replicated, may hold values from -1 to 1
- second_kernel: bfloat16 [32, 18], replicated, may hold values from -1.5 to 1.5
Outputs:
- grad_state: float32 [2, 2048, 4096], P(None, 'row', 'col')
- grad_first: float32 [18, 32], replicated
- grad_second: float32 [32, 18], replicated
- grad_bias: float32 [32], replicated
The draws below stay inside these ranges and needn't reach their ends.
All inputs are finite; a program needn't handle non-finite values.
Results may differ from the reference program's by a relative error of at most 0.0047.
Values sent between devices are 32-bit elements; how exact they have to be, the bound alone decides.
No kernel may reach another device: no remote copies, remote signals or barrier semaphores. Data moves between devices by JAX's collectives and lax.ppermute only.
A program may use at most 64 MiB of HBM per device.

```python
import math
import jax
import jax.numpy as jnp
from jax import lax

FEATS = 32
NX = 2048
NY = 4096


def draw_cotangent(key, part):
    values = jax.random.truncated_normal(key, -4.0, 4.0, (2, NX, NY), jnp.float32)
    return values


def block_levels(key, extent, split, least, top_value):
    level = 1.0
    for dim, blocks in split:
        steps = jax.random.uniform(jax.random.fold_in(jax.random.fold_in(key, 6), dim), (blocks,), jnp.float32, least / len(split), top_value / len(split))
        level = level * jnp.repeat(jnp.exp(steps), extent[dim] // blocks).reshape((-1,) + (1,) * (len(extent) - 1 - dim))
    return level


def bell_draw(own_key, extent, deviation, bound, cuts=(), held_as=jnp.bfloat16):
    values = deviation * jax.random.normal(own_key, extent, jnp.float32)
    if cuts:
        values = values * block_levels(own_key, extent, cuts, -0.22, 0.18)
    return jnp.clip(values, -bound, bound).astype(held_as)


def setup_inputs(seed: int = 0) -> dict:
    keys = jax.random.split(jax.random.key(seed), 6)
    state = bell_draw(keys[0], (2, NX, NY), 1.0, 6.0, ((1, 8), (2, 32)), jnp.float32)
    cotangent = draw_cotangent(jax.random.fold_in(keys[5], 71), 0)
    first_kernel = bell_draw(keys[2], (18, FEATS), 18 ** -0.5, 1.5)
    first_bias = jnp.clip(jax.random.uniform(keys[3], (FEATS,), jnp.float32, -1.0, 1.0), -1.0, 1.0)
    second_kernel = bell_draw(keys[4], (FEATS, 18), (FEATS // 2) ** -0.5, 1.5)
    return dict(state=state, cotangent=cotangent, first_kernel=first_kernel, first_bias=first_bias, second_kernel=second_kernel)


step_size = 0.1
viscosity = 1.0

def project_field(cotangent):
    spectrum = jnp.fft.rfft2(cotangent, axes=(1, 2))
    wave_x = jnp.fft.fftfreq(NX).astype(cotangent.dtype)[:, None]
    wave_y = jnp.fft.rfftfreq(NY).astype(cotangent.dtype)[None, :]
    size_sq = wave_x * wave_x + wave_y * wave_y
    inverse = jnp.where(size_sq > 0, 1.0 / jnp.where(size_sq > 0, size_sq, 1.0), 0.0)
    nyquist = (jnp.abs(wave_x) == 0.5) | (jnp.abs(wave_y) == 0.5)
    cross = jnp.where(nyquist, 0.0, 1.0).astype(cotangent.dtype)
    first = spectrum[0] - wave_x * (wave_x * spectrum[0] + cross * wave_y * spectrum[1]) * inverse
    second = spectrum[1] - wave_y * (cross * wave_x * spectrum[0] + wave_y * spectrum[1]) * inverse
    kept = jnp.stack([first, second])
    return jnp.fft.irfft2(kept, s=(NX, NY), axes=(1, 2)).astype(cotangent.dtype)

def transport_grad(state_ext, scaled_ext):

    def middle(values):
        return values[:, 1:-1, 1:-1]

    def along_rows(values):
        return 0.5 * (values[:, 2:, 1:-1] - values[:, :-2, 1:-1])

    def along_cols(values):
        return 0.5 * (values[:, 1:-1, 2:] - values[:, 1:-1, :-2])
    carried = along_rows(state_ext[0:1] * scaled_ext) + along_cols(state_ext[1:2] * scaled_ext)
    centre = middle(scaled_ext)
    coupling = jnp.stack([-lax.optimization_barrier(jnp.sum(centre * along_rows(state_ext), 0)), -lax.optimization_barrier(jnp.sum(centre * along_cols(state_ext), 0))])
    laplace = scaled_ext[:, 2:, 1:-1] + scaled_ext[:, :-2, 1:-1] + scaled_ext[:, 1:-1, 2:] + scaled_ext[:, 1:-1, :-2] - 4.0 * centre
    return carried + coupling + viscosity * laplace

def forward_taps(values, height, breadth):
    pieces = [values[:, shift_row:shift_row + height, shift_col:shift_col + breadth] for shift_row in range(3) for shift_col in range(3)]
    return jnp.concatenate(pieces, 0)

def backward_taps(values, height, breadth):
    pieces = [values[:, 2 - shift_row:2 - shift_row + height, 2 - shift_col:2 - shift_col + breadth] for shift_row in range(3) for shift_col in range(3)]
    return jnp.concatenate(pieces, 0)

def fold_taps(spread, height, breadth):
    folded = jnp.zeros((2, height, breadth), jnp.float32)
    for shift_row in range(3):
        for shift_col in range(3):
            tap_number = 3 * shift_row + shift_col
            folded = folded + spread[2 * tap_number:2 * tap_number + 2, 2 - shift_row:2 - shift_row + height, 2 - shift_col:2 - shift_col + breadth]
    return folded

def interior(values, margin):
    inner_part = values[:, margin:values.shape[1] - margin, margin:values.shape[2] - margin]
    return inner_part.reshape(values.shape[0], -1)

def closure_block(state_part, scaled_part, first_kernel, first_bias, second_kernel, margin):
    height = state_part.shape[1] - 2
    breadth = state_part.shape[2] - 2
    cell_count = height * breadth
    taps_ahead = forward_taps(state_part, height, breadth)
    behind = backward_taps(scaled_part, height, breadth)
    preact = jnp.dot(first_kernel.T, taps_ahead.reshape(-1, cell_count), preferred_element_type=jnp.float32) + first_bias[:, None]
    active = jnp.tanh(preact)
    hidden = active.astype(jnp.bfloat16)
    hidden_grad = jnp.dot(second_kernel, behind.reshape(-1, cell_count), preferred_element_type=jnp.float32)
    pre_grad = (hidden_grad * (1.0 - active * active)).astype(jnp.bfloat16)
    spread = jnp.dot(first_kernel, pre_grad, preferred_element_type=jnp.float32).reshape(-1, height, breadth)
    inner_ahead = interior(taps_ahead, margin)
    inner_grad = interior(pre_grad.reshape(-1, height, breadth), margin)
    inner_hidden = interior(hidden.reshape(-1, height, breadth), margin)
    inner_behind = interior(behind, margin)
    part_first = jnp.dot(inner_ahead, inner_grad.T, preferred_element_type=jnp.float32)
    part_second = jnp.dot(inner_hidden, inner_behind.T, preferred_element_type=jnp.float32)
    part_bias = lax.optimization_barrier(jnp.sum(inner_grad.astype(jnp.float32), 1))
    return (spread, (part_first, part_second, part_bias))

def reference(state, cotangent, first_kernel, first_bias, second_kernel):
    projected = project_field(cotangent)
    scaled = step_size * projected
    state_cycle = jnp.pad(state, ((0, 0), (1, 1), (1, 1)), mode='wrap')
    scaled_cycle = jnp.pad(scaled, ((0, 0), (1, 1), (1, 1)), mode='wrap')
    transport = transport_grad(state_cycle, scaled_cycle)
    state_low = jnp.pad(state.astype(jnp.bfloat16), ((0, 0), (2, 2), (2, 2)), mode='wrap')
    scaled_low = jnp.pad(scaled.astype(jnp.bfloat16), ((0, 0), (2, 2), (2, 2)), mode='wrap')
    block_rows = 128 if NX % 128 == 0 else NX
    starts = jnp.arange(NX // block_rows, dtype=jnp.int32) * block_rows

    def one_block(offset):
        state_part = lax.dynamic_slice_in_dim(state_low, offset, block_rows + 4, 1)
        scaled_part = lax.dynamic_slice_in_dim(scaled_low, offset, block_rows + 4, 1)
        spread, partials = closure_block(state_part, scaled_part, first_kernel, first_bias, second_kernel, 1)
        return (fold_taps(spread, block_rows, NY), partials)
    folded, partials = lax.map(one_block, starts)
    closure = jnp.swapaxes(folded, 0, 1).reshape(2, NX, NY)
    norm_factor = 1.0 / math.sqrt(NX * NY)
    grad_first = lax.optimization_barrier(jnp.sum(partials[0], 0)) * norm_factor
    grad_second = lax.optimization_barrier(jnp.sum(partials[1], 0)) * norm_factor
    grad_bias = lax.optimization_barrier(jnp.sum(partials[2], 0)) * norm_factor
    return (projected + transport + closure, grad_first, grad_second, grad_bias)
```

```python
import math

import jax
import jax.numpy as jnp
import numpy as np
from jax import lax
from jax.experimental import pallas as pl
from jax.experimental.pallas import tpu as pltpu
from jax.sharding import PartitionSpec as P

NX, NY = 2048, 4096
ROWS, COLS = 8, 32
DEV = ROWS * COLS
FEATS = 32
WIDE = 24
f32, bf16 = jnp.float32, jnp.bfloat16
STEP = 0.1
NT = (((1,), (1,)), ((), ()))
NN = (((1,), (0,)), ((), ()))


def pair(table):
    high = table.astype(jnp.bfloat16)
    low = (table - high.astype(np.float64)).astype(jnp.bfloat16)
    return np.stack([high, low])


def tables():
    index = np.arange(256)
    angle = 2 * np.pi * (np.outer(index, index) % 256) / 256
    dft = np.concatenate([pair(np.cos(angle)), pair(np.sin(angle))])
    small = 2 * np.pi * (np.outer(np.arange(16), np.arange(16)) % 16) / 16
    eye = np.eye(8)
    group = np.concatenate([np.kron(eye, np.cos(small)), np.kron(eye, np.sin(small))], 1)
    twist_y = 2 * np.pi * np.outer(index, np.arange(128) % 16) / NY
    twist_x = 2 * np.pi * np.outer(np.arange(1, 5), index) / NX
    return dict(
        dft=dft,
        group=pair(group),
        twist_y=np.stack([np.cos(twist_y), np.sin(twist_y)]).astype(np.float32),
        twist_x=np.concatenate([np.cos(twist_x), np.sin(twist_x)]).astype(np.float32),
    )


def picks():
    first = np.zeros((18, 256))
    second = np.zeros((18, 256))
    out_first = np.zeros((256, 128))
    out_second = np.zeros((256, 128))
    for a in range(3):
        for b in range(3):
            for c in range(2):
                row = 2 * (3 * a + b) + c
                lane = (2 * a + c) * WIDE
                first[row, lane + b] = 1
                second[row, lane + 2 - b] = 1
                out_first[lane + b, row] = 1
                out_second[lane + 2 - b, 32 + row] = 1
    out_first[6 * WIDE, 18] = 1
    return [x.astype(jnp.bfloat16) for x in (first, second, out_first, out_second)]


def split(values):
    high = values.astype(bf16)
    return high, (values - high.astype(f32)).astype(bf16)


def dot(left, right, dims=NN):
    return lax.dot_general(left, right, dims, preferred_element_type=f32)


def left_dot(table_ref, base, values, dims=NN, keep=None):
    high, low = split(values)
    t_high, t_low = table_ref[base], table_ref[base + 1]
    if keep is not None:
        t_high, t_low = t_high[:, :keep], t_low[:, :keep]
    return dot(t_high, high, dims) + (dot(t_high, low, dims) + dot(t_low, high, dims))


def right_dot(values, table_ref):
    high, low = split(values)
    return dot(high, table_ref[0]) + (dot(low, table_ref[0]) + dot(high, table_ref[1]))


def pack_kernel(cot_ref, state_ref, out_ref):
    for f, ref in enumerate((cot_ref, state_ref)):
        for c in range(2):
            turned = ref[c].T
            row = (2 * f + c) * 16
            for r in range(ROWS):
                out_ref[r, row : row + 16, :] = turned[16 * r : 16 * r + 16]


def ahead_kernel(in_ref, dft_ref, twist_ref, out_ref, low_ref, high_ref):
    u = [in_ref[r, 0:32, :] for r in range(8)]
    root = math.sqrt(0.5)
    a, b, c, d = (u[k] - u[k + 4] for k in range(4))
    e0, e1, e2, e3 = (u[k] + u[k + 4] for k in range(4))
    s0, s1 = e0 + e2, e1 + e3
    parts = [
        (a + root * (b - d), -c - root * (b + d)),
        (e0 - e2, e3 - e1),
        (a - root * (b - d), c - root * (b + d)),
    ]
    reals, imags = [], []
    for k, (re, im) in enumerate(parts):
        cos, sin = twist_ref[k : k + 1, :], twist_ref[4 + k : 5 + k, :]
        reals.append(re * cos + im * sin)
        imags.append(im * cos - re * sin)
    even, odd = s0 + s1, s0 - s1
    zero = jnp.zeros_like(even)
    last_re = odd * twist_ref[3:4, :]
    last_im = -odd * twist_ref[7:8, :]
    stack = jnp.concatenate(
        reals + [even] + imags + [zero] + [zero] * 3 + [last_re] + [zero] * 3 + [last_im], 0
    )
    cosine = left_dot(dft_ref, 0, stack, NT)
    sine = left_dot(dft_ref, 2, stack, NT)
    main_re = cosine[:, 0:128] + sine[:, 128:256]
    main_im = cosine[:, 128:256] - sine[:, 0:128]
    odd_re = cosine[:128, 256:384] + sine[:128, 384:512]
    odd_im = cosine[:128, 384:512] - sine[:128, 256:384]
    lane = lax.broadcasted_iota(jnp.int32, (128, 128), 1)
    row = lax.broadcasted_iota(jnp.int32, (128, 128), 0)
    last = lane >= 96
    edge = last & (row == 0)
    top_re = jnp.where(edge, main_re[128:129], main_re[:128])
    top_im = jnp.where(edge, main_re[0:1], main_im[:128])
    out_ref[pl.ds(0, 128, 2), :] = top_re
    out_ref[pl.ds(1, 128, 2), :] = top_im
    out_ref[pl.ds(256, 128, 2), :] = jnp.where(last, odd_re, main_re[128:])
    out_ref[pl.ds(257, 128, 2), :] = jnp.where(last, odd_im, main_im[128:])
    for r in range(8):
        for ch in range(2):
            row0 = 32 + 16 * ch
            low_ref[2 * ch : 2 * ch + 2, 256 * r : 256 * r + 256] = in_ref[r, row0 : row0 + 2, :]
            high_ref[2 * ch : 2 * ch + 2, 256 * r : 256 * r + 256] = in_ref[
                r, row0 + 14 : row0 + 16, :
            ]


def waves(place):
    lane = lax.broadcasted_iota(jnp.int32, (256, 128), 1)
    row = lax.broadcasted_iota(jnp.int32, (256, 128), 0)
    slot = lane // 32
    plain = 8 * place + slot + 1
    last = jnp.where(place == 0, NX // 2, jnp.where(place < 128, 8 * place, 8 * place - 1020))
    mx = jnp.where(slot == 3, last, plain)
    mx = jnp.where(mx >= NX // 2, mx - NX, mx)
    my = row + 256 * (lane % 16)
    my = jnp.where(my >= NY // 2, my - NY, my)
    kx = mx.astype(f32) * (1.0 / NX)
    ky = my.astype(f32) * (1.0 / NY)
    inverse = 1.0 / (kx * kx + ky * ky)
    cross = jnp.where((mx == -(NX // 2)) | (my == -(NY // 2)), 0.0, kx * ky)
    own = jnp.where((lane & 16) == 0, kx * kx, ky * ky)
    return 1.0 - own * inverse, -cross * inverse, lane


def swap16(values, lane):
    return jnp.where((lane & 16) == 0, pltpu.roll(values, 112, 1), pltpu.roll(values, 16, 1))


def middle_kernel(place_ref, in_ref, dft_ref, group_ref, twist_ref, out_ref):
    place = place_ref[0]
    re, im = in_ref[pl.ds(0, 256, 2), :], in_ref[pl.ds(1, 256, 2), :]
    cos, sin = twist_ref[0], twist_ref[1]
    both = jnp.concatenate([re, im], 1)
    cosine, sine = left_dot(dft_ref, 0, both), left_dot(dft_ref, 2, both)
    f_re, f_im = cosine[:, :128] + sine[:, 128:], cosine[:, 128:] - sine[:, :128]
    t_re, t_im = f_re * cos + f_im * sin, f_im * cos - f_re * sin
    g = right_dot(jnp.concatenate([t_re, t_im], 0), group_ref)
    g_re, g_im = g[:256, :128] + g[256:, 128:], g[256:, :128] - g[:256, 128:]
    keep, mix, lane = waves(place)
    p_re = keep * g_re + mix * swap16(g_re, lane)
    p_im = keep * g_im + mix * swap16(g_im, lane)
    h = right_dot(jnp.concatenate([p_re, p_im], 0), group_ref)
    h_re, h_im = h[:256, :128] - h[256:, 128:], h[256:, :128] + h[:256, 128:]
    t_re, t_im = h_re * cos - h_im * sin, h_im * cos + h_re * sin
    both = jnp.concatenate([t_re, t_im], 1)
    cosine, sine = left_dot(dft_ref, 0, both), left_dot(dft_ref, 2, both)
    scale = 1.0 / (NX * NY)
    o_re = (cosine[:, :128] - sine[:, 128:]) * scale
    o_im = (cosine[:, 128:] + sine[:, :128]) * scale
    sums = jnp.sum(im, 0, keepdims=True)
    sums = jnp.where(lane[:1] >= 112, sums, 0.0)
    mean = jnp.sum(sums, 1, keepdims=True) * scale
    zeroth = (lane >= 96) & (place == 0)
    o_im = jnp.where(zeroth, jnp.where(lane >= 112, mean, im * (1.0 / NX)), o_im)
    near = (lane & 8) == 0
    out_ref[pl.ds(0, 256, 4), :] = o_re
    out_ref[pl.ds(1, 256, 4), :] = o_im
    out_ref[pl.ds(2, 256, 4), :] = jnp.where(near, pltpu.roll(o_re, 255, 0), pltpu.roll(o_re, 1, 0))
    out_ref[pl.ds(3, 256, 4), :] = jnp.where(near, pltpu.roll(o_im, 255, 0), pltpu.roll(o_im, 1, 0))


def back_kernel(in_ref, dft_ref, twist_ref, out_ref):
    lane = lax.broadcasted_iota(jnp.int32, (128, 128), 1)
    row = lax.broadcasted_iota(jnp.int32, (128, 128), 0)
    last = lane >= 96
    edge = last & (row == 0)
    mains, odds = [], []
    for k in (0, 2):
        top_re, top_im = in_ref[pl.ds(k, 128, 4), :], in_ref[pl.ds(k + 1, 128, 4), :]
        low_re, low_im = in_ref[pl.ds(512 + k, 128, 4), :], in_ref[pl.ds(513 + k, 128, 4), :]
        nyquist = jnp.where(edge, 0.5 * top_re[0:1], 0.0)
        main_re = jnp.concatenate(
            [jnp.where(edge, 0.5 * top_im, top_re), jnp.where(last, nyquist, low_re)], 0
        )
        main_im = jnp.concatenate(
            [jnp.where(edge, 0.0, top_im), jnp.where(last, 0.0, low_im)], 0
        )
        mains += [main_re, main_im]
        odds += [low_re, low_im]
    main = jnp.concatenate(mains, 1).T
    odd = jnp.concatenate(odds, 1).T
    m_high, m_low = split(main)
    o_high, o_low = split(odd)

    def turn(high, low, base, keep):
        t_high, t_low = dft_ref[base][:keep], dft_ref[base + 1][:keep]
        return dot(high, t_high) + (dot(low, t_high) + dot(high, t_low))

    m_cos, m_sin = turn(m_high, m_low, 0, 256), turn(m_high, m_low, 2, 256)
    o_cos, o_sin = turn(o_high, o_low, 0, 128), turn(o_high, o_low, 2, 128)
    root = math.sqrt(0.5)
    for k in (0, 256):
        re = m_cos[k : k + 128] - m_sin[k + 128 : k + 256]
        im = m_cos[k + 128 : k + 256] + m_sin[k : k + 128]
        last_re = o_cos[k + 96 : k + 128] - o_sin[k + 224 : k + 256]
        last_im = o_cos[k + 224 : k + 256] + o_sin[k + 96 : k + 128]
        w4 = last_re * twist_ref[3:4, :] - last_im * twist_ref[7:8, :]
        w0 = re[96:128]
        ws = []
        for p in range(3):
            cos, sin = twist_ref[p : p + 1, :], twist_ref[4 + p : 5 + p, :]
            r_p, i_p = re[32 * p : 32 * p + 32], im[32 * p : 32 * p + 32]
            ws.append((r_p * cos - i_p * sin, i_p * cos + r_p * sin))
        for r in range(8):
            total = w0 + w4 if r % 2 == 0 else w0 - w4
            for p in range(3):
                turn_by = (r * (p + 1)) % 8
                cos_r = [1.0, root, 0.0, -root, -1.0, -root, 0.0, root][turn_by]
                sin_r = [0.0, root, 1.0, root, 0.0, -root, -1.0, -root][turn_by]
                if cos_r:
                    total = total + cos_r * ws[p][0]
                if sin_r:
                    total = total - sin_r * ws[p][1]
            total = total + total
            lanes = slice(256 * r, 256 * r + 256)
            for ch in range(2):
                if k == 0:
                    out_ref[ch, 2:18, lanes] = total[16 * ch : 16 * ch + 16]
                else:
                    out_ref[ch, 0:2, lanes] = total[16 * ch + 14 : 16 * ch + 16]
                    out_ref[ch, 18:20, lanes] = total[16 * ch : 16 * ch + 2]
                    if r == 0:
                        out_ref[ch, 20:24, :] = jnp.zeros((4, NX), f32)


def closure_kernel(
    proj_ref, own_ref, before_ref, after_ref, first_ref, bias_ref, second_ref,
    pick1_ref, pick2_ref, take1_ref, take2_ref,
    out_ref,
    field_ref, build_ref, state_low, scaled_low, grads, acts, w1_ref, w2_ref,
):
    lane = lax.broadcasted_iota(jnp.int32, (FEATS, 256), 1)
    bias = bias_ref[...]
    bias_high = bias.astype(bf16).astype(f32)
    bias_part = jnp.where(
        lane == 6 * WIDE, bias_high, jnp.where(lane == 6 * WIDE + 1, bias - bias_high, 0.0)
    )
    base1 = dot(first_ref[...].astype(f32).T.astype(bf16), pick1_ref[...])
    base2 = dot(second_ref[...], pick2_ref[...])
    for j in range(18):
        rows = slice(32 * j, 32 * j + 32)
        moved1 = pltpu.roll(base1, j, 1) if j else base1
        moved2 = pltpu.roll(base2, j, 1) if j else base2
        w1_ref[rows, :] = moved1 + bias_part
        w2_ref[rows, :] = moved2.astype(bf16)
    for c in range(2):
        field_ref[c, 20:24, :] = jnp.zeros((4, NX), f32)
        for r in range(8):
            field_ref[c, 2:18, 256 * r : 256 * r + 256] = own_ref[
                r, 32 + 16 * c : 48 + 16 * c, :
            ]
        field_ref[c, 0:2, :] = before_ref[2 * c : 2 * c + 2, :]
        field_ref[c, 18:20, :] = after_ref[2 * c : 2 * c + 2, :]

    def ahead(values):
        return pltpu.roll(values, NX - 1, 1)

    def behind(values):
        return pltpu.roll(values, 1, 1)

    for target, sign in ((state_low, 1), (scaled_low, -1)):
        for c in range(2):
            whole = field_ref[c] if sign == 1 else STEP * proj_ref[c]
            moves = (behind(whole), whole, ahead(whole))[::sign]
            for a in range(3):
                row = (2 * a + c) * WIDE
                build_ref[row : row + WIDE, :] = moves[a]
        build_ref[144:152, :] = jnp.ones((8, NX), f32)
        build_ref[152:160, :] = jnp.zeros((8, NX), f32)
        target[0:160, :] = build_ref[...].astype(bf16)
        target[160:256, :] = jnp.zeros((96, NX), bf16)

    w1 = w1_ref[...]
    w1_low = w1[:, :160].astype(bf16)
    w1_turn = w1.T[:160].astype(bf16)
    w2_low = w2_ref[:, :160]
    size = 256

    def chunk(k, carry):
        cols = pl.ds(pl.multiple_of(k * size, size), size)
        preact = dot(w1_low, state_low[0:160, cols])
        active = jnp.tanh(preact)
        acts[:, cols] = active.astype(bf16)
        back = dot(w2_low, scaled_low[0:160, cols])
        grads[:, cols] = (back * (1.0 - active * active)).astype(bf16)
        build_ref[:, cols] = dot(w1_turn, grads[:, cols])
        return carry

    lax.fori_loop(0, NX // size, chunk, 0)
    first_sums = dot(grads[32:544, :], state_low[...], NT)
    second_sums = dot(acts[32:544, :], scaled_low[...], NT)
    total1 = total2 = plain = jnp.zeros((FEATS, 256), f32)
    for j in range(16):
        rows = slice(32 * j, 32 * j + 32)
        total1 = total1 + pltpu.roll(first_sums[rows], 255 - j, 1)
        total2 = total2 + pltpu.roll(second_sums[rows], 255 - j, 1)
        plain = plain + first_sums[rows]
    total1 = jnp.where(lane >= 6 * WIDE, plain, total1)
    high1, low1 = split(total1)
    high2, low2 = split(total2)
    packed = (dot(high1, take1_ref[...]) + dot(low1, take1_ref[...])) + (
        dot(high2, take2_ref[...]) + dot(low2, take2_ref[...])
    )
    left = packed[0:8] + pltpu.roll(packed[8:16], 64, 1)
    right = packed[16:24] + pltpu.roll(packed[24:32], 64, 1)
    for r in range(8):
        out_ref[r, 32:40, 0:128] = left
        out_ref[r, 32:40, 128:256] = right

    inner, up, down = slice(2, 18), slice(3, 19), slice(1, 17)
    su, sv = field_ref[0, inner, :], field_ref[1, inner, :]
    centre = [STEP * proj_ref[c, inner, :] for c in range(2)]
    coupling = [None, None]
    for c, mine in enumerate((su, sv)):
        along_x = 0.5 * (ahead(mine) - behind(mine))
        along_y = 0.5 * (field_ref[c, up, :] - field_ref[c, down, :])
        coupling[0] = centre[c] * along_x + (coupling[0] if c else 0.0)
        coupling[1] = centre[c] * along_y + (coupling[1] if c else 0.0)
    for c in range(2):
        mine = centre[c]
        above = STEP * proj_ref[c, up, :]
        below = STEP * proj_ref[c, down, :]
        carried = su * mine
        total = 0.5 * (ahead(carried) - behind(carried))
        total = total + 0.5 * (field_ref[1, up, :] * above - field_ref[1, down, :] * below)
        total = total - coupling[c]
        total = total + (ahead(mine) + behind(mine) + above + below - 4.0 * mine)
        total = total + proj_ref[c, inner, :]
        for a, move in enumerate((ahead, None, behind)):
            row = (2 * a + c) * WIDE
            part = build_ref[row + 2 : row + 18, :]
            total = total + (move(part) if move else part)
        for r in range(8):
            out_ref[r, 16 * c : 16 * c + 16, :] = total[:, 256 * r : 256 * r + 256]


def unpack_kernel(in_ref, out_ref, part_ref):
    for c in range(2):
        lines = jnp.concatenate([in_ref[r, 16 * c : 16 * c + 16, :] for r in range(8)], 0)
        out_ref[c] = lines.T
    total = in_ref[0, 32:40, :]
    for r in range(1, 8):
        total = total + in_ref[r, 32:40, :]
    part_ref[...] = jnp.broadcast_to(total[None], (COLS, 8, 256))


def sums_kernel(in_ref, first_ref, second_ref, bias_ref):
    total = in_ref[0]
    for r in range(1, COLS):
        total = total + in_ref[r]
    total = total * (1.0 / math.sqrt(NX * NY))
    left, right = total[:, 0:128], total[:, 128:256]
    whole = jnp.concatenate(
        [left, pltpu.roll(left, 64, 1), right, pltpu.roll(right, 64, 1)], 0
    )
    turned = whole.T
    first_ref[...] = turned[0:18, :]
    bias_ref[...] = turned[18:19, :]
    second_ref[...] = pltpu.roll(whole, 96, 1)[:, 0:18]


def call(kernel, outs, scratch=(), scalars=0, count=0, name=None):
    space = [pl.BlockSpec(memory_space=pltpu.SMEM)] * scalars
    space += [pl.BlockSpec(memory_space=pltpu.VMEM)] * (count - scalars)
    many = isinstance(outs, (list, tuple))
    out_space = pl.BlockSpec(memory_space=pltpu.VMEM)
    return pl.pallas_call(
        kernel,
        out_shape=outs,
        in_specs=space,
        out_specs=[out_space] * len(outs) if many else out_space,
        scratch_shapes=list(scratch),
        compiler_params=pltpu.CompilerParams(vmem_limit_bytes=48 * 2**20),
        name=name,
    )


def shape(*dims, dtype=f32):
    return jax.ShapeDtypeStruct(dims, dtype)


def shards(state, cotangent, first_kernel, first_bias, second_kernel):
    t = tables()
    first_pick, second_pick, first_take, second_take = picks()
    dft = jnp.asarray(t["dft"])
    group = jnp.asarray(t["group"])
    twist_y = jnp.asarray(t["twist_y"])
    twist_x = jnp.asarray(t["twist_x"])
    every = ("col", "row")
    place = (lax.axis_index("col") * ROWS + lax.axis_index("row")).astype(jnp.int32).reshape(1)
    lanes = lax.broadcasted_iota(jnp.int32, (FEATS, 256), 1)
    bias = jnp.where(lanes >= 6 * WIDE, first_bias[:, None], 0.0)

    def exchange(values, axis):
        return lax.all_to_all(values, axis, 0, 0, tiled=True)

    packed = call(pack_kernel, shape(8, 64, 256), count=2, name="pack")(cotangent, state)
    lines = exchange(packed, "row")
    modes, low, high = call(
        ahead_kernel, [shape(512, 128), shape(4, NX), shape(4, NX)], count=3, name="ahead"
    )(lines, dft, twist_x)
    order = [(i % ROWS) * COLS + i // ROWS for i in range(DEV)]
    up = [(order[i], order[(i + 1) % DEV]) for i in range(DEV)]
    before = lax.ppermute(high, ("row", "col"), up)
    after = lax.ppermute(low, ("row", "col"), [(j, i) for i, j in up])
    modes = exchange(modes.reshape(DEV, 2, 128), every).reshape(512, 128)
    modes = call(middle_kernel, shape(1024, 128), scalars=1, count=5, name="middle")(
        place, modes, dft, group, twist_y
    )
    modes = exchange(modes.reshape(DEV, 4, 128), every).reshape(1024, 128)
    projected = call(back_kernel, shape(2, WIDE, NX), count=3, name="back")(modes, dft, twist_x)
    scratch = [
        pltpu.VMEM((2, WIDE, NX), f32),
        pltpu.VMEM((160, NX), f32),
        pltpu.VMEM((256, NX), bf16),
        pltpu.VMEM((256, NX), bf16),
        pltpu.VMEM((576, NX), bf16),
        pltpu.VMEM((576, NX), bf16),
        pltpu.VMEM((576, 256), f32),
        pltpu.VMEM((576, 256), bf16),
    ]
    result = call(closure_kernel, shape(8, 40, 256), scratch, count=11, name="closure")(
        projected, lines, before, after, first_kernel, bias, second_kernel,
        first_pick, second_pick, first_take, second_take,
    )
    result = exchange(result, "row")
    grad_state, part = call(
        unpack_kernel, [shape(2, 256, 128), shape(COLS, 8, 256)], count=1, name="unpack"
    )(result)
    part = exchange(part, "col")
    grad_first, grad_second, grad_bias = call(
        sums_kernel, [shape(18, 32), shape(32, 18), shape(1, 32)], count=1, name="sums"
    )(part)
    return grad_state, grad_first, grad_second, grad_bias.reshape(32)


def solution(mesh):
    placed = (P(None, "row", "col"), P(None, "row", "col"), P(), P(), P())
    return jax.shard_map(
        shards,
        mesh=mesh,
        in_specs=placed,
        out_specs=(P(None, "row", "col"), P(), P(), P()),
        check_vma=False,
    )
```

```python
import math

import jax
import jax.numpy as jnp
import numpy as np
from jax import lax
from jax.experimental import pallas as pl
from jax.experimental.pallas import tpu as pltpu
from jax.sharding import PartitionSpec as P

NX, NY = 2048, 4096
ROWS, COLS = 8, 32
DEV = ROWS * COLS
FEATS = 32
WIDE = 24
f32, bf16 = jnp.float32, jnp.bfloat16
STEP = 0.1
NT = (((1,), (1,)), ((), ()))
NN = (((1,), (0,)), ((), ()))


def pair(table):
    high = table.astype(jnp.bfloat16)
    low = (table - high.astype(np.float64)).astype(jnp.bfloat16)
    return np.stack([high, low])


def tables():
    index = np.arange(256)
    angle = 2 * np.pi * (np.outer(index, index) % 256) / 256
    dft = np.concatenate([pair(np.cos(angle)), pair(np.sin(angle))])
    small = 2 * np.pi * (np.outer(np.arange(16), np.arange(16)) % 16) / 16
    eye = np.eye(8)
    group = np.concatenate([np.kron(eye, np.cos(small)), np.kron(eye, np.sin(small))], 1)
    twist_y = 2 * np.pi * np.outer(index, np.arange(128) % 16) / NY
    twist_x = 2 * np.pi * np.outer(np.arange(1, 5), index) / NX
    return dict(
        dft=dft,
        group=pair(group),
        twist_y=np.stack([np.cos(twist_y), np.sin(twist_y)]).astype(np.float32),
        twist_x=np.concatenate([np.cos(twist_x), np.sin(twist_x)]).astype(np.float32),
    )


def picks():
    first = np.zeros((18, 256))
    second = np.zeros((18, 256))
    out_first = np.zeros((256, 128))
    out_second = np.zeros((256, 128))
    for a in range(3):
        for b in range(3):
            for c in range(2):
                row = 2 * (3 * a + b) + c
                lane = (2 * a + c) * WIDE
                first[row, lane + b] = 1
                second[row, lane + 2 - b] = 1
                out_first[lane + b, row] = 1
                out_second[lane + 2 - b, 19 + row] = 1
    out_first[6 * WIDE, 18] = 1
    return [x.astype(jnp.bfloat16) for x in (first, second, out_first, out_second)]


def split(values):
    high = values.astype(bf16)
    return high, (values - high.astype(f32)).astype(bf16)


def dot(left, right, dims=NN):
    return lax.dot_general(left, right, dims, preferred_element_type=f32)


def left_dot(table_ref, base, values, dims=NN, keep=None):
    high, low = split(values)
    t_high, t_low = table_ref[base], table_ref[base + 1]
    if keep is not None:
        t_high, t_low = t_high[:, :keep], t_low[:, :keep]
    return dot(t_high, high, dims) + (dot(t_high, low, dims) + dot(t_low, high, dims))


def right_dot(values, table_ref):
    high, low = split(values)
    return dot(high, table_ref[0]) + (dot(low, table_ref[0]) + dot(high, table_ref[1]))


def far(values):
    return pltpu.with_memory_space_constraint(values, pltpu.HBM)


def fetch(sources, targets, sems):
    copies = [
        pltpu.make_async_copy(source, target, sems.at[k])
        for k, (source, target) in enumerate(zip(sources, targets))
    ]
    for copy in copies:
        copy.start()
    return copies


def pack_kernel(cot_ref, state_ref, out_ref, buffer_ref, sems):
    copies = []
    for f, ref in enumerate((cot_ref, state_ref)):
        for c in range(2):
            k = 2 * f + c
            copies.append(pltpu.make_async_copy(ref.at[c], buffer_ref.at[k], sems.at[k]))
    for copy in copies:
        copy.start()
    for k, copy in enumerate(copies):
        copy.wait()
        turned = buffer_ref[k].T
        for r in range(ROWS):
            out_ref[r, 16 * k : 16 * k + 16, :] = turned[16 * r : 16 * r + 16]


def ahead_kernel(
    dft_far, twist_far, in_ref, out_ref, low_ref, high_ref, dft_ref, twist_ref, sems
):
    copies = fetch((twist_far, dft_far), (twist_ref, dft_ref), sems)
    u = [in_ref[r, 0:32, :] for r in range(8)]
    root = math.sqrt(0.5)
    a, b, c, d = (u[k] - u[k + 4] for k in range(4))
    e0, e1, e2, e3 = (u[k] + u[k + 4] for k in range(4))
    s0, s1 = e0 + e2, e1 + e3
    parts = [
        (a + root * (b - d), -c - root * (b + d)),
        (e0 - e2, e3 - e1),
        (a - root * (b - d), c - root * (b + d)),
    ]
    copies[0].wait()
    reals, imags = [], []
    for k, (re, im) in enumerate(parts):
        cos, sin = twist_ref[k : k + 1, :], twist_ref[4 + k : 5 + k, :]
        reals.append(re * cos + im * sin)
        imags.append(im * cos - re * sin)
    even, odd = s0 + s1, s0 - s1
    zero = jnp.zeros_like(even)
    last_re = odd * twist_ref[3:4, :]
    last_im = -odd * twist_ref[7:8, :]
    stack = jnp.concatenate(
        reals + [even] + imags + [zero] + [zero] * 3 + [last_re] + [zero] * 3 + [last_im], 0
    )
    copies[1].wait()
    cosine = left_dot(dft_ref, 0, stack, NT)
    sine = left_dot(dft_ref, 2, stack, NT)
    main_re = cosine[:, 0:128] + sine[:, 128:256]
    main_im = cosine[:, 128:256] - sine[:, 0:128]
    odd_re = cosine[:128, 256:384] + sine[:128, 384:512]
    odd_im = cosine[:128, 384:512] - sine[:128, 256:384]
    lane = lax.broadcasted_iota(jnp.int32, (128, 128), 1)
    row = lax.broadcasted_iota(jnp.int32, (128, 128), 0)
    last = lane >= 96
    edge = last & (row == 0)
    top_re = jnp.where(edge, main_re[128:129], main_re[:128])
    top_im = jnp.where(edge, main_re[0:1], main_im[:128])
    out_ref[pl.ds(0, 128, 2), :] = top_re
    out_ref[pl.ds(1, 128, 2), :] = top_im
    out_ref[pl.ds(256, 128, 2), :] = jnp.where(last, odd_re, main_re[128:])
    out_ref[pl.ds(257, 128, 2), :] = jnp.where(last, odd_im, main_im[128:])
    for r in range(8):
        for ch in range(2):
            row0 = 32 + 16 * ch
            low_ref[2 * ch : 2 * ch + 2, 256 * r : 256 * r + 256] = in_ref[r, row0 : row0 + 2, :]
            high_ref[2 * ch : 2 * ch + 2, 256 * r : 256 * r + 256] = in_ref[
                r, row0 + 14 : row0 + 16, :
            ]


def waves_kernel(place_ref, keep_ref, mix_ref):
    place = place_ref[0]
    lane = lax.broadcasted_iota(jnp.int32, (256, 128), 1)
    row = lax.broadcasted_iota(jnp.int32, (256, 128), 0)
    slot = lane // 32
    plain = 8 * place + slot + 1
    last = jnp.where(place == 0, NX // 2, jnp.where(place < 128, 8 * place, 8 * place - 1020))
    mx = jnp.where(slot == 3, last, plain)
    mx = jnp.where(mx >= NX // 2, mx - NX, mx)
    my = row + 256 * (lane % 16)
    my = jnp.where(my >= NY // 2, my - NY, my)
    kx = mx.astype(f32) * (1.0 / NX)
    ky = my.astype(f32) * (1.0 / NY)
    inverse = 1.0 / (kx * kx + ky * ky)
    cross = jnp.where((mx == -(NX // 2)) | (my == -(NY // 2)), 0.0, kx * ky)
    own = jnp.where((lane & 16) == 0, kx * kx, ky * ky)
    keep_ref[...] = 1.0 - own * inverse
    mix_ref[...] = -cross * inverse


def swap16(values, lane):
    return jnp.where((lane & 16) == 0, pltpu.roll(values, 112, 1), pltpu.roll(values, 16, 1))


def middle_kernel(
    place_ref, dft_far, twist_far, group_far, in_ref, keep_ref, mix_ref, out_ref,
    dft_ref, twist_ref, group_ref, sems,
):
    copies = fetch((dft_far, twist_far, group_far), (dft_ref, twist_ref, group_ref), sems)
    place = place_ref[0]
    re, im = in_ref[pl.ds(0, 256, 2), :], in_ref[pl.ds(1, 256, 2), :]
    both = jnp.concatenate([re, im], 1)
    copies[0].wait()
    cosine, sine = left_dot(dft_ref, 0, both), left_dot(dft_ref, 2, both)
    f_re, f_im = cosine[:, :128] + sine[:, 128:], cosine[:, 128:] - sine[:, :128]
    copies[1].wait()
    copies[2].wait()
    cos, sin = twist_ref[0], twist_ref[1]
    t_re, t_im = f_re * cos + f_im * sin, f_im * cos - f_re * sin
    g = right_dot(jnp.concatenate([t_re, t_im], 0), group_ref)
    g_re, g_im = g[:256, :128] + g[256:, 128:], g[256:, :128] - g[:256, 128:]
    keep, mix = keep_ref[...], mix_ref[...]
    lane = lax.broadcasted_iota(jnp.int32, (256, 128), 1)
    p_re = keep * g_re + mix * swap16(g_re, lane)
    p_im = keep * g_im + mix * swap16(g_im, lane)
    h = right_dot(jnp.concatenate([p_re, p_im], 0), group_ref)
    h_re, h_im = h[:256, :128] - h[256:, 128:], h[256:, :128] + h[:256, 128:]
    t_re, t_im = h_re * cos - h_im * sin, h_im * cos + h_re * sin
    both = jnp.concatenate([t_re, t_im], 1)
    cosine, sine = left_dot(dft_ref, 0, both), left_dot(dft_ref, 2, both)
    scale = 1.0 / (NX * NY)
    o_re = (cosine[:, :128] - sine[:, 128:]) * scale
    o_im = (cosine[:, 128:] + sine[:, :128]) * scale
    sums = jnp.sum(im, 0, keepdims=True)
    sums = jnp.where(lane[:1] >= 112, sums, 0.0)
    mean = jnp.sum(sums, 1, keepdims=True) * scale
    zeroth = (lane >= 96) & (place == 0)
    o_im = jnp.where(zeroth, jnp.where(lane >= 112, mean, im * (1.0 / NX)), o_im)
    near = (lane & 8) == 0
    outer = ((lane + 2) & 15) < 4

    def beside(values):
        return jnp.where(near, pltpu.roll(values, 255, 0), pltpu.roll(values, 1, 0))

    out_ref[pl.ds(0, 256, 3), :] = o_re
    out_ref[pl.ds(1, 256, 3), :] = o_im
    edge_im = beside(o_im)
    edge_im = jnp.where(near, pltpu.roll(edge_im, 4, 1), pltpu.roll(edge_im, 124, 1))
    out_ref[pl.ds(2, 256, 3), :] = jnp.where(outer, beside(o_re), edge_im)


def back_part(in_ref, dft_ref, twist_ref, out_ref, copies):
    lane = lax.broadcasted_iota(jnp.int32, (128, 128), 1)
    row = lax.broadcasted_iota(jnp.int32, (128, 128), 0)
    last = lane >= 96
    edge = last & (row == 0)
    near = (lane & 8) == 0
    outer = ((lane + 2) & 15) < 4
    top_re, top_im, top_h = (in_ref[pl.ds(k, 128, 3), :] for k in range(3))
    low_re, low_im, low_h = (in_ref[pl.ds(384 + k, 128, 3), :] for k in range(3))
    head = top_h[0:1]
    head_im = jnp.where(near[0:1], pltpu.roll(head, 124, 1), pltpu.roll(head, 4, 1))
    half_im = jnp.where(outer[0:1], 0.5 * head_im, 0.0)
    half_re = jnp.where(outer[0:1], 0.5 * head, 0.0)
    nyquist = jnp.where(edge, 0.5 * top_re[0:1], 0.0)
    mains = [
        jnp.concatenate(
            [jnp.where(edge, 0.5 * top_im, top_re), jnp.where(last, nyquist, low_re)], 0
        ),
        jnp.concatenate([jnp.where(edge, 0.0, top_im), jnp.where(last, 0.0, low_im)], 0),
        jnp.concatenate(
            [
                jnp.where(edge, half_im, top_h),
                jnp.where(last, jnp.where(edge, half_re, 0.0), low_h),
            ],
            0,
        ),
    ]
    m_high, m_low = split(jnp.concatenate(mains, 1).T)
    o_high, o_low = split(jnp.concatenate([low_re, low_im, low_h], 1).T)

    def turn(high, low, base, keep):
        t_high, t_low = dft_ref[base][:keep], dft_ref[base + 1][:keep]
        return dot(high, t_high) + (dot(low, t_high) + dot(high, t_low))

    for copy in copies:
        copy.wait()
    m_cos, m_sin = turn(m_high, m_low, 0, 256), turn(m_high, m_low, 2, 256)
    o_cos, o_sin = turn(o_high, o_low, 0, 128), turn(o_high, o_low, 2, 128)
    root = math.sqrt(0.5)
    near_row = (lax.broadcasted_iota(jnp.int32, (128, 256), 0) & 8) == 0

    def imag_rows(values):
        return jnp.where(near_row, pltpu.roll(values, 124, 0), pltpu.roll(values, 4, 0))

    for k in (0, 256):
        if k == 0:
            re, im = m_cos[0:128] - m_sin[128:256], m_cos[128:256] + m_sin[0:128]
            last_re, last_im = o_cos[96:128] - o_sin[224:256], o_cos[224:256] + o_sin[96:128]
        else:
            m_c, m_s, o_c, o_s = (v[256:384] for v in (m_cos, m_sin, o_cos, o_sin))
            re, im = m_c - imag_rows(m_s), imag_rows(m_c) + m_s
            last_re, last_im = (o_c - imag_rows(o_s))[96:], (imag_rows(o_c) + o_s)[96:]
        w4 = last_re * twist_ref[3:4, :] - last_im * twist_ref[7:8, :]
        w0 = re[96:128]
        ws = []
        for p in range(3):
            cos, sin = twist_ref[p : p + 1, :], twist_ref[4 + p : 5 + p, :]
            r_p, i_p = re[32 * p : 32 * p + 32], im[32 * p : 32 * p + 32]
            ws.append((r_p * cos - i_p * sin, i_p * cos + r_p * sin))
        for r in range(8):
            total = w0 + w4 if r % 2 == 0 else w0 - w4
            for p in range(3):
                turn_by = (r * (p + 1)) % 8
                cos_r = [1.0, root, 0.0, -root, -1.0, -root, 0.0, root][turn_by]
                sin_r = [0.0, root, 1.0, root, 0.0, -root, -1.0, -root][turn_by]
                if cos_r:
                    total = total + cos_r * ws[p][0]
                if sin_r:
                    total = total - sin_r * ws[p][1]
            total = total + total
            lanes = slice(256 * r, 256 * r + 256)
            for ch in range(2):
                if k == 0:
                    out_ref[ch, 2:18, lanes] = total[16 * ch : 16 * ch + 16]
                else:
                    out_ref[ch, 0:2, lanes] = total[16 * ch + 14 : 16 * ch + 16]
                    out_ref[ch, 18:20, lanes] = total[16 * ch : 16 * ch + 2]
                    if r == 0:
                        out_ref[ch, 20:24, :] = jnp.zeros((4, NX), f32)


def ahead_of(values):
    return pltpu.roll(values, NX - 1, 1)


def behind_of(values):
    return pltpu.roll(values, 1, 1)


def fill_taps(build_ref, target, fields, sign):
    for c in range(2):
        whole = fields[c]
        moves = (behind_of(whole), whole, ahead_of(whole))[::sign]
        for a in range(3):
            row = (2 * a + c) * WIDE
            build_ref[row : row + WIDE, :] = moves[a]
    build_ref[144:152, :] = jnp.ones((8, NX), f32)
    build_ref[152:160, :] = jnp.zeros((8, NX), f32)
    target[0:160, :] = build_ref[...].astype(bf16)
    target[160:256, :] = jnp.zeros((96, NX), bf16)


CHUNK = 256


def state_kernel(
    own_ref, before_ref, after_ref, first_ref, bias_ref, second_ref, pick1_ref, pick2_ref,
    field_ref, slope_ref, state_low, acts, acts_turn, w2_ref, turn_ref,
    build_ref, w1_ref,
):
    lane = lax.broadcasted_iota(jnp.int32, (FEATS, 256), 1)
    bias = bias_ref[...]
    bias_high = bias.astype(bf16).astype(f32)
    bias_part = jnp.where(
        lane == 6 * WIDE, bias_high, jnp.where(lane == 6 * WIDE + 1, bias - bias_high, 0.0)
    )
    base1 = dot(first_ref[...].astype(f32).T.astype(bf16), pick1_ref[...])
    base2 = dot(second_ref[...], pick2_ref[...])
    for j in range(18):
        rows = slice(32 * j, 32 * j + 32)
        moved1 = pltpu.roll(base1, j, 1) if j else base1
        moved2 = pltpu.roll(base2, j, 1) if j else base2
        w1_ref[rows, :] = moved1 + bias_part
        w2_ref[rows, :] = moved2.astype(bf16)
    for c in range(2):
        field_ref[c, 20:24, :] = jnp.zeros((4, NX), f32)
        for r in range(8):
            field_ref[c, 2:18, 256 * r : 256 * r + 256] = own_ref[
                r, 32 + 16 * c : 48 + 16 * c, :
            ]
        field_ref[c, 0:2, :] = before_ref[2 * c : 2 * c + 2, :]
        field_ref[c, 18:20, :] = after_ref[2 * c : 2 * c + 2, :]
    fill_taps(build_ref, state_low, (field_ref[0], field_ref[1]), 1)
    for c in range(2):
        mine = field_ref[c, 2:18, :]
        slope_ref[2 * c] = 0.5 * (ahead_of(mine) - behind_of(mine))
        slope_ref[2 * c + 1] = 0.5 * (field_ref[c, 3:19, :] - field_ref[c, 1:17, :])
    w1 = w1_ref[...]
    turn_ref[...] = w1.T[:160].astype(bf16)
    w1_low = w1[:, :160].astype(bf16)

    def chunk(k, carry):
        cols = pl.ds(pl.multiple_of(k * CHUNK, CHUNK), CHUNK)
        active = jnp.tanh(dot(w1_low, state_low[0:160, cols]))
        acts[:, cols] = active[32:544].astype(bf16)
        acts_turn[:, cols] = 1.0 - active * active
        return carry

    lax.fori_loop(0, NX // CHUNK, chunk, 0)


def closure_kernel(
    dft_far, twist_far, w2_far, acts_turn_far, turn_far, state_far, acts_far,
    field_far, slope_far, take1_far, take2_far, in_ref,
    out_ref,
    dft_ref, twist_ref, w2_ref, acts_turn, turn_ref, state_low, acts,
    field_ref, slope_ref, take1_ref, take2_ref, sems,
    proj_ref, build_ref, scaled_low, grads,
):
    copies = fetch(
        (dft_far, twist_far, w2_far, acts_turn_far, turn_far, state_far, acts_far,
         field_far, slope_far, take1_far, take2_far),
        (dft_ref, twist_ref, w2_ref, acts_turn, turn_ref, state_low, acts,
         field_ref, slope_ref, take1_ref, take2_ref),
        sems,
    )
    back_part(in_ref, dft_ref, twist_ref, proj_ref, copies[:2])
    fill_taps(build_ref, scaled_low, (STEP * proj_ref[0], STEP * proj_ref[1]), -1)
    for copy in copies[2:5]:
        copy.wait()
    w2_low = w2_ref[:, :160]
    w1_turn = turn_ref[...]

    def chunk(k, carry):
        cols = pl.ds(pl.multiple_of(k * CHUNK, CHUNK), CHUNK)
        back = dot(w2_low, scaled_low[0:160, cols])
        grads[:, cols] = (back * acts_turn[:, cols]).astype(bf16)
        build_ref[:, cols] = dot(w1_turn, grads[:, cols])
        return carry

    lax.fori_loop(0, NX // CHUNK, chunk, 0)
    for copy in copies[5:]:
        copy.wait()
    first_sums = dot(grads[32:544, :], state_low[...], NT)
    second_sums = dot(acts[...], scaled_low[...], NT)
    lane = lax.broadcasted_iota(jnp.int32, (FEATS, 256), 1)
    total1 = total2 = plain = jnp.zeros((FEATS, 256), f32)
    for j in range(16):
        rows = slice(32 * j, 32 * j + 32)
        total1 = total1 + pltpu.roll(first_sums[rows], 255 - j, 1)
        total2 = total2 + pltpu.roll(second_sums[rows], 255 - j, 1)
        plain = plain + first_sums[rows]
    total1 = jnp.where(lane >= 6 * WIDE, plain, total1)
    high1, low1 = split(total1)
    high2, low2 = split(total2)
    packed = (dot(high1, take1_ref[...]) + dot(low1, take1_ref[...])) + (
        dot(high2, take2_ref[...]) + dot(low2, take2_ref[...])
    )
    turned = jnp.concatenate([packed, jnp.zeros((96, 128), f32)], 0).T
    ten = turned[0:10]
    for g in range(1, 4):
        ten = ten + pltpu.roll(turned[10 * g : 10 * g + 10], 32 * g, 1)
    for r in range(8):
        out_ref[r, 32:40, 0:128] = ten[0:8]
        out_ref[r, 32:34, 128:256] = ten[8:10]
        out_ref[r, 34:40, 128:256] = jnp.zeros((6, 128), f32)

    inner, up, down = slice(2, 18), slice(3, 19), slice(1, 17)
    su = field_ref[0, inner, :]
    centre = [STEP * proj_ref[c, inner, :] for c in range(2)]
    for c in range(2):
        mine = centre[c]
        above = STEP * proj_ref[c, up, :]
        below = STEP * proj_ref[c, down, :]
        carried = su * mine
        total = 0.5 * (ahead_of(carried) - behind_of(carried))
        total = total + 0.5 * (field_ref[1, up, :] * above - field_ref[1, down, :] * below)
        total = total - (centre[0] * slope_ref[c] + centre[1] * slope_ref[2 + c])
        total = total + (ahead_of(mine) + behind_of(mine) + above + below - 4.0 * mine)
        total = total + proj_ref[c, inner, :]
        for a, move in enumerate((ahead_of, None, behind_of)):
            row = (2 * a + c) * WIDE
            part = build_ref[row + 2 : row + 18, :]
            total = total + (move(part) if move else part)
        for r in range(8):
            out_ref[r, 16 * c : 16 * c + 16, :] = total[:, 256 * r : 256 * r + 256]


def unpack_kernel(in_ref, out_ref, part_ref):
    total = in_ref[0, 32:40, :]
    for r in range(1, 8):
        total = total + in_ref[r, 32:40, :]
    ten = jnp.concatenate([total[:, 0:128], total[0:2, 128:256]], 0)
    for d in range(COLS):
        part_ref[10 * d : 10 * d + 10, :] = ten
    for c in range(2):
        lines = jnp.concatenate([in_ref[r, 16 * c : 16 * c + 16, :] for r in range(8)], 0)
        out_ref[c] = lines.T


def sums_kernel(in_ref, first_ref, second_ref, bias_ref):
    total = in_ref[0:10, :]
    for d in range(1, COLS):
        total = total + in_ref[10 * d : 10 * d + 10, :]
    total = total * (1.0 / math.sqrt(NX * NY))
    moved = [total] + [pltpu.roll(total, 128 - 32 * g, 1) for g in range(1, 4)]
    first_ref[0:10, :] = moved[0][:, 0:32]
    first_ref[10:18, :] = moved[1][0:8, 0:32]
    bias_ref[...] = moved[1][8:9, 0:32]
    second_ref[0:1, :] = moved[1][9:10, 0:32]
    second_ref[1:11, :] = moved[2][:, 0:32]
    second_ref[11:18, :] = moved[3][0:7, 0:32]


def call(kernel, outs, scratch=(), scalars=0, count=0, name=None, remote=0, mib=8):
    space = [pl.BlockSpec(memory_space=pltpu.SMEM)] * scalars
    space += [pl.BlockSpec(memory_space=pltpu.HBM)] * remote
    space += [pl.BlockSpec(memory_space=pltpu.VMEM)] * (count - scalars - remote)
    many = isinstance(outs, (list, tuple))
    out_space = pl.BlockSpec(memory_space=pltpu.VMEM)
    return pl.pallas_call(
        kernel,
        out_shape=outs,
        in_specs=space,
        out_specs=[out_space] * len(outs) if many else out_space,
        scratch_shapes=list(scratch),
        compiler_params=pltpu.CompilerParams(vmem_limit_bytes=mib * 2**20),
        name=name,
    )


def shape(*dims, dtype=f32):
    return jax.ShapeDtypeStruct(dims, dtype)


def shards(state, cotangent, first_kernel, first_bias, second_kernel):
    t = tables()
    first_pick, second_pick, first_take, second_take = picks()
    dft, group, twist_y, twist_x = (
        far(jnp.asarray(t[k])) for k in ("dft", "group", "twist_y", "twist_x")
    )
    dma = lambda count: pltpu.SemaphoreType.DMA((count,))
    every = ("col", "row")
    place = (lax.axis_index("col") * ROWS + lax.axis_index("row")).astype(jnp.int32).reshape(1)
    lanes = lax.broadcasted_iota(jnp.int32, (FEATS, 256), 1)
    bias = jnp.where(lanes >= 6 * WIDE, first_bias[:, None], 0.0)

    def exchange(values, axis):
        return lax.all_to_all(values, axis, 0, 0, tiled=True)

    space = [pltpu.VMEM((4, 256, 128), f32), pltpu.SemaphoreType.DMA((4,))]
    packed = call(pack_kernel, shape(8, 64, 256), space, count=2, name="pack", remote=2)(
        far(cotangent), far(state)
    )
    lines = exchange(packed, "row")
    modes, low, high = call(
        ahead_kernel, [shape(512, 128), shape(4, NX), shape(4, NX)],
        [pltpu.VMEM((4, 256, 256), bf16), pltpu.VMEM((8, 256), f32), dma(2)],
        count=3, remote=2, name="ahead",
    )(dft, twist_x, lines)
    order = [(i % ROWS) * COLS + i // ROWS for i in range(DEV)]
    up = [(order[i], order[(i + 1) % DEV]) for i in range(DEV)]
    before = lax.ppermute(high, ("row", "col"), up)
    after = lax.ppermute(low, ("row", "col"), [(j, i) for i, j in up])
    modes = exchange(modes.reshape(DEV, 2, 128), every).reshape(512, 128)
    keep, mix = call(
        waves_kernel, [shape(256, 128), shape(256, 128)], scalars=1, count=1, name="waves"
    )(place)
    space = [
        pltpu.VMEM((4, 256, 256), bf16), pltpu.VMEM((2, 256, 128), f32),
        pltpu.VMEM((2, 128, 256), bf16), dma(3),
    ]
    modes = call(
        middle_kernel, shape(768, 128), space, scalars=1, count=7, remote=3, name="middle"
    )(place, dft, twist_y, group, modes, keep, mix)
    modes = exchange(modes.reshape(DEV, 1, 384), every).reshape(768, 128)
    prepared = call(
        state_kernel,
        [
            shape(2, WIDE, NX), shape(4, 16, NX), shape(256, NX, dtype=bf16),
            shape(512, NX, dtype=bf16), shape(576, NX), shape(576, 256, dtype=bf16),
            shape(160, 576, dtype=bf16),
        ],
        [pltpu.VMEM((160, NX), f32), pltpu.VMEM((576, 256), f32)],
        count=8,
        name="state",
        mib=12,
    )(lines, before, after, first_kernel, bias, second_kernel, first_pick, second_pick)
    field, slope, low_state, acts, acts_turn, second_taps, first_turn = map(far, prepared)
    remote = (
        dft, twist_x, second_taps, acts_turn, first_turn, low_state, acts, field, slope,
        far(jnp.asarray(first_take)), far(jnp.asarray(second_take)),
    )
    scratch = [pltpu.VMEM(x.shape, x.dtype) for x in remote] + [
        dma(len(remote)),
        pltpu.VMEM((2, WIDE, NX), f32),
        pltpu.VMEM((160, NX), f32),
        pltpu.VMEM((256, NX), bf16),
        pltpu.VMEM((576, NX), bf16),
    ]
    result = call(
        closure_kernel, shape(8, 40, 256), scratch, count=12, remote=11, name="closure", mib=32
    )(*remote, modes)
    result = exchange(result, "row")
    grad_state, part = call(
        unpack_kernel, [shape(2, 256, 128), shape(320, 128)], count=1, name="unpack"
    )(result)
    part = exchange(part.reshape(COLS, 1, 1280), "col").reshape(320, 128)
    grad_first, grad_second, grad_bias = call(
        sums_kernel, [shape(18, 32), shape(18, 32), shape(1, 32)], count=1, name="sums"
    )(part)
    return grad_state, grad_first, grad_second.T, grad_bias.reshape(32)


def solution(mesh):
    placed = (P(None, "row", "col"), P(None, "row", "col"), P(), P(), P())
    return jax.shard_map(
        shards,
        mesh=mesh,
        in_specs=placed,
        out_specs=(P(None, "row", "col"), P(), P(), P()),
        check_vma=False,
    )
```

```python
import math

import jax
import jax.numpy as jnp
import numpy as np
from jax import lax
from jax.experimental import pallas as pl
from jax.experimental.pallas import tpu as pltpu
from jax.sharding import PartitionSpec as P

NX, NY = 2048, 4096
ROWS, COLS = 8, 32
DEV = ROWS * COLS
FEATS = 32
WIDE = 24
f32, bf16 = jnp.float32, jnp.bfloat16
STEP = 0.1
NT = (((1,), (1,)), ((), ()))
NN = (((1,), (0,)), ((), ()))


def pair(table):
    high = table.astype(jnp.bfloat16)
    low = (table - high.astype(np.float64)).astype(jnp.bfloat16)
    return np.stack([high, low])


def tables():
    index = np.arange(256)
    angle = 2 * np.pi * (np.outer(index, index) % 256) / 256
    dft = np.concatenate([pair(np.cos(angle)), pair(np.sin(angle))])
    small = 2 * np.pi * (np.outer(np.arange(16), np.arange(16)) % 16) / 16
    eye = np.eye(8)
    group = np.concatenate([np.kron(eye, np.cos(small)), np.kron(eye, np.sin(small))], 1)
    twist_y = 2 * np.pi * np.outer(index, np.arange(128) % 16) / NY
    twist_x = 2 * np.pi * np.outer(np.arange(1, 5), index) / NX
    return dict(
        dft=dft,
        group=pair(group),
        twist_y=np.stack([np.cos(twist_y), np.sin(twist_y)]).astype(np.float32),
        twist_x=np.concatenate([np.cos(twist_x), np.sin(twist_x)]).astype(np.float32),
    )


def picks():
    first = np.zeros((18, 256))
    second = np.zeros((18, 256))
    out_first = np.zeros((256, 128))
    out_second = np.zeros((256, 128))
    for a in range(3):
        for b in range(3):
            for c in range(2):
                row = 2 * (3 * a + b) + c
                lane = (2 * a + c) * WIDE
                first[row, lane + b] = 1
                second[row, lane + 2 - b] = 1
                out_first[lane + b, row] = 1
                out_second[lane + 2 - b, 19 + row] = 1
    out_first[6 * WIDE, 18] = 1
    return [x.astype(jnp.bfloat16) for x in (first, second, out_first, out_second)]


def split(values):
    high = values.astype(bf16)
    return high, (values - high.astype(f32)).astype(bf16)


def dot(left, right, dims=NN):
    return lax.dot_general(left, right, dims, preferred_element_type=f32)


def left_dot(table_ref, base, values, dims=NN, keep=None):
    high, low = split(values)
    t_high, t_low = table_ref[base], table_ref[base + 1]
    if keep is not None:
        t_high, t_low = t_high[:, :keep], t_low[:, :keep]
    return dot(t_high, high, dims) + (dot(t_high, low, dims) + dot(t_low, high, dims))


def right_dot(values, table_ref):
    high, low = split(values)
    return dot(high, table_ref[0]) + (dot(low, table_ref[0]) + dot(high, table_ref[1]))


def far(values):
    return pltpu.with_memory_space_constraint(values, pltpu.HBM)


def fetch(sources, targets, sems):
    copies = [
        pltpu.make_async_copy(source, target, sems.at[k])
        for k, (source, target) in enumerate(zip(sources, targets))
    ]
    for copy in copies:
        copy.start()
    return copies


def pack_kernel(cot_ref, state_ref, out_ref, buffer_ref, sems):
    copies = []
    for f, ref in enumerate((cot_ref, state_ref)):
        for c in range(2):
            k = 2 * f + c
            copies.append(pltpu.make_async_copy(ref.at[c], buffer_ref.at[k], sems.at[k]))
    for copy in copies:
        copy.start()
    for k, copy in enumerate(copies):
        copy.wait()
        turned = buffer_ref[k].T
        for r in range(ROWS):
            out_ref[r, 16 * k : 16 * k + 16, :] = turned[16 * r : 16 * r + 16]


def ahead_kernel(dft_ref, twist_ref, in_ref, out_ref, low_ref, high_ref):
    u = [in_ref[r, 0:32, :] for r in range(8)]
    root = math.sqrt(0.5)
    a, b, c, d = (u[k] - u[k + 4] for k in range(4))
    e0, e1, e2, e3 = (u[k] + u[k + 4] for k in range(4))
    s0, s1 = e0 + e2, e1 + e3
    parts = [
        (a + root * (b - d), -c - root * (b + d)),
        (e0 - e2, e3 - e1),
        (a - root * (b - d), c - root * (b + d)),
    ]
    reals, imags = [], []
    for k, (re, im) in enumerate(parts):
        cos, sin = twist_ref[k : k + 1, :], twist_ref[4 + k : 5 + k, :]
        reals.append(re * cos + im * sin)
        imags.append(im * cos - re * sin)
    even, odd = s0 + s1, s0 - s1
    zero = jnp.zeros_like(even)
    last_re = odd * twist_ref[3:4, :]
    last_im = -odd * twist_ref[7:8, :]
    stack = jnp.concatenate(
        reals + [even] + imags + [zero] + [zero] * 3 + [last_re] + [zero] * 3 + [last_im], 0
    )
    cosine = left_dot(dft_ref, 0, stack, NT)
    sine = left_dot(dft_ref, 2, stack, NT)
    main_re = cosine[:, 0:128] + sine[:, 128:256]
    main_im = cosine[:, 128:256] - sine[:, 0:128]
    odd_re = cosine[:128, 256:384] + sine[:128, 384:512]
    odd_im = cosine[:128, 384:512] - sine[:128, 256:384]
    lane = lax.broadcasted_iota(jnp.int32, (128, 128), 1)
    row = lax.broadcasted_iota(jnp.int32, (128, 128), 0)
    last = lane >= 96
    edge = last & (row == 0)
    top_re = jnp.where(edge, main_re[128:129], main_re[:128])
    top_im = jnp.where(edge, main_re[0:1], main_im[:128])
    out_ref[pl.ds(0, 128, 2), :] = top_re
    out_ref[pl.ds(1, 128, 2), :] = top_im
    out_ref[pl.ds(256, 128, 2), :] = jnp.where(last, odd_re, main_re[128:])
    out_ref[pl.ds(257, 128, 2), :] = jnp.where(last, odd_im, main_im[128:])
    for r in range(8):
        for ch in range(2):
            row0 = 32 + 16 * ch
            low_ref[2 * ch : 2 * ch + 2, 256 * r : 256 * r + 256] = in_ref[r, row0 : row0 + 2, :]
            high_ref[2 * ch : 2 * ch + 2, 256 * r : 256 * r + 256] = in_ref[
                r, row0 + 14 : row0 + 16, :
            ]


def waves_kernel(place_ref, keep_ref, mix_ref):
    place = place_ref[0]
    lane = lax.broadcasted_iota(jnp.int32, (256, 128), 1)
    row = lax.broadcasted_iota(jnp.int32, (256, 128), 0)
    slot = lane // 32
    plain = 8 * place + slot + 1
    last = jnp.where(place == 0, NX // 2, jnp.where(place < 128, 8 * place, 8 * place - 1020))
    mx = jnp.where(slot == 3, last, plain)
    mx = jnp.where(mx >= NX // 2, mx - NX, mx)
    my = row + 256 * (lane % 16)
    my = jnp.where(my >= NY // 2, my - NY, my)
    kx = mx.astype(f32) * (1.0 / NX)
    ky = my.astype(f32) * (1.0 / NY)
    inverse = 1.0 / (kx * kx + ky * ky)
    cross = jnp.where((mx == -(NX // 2)) | (my == -(NY // 2)), 0.0, kx * ky)
    own = jnp.where((lane & 16) == 0, kx * kx, ky * ky)
    keep_ref[...] = 1.0 - own * inverse
    mix_ref[...] = -cross * inverse


def swap16(values, lane):
    return jnp.where((lane & 16) == 0, pltpu.roll(values, 112, 1), pltpu.roll(values, 16, 1))


def middle_kernel(
    place_ref, dft_ref, twist_ref, group_ref, in_ref, keep_ref, mix_ref, out_ref
):
    place = place_ref[0]
    re, im = in_ref[pl.ds(0, 256, 2), :], in_ref[pl.ds(1, 256, 2), :]
    both = jnp.concatenate([re, im], 1)
    cosine, sine = left_dot(dft_ref, 0, both), left_dot(dft_ref, 2, both)
    f_re, f_im = cosine[:, :128] + sine[:, 128:], cosine[:, 128:] - sine[:, :128]
    cos, sin = twist_ref[0], twist_ref[1]
    t_re, t_im = f_re * cos + f_im * sin, f_im * cos - f_re * sin
    g = right_dot(jnp.concatenate([t_re, t_im], 0), group_ref)
    g_re, g_im = g[:256, :128] + g[256:, 128:], g[256:, :128] - g[:256, 128:]
    keep, mix = keep_ref[...], mix_ref[...]
    lane = lax.broadcasted_iota(jnp.int32, (256, 128), 1)
    p_re = keep * g_re + mix * swap16(g_re, lane)
    p_im = keep * g_im + mix * swap16(g_im, lane)
    h = right_dot(jnp.concatenate([p_re, p_im], 0), group_ref)
    h_re, h_im = h[:256, :128] - h[256:, 128:], h[256:, :128] + h[:256, 128:]
    t_re, t_im = h_re * cos - h_im * sin, h_im * cos + h_re * sin
    both = jnp.concatenate([t_re, t_im], 1)
    cosine, sine = left_dot(dft_ref, 0, both), left_dot(dft_ref, 2, both)
    scale = 1.0 / (NX * NY)
    o_re = (cosine[:, :128] - sine[:, 128:]) * scale
    o_im = (cosine[:, 128:] + sine[:, :128]) * scale
    sums = jnp.sum(im, 0, keepdims=True)
    sums = jnp.where(lane[:1] >= 112, sums, 0.0)
    mean = jnp.sum(sums, 1, keepdims=True) * scale
    zeroth = (lane >= 96) & (place == 0)
    o_im = jnp.where(zeroth, jnp.where(lane >= 112, mean, im * (1.0 / NX)), o_im)
    near = (lane & 8) == 0
    outer = ((lane + 2) & 15) < 4

    def beside(values):
        return jnp.where(near, pltpu.roll(values, 255, 0), pltpu.roll(values, 1, 0))

    out_ref[pl.ds(0, 256, 3), :] = o_re
    out_ref[pl.ds(1, 256, 3), :] = o_im
    edge_im = beside(o_im)
    edge_im = jnp.where(near, pltpu.roll(edge_im, 4, 1), pltpu.roll(edge_im, 124, 1))
    out_ref[pl.ds(2, 256, 3), :] = jnp.where(outer, beside(o_re), edge_im)


def back_part(in_ref, dft_ref, twist_ref, out_ref):
    lane = lax.broadcasted_iota(jnp.int32, (128, 128), 1)
    row = lax.broadcasted_iota(jnp.int32, (128, 128), 0)
    last = lane >= 96
    edge = last & (row == 0)
    near = (lane & 8) == 0
    outer = ((lane + 2) & 15) < 4
    top_re, top_im, top_h = (in_ref[pl.ds(k, 128, 3), :] for k in range(3))
    low_re, low_im, low_h = (in_ref[pl.ds(384 + k, 128, 3), :] for k in range(3))
    head = top_h[0:1]
    head_im = jnp.where(near[0:1], pltpu.roll(head, 124, 1), pltpu.roll(head, 4, 1))
    half_im = jnp.where(outer[0:1], 0.5 * head_im, 0.0)
    half_re = jnp.where(outer[0:1], 0.5 * head, 0.0)
    nyquist = jnp.where(edge, 0.5 * top_re[0:1], 0.0)
    mains = [
        jnp.concatenate(
            [jnp.where(edge, 0.5 * top_im, top_re), jnp.where(last, nyquist, low_re)], 0
        ),
        jnp.concatenate([jnp.where(edge, 0.0, top_im), jnp.where(last, 0.0, low_im)], 0),
        jnp.concatenate(
            [
                jnp.where(edge, half_im, top_h),
                jnp.where(last, jnp.where(edge, half_re, 0.0), low_h),
            ],
            0,
        ),
    ]
    m_high, m_low = split(jnp.concatenate(mains, 1).T)
    o_high, o_low = split(jnp.concatenate([low_re, low_im, low_h], 1).T)

    def turn(high, low, base, keep):
        t_high, t_low = dft_ref[base][:keep], dft_ref[base + 1][:keep]
        return dot(high, t_high) + (dot(low, t_high) + dot(high, t_low))

    m_cos, m_sin = turn(m_high, m_low, 0, 256), turn(m_high, m_low, 2, 256)
    o_cos, o_sin = turn(o_high, o_low, 0, 128), turn(o_high, o_low, 2, 128)
    root = math.sqrt(0.5)
    near_row = (lax.broadcasted_iota(jnp.int32, (128, 256), 0) & 8) == 0

    def imag_rows(values):
        return jnp.where(near_row, pltpu.roll(values, 124, 0), pltpu.roll(values, 4, 0))

    for k in (0, 256):
        if k == 0:
            re, im = m_cos[0:128] - m_sin[128:256], m_cos[128:256] + m_sin[0:128]
            last_re, last_im = o_cos[96:128] - o_sin[224:256], o_cos[224:256] + o_sin[96:128]
        else:
            m_c, m_s, o_c, o_s = (v[256:384] for v in (m_cos, m_sin, o_cos, o_sin))
            re, im = m_c - imag_rows(m_s), imag_rows(m_c) + m_s
            last_re, last_im = (o_c - imag_rows(o_s))[96:], (imag_rows(o_c) + o_s)[96:]
        w4 = last_re * twist_ref[3:4, :] - last_im * twist_ref[7:8, :]
        w0 = re[96:128]
        ws = []
        for p in range(3):
            cos, sin = twist_ref[p : p + 1, :], twist_ref[4 + p : 5 + p, :]
            r_p, i_p = re[32 * p : 32 * p + 32], im[32 * p : 32 * p + 32]
            ws.append((r_p * cos - i_p * sin, i_p * cos + r_p * sin))
        for r in range(8):
            total = w0 + w4 if r % 2 == 0 else w0 - w4
            for p in range(3):
                turn_by = (r * (p + 1)) % 8
                cos_r = [1.0, root, 0.0, -root, -1.0, -root, 0.0, root][turn_by]
                sin_r = [0.0, root, 1.0, root, 0.0, -root, -1.0, -root][turn_by]
                if cos_r:
                    total = total + cos_r * ws[p][0]
                if sin_r:
                    total = total - sin_r * ws[p][1]
            total = total + total
            lanes = slice(256 * r, 256 * r + 256)
            for ch in range(2):
                if k == 0:
                    out_ref[ch, 2:18, lanes] = total[16 * ch : 16 * ch + 16]
                else:
                    out_ref[ch, 0:2, lanes] = total[16 * ch + 14 : 16 * ch + 16]
                    out_ref[ch, 18:20, lanes] = total[16 * ch : 16 * ch + 2]
                    if r == 0:
                        out_ref[ch, 20:24, :] = jnp.zeros((4, NX), f32)


def ahead_of(values):
    return pltpu.roll(values, NX - 1, 1)


def behind_of(values):
    return pltpu.roll(values, 1, 1)


def fill_taps(build_ref, target, fields, sign):
    for c in range(2):
        whole = fields[c]
        moves = (behind_of(whole), whole, ahead_of(whole))[::sign]
        for a in range(3):
            row = (2 * a + c) * WIDE
            build_ref[row : row + WIDE, :] = moves[a]
    build_ref[144:152, :] = jnp.ones((8, NX), f32)
    build_ref[152:160, :] = jnp.zeros((8, NX), f32)
    target[0:160, :] = build_ref[...].astype(bf16)
    target[160:256, :] = jnp.zeros((96, NX), bf16)


CHUNK = 256


def state_kernel(
    own_ref, before_ref, after_ref, first_ref, bias_ref, second_ref, pick1_ref, pick2_ref,
    w2_far, acts_turn_far, turn_far, state_far, acts_far, field_far,
    w2_ref, acts_turn, turn_ref, state_low, acts, field_ref, sems,
    build_ref, w1_ref,
):
    lane = lax.broadcasted_iota(jnp.int32, (FEATS, 256), 1)
    bias = bias_ref[...]
    bias_high = bias.astype(bf16).astype(f32)
    bias_part = jnp.where(
        lane == 6 * WIDE, bias_high, jnp.where(lane == 6 * WIDE + 1, bias - bias_high, 0.0)
    )
    base1 = dot(first_ref[...].astype(f32).T.astype(bf16), pick1_ref[...])
    base2 = dot(second_ref[...], pick2_ref[...])
    for j in range(18):
        rows = slice(32 * j, 32 * j + 32)
        moved1 = pltpu.roll(base1, j, 1) if j else base1
        moved2 = pltpu.roll(base2, j, 1) if j else base2
        w1_ref[rows, :] = moved1 + bias_part
        w2_ref[rows, :] = moved2.astype(bf16)
    for c in range(2):
        field_ref[c, 20:24, :] = jnp.zeros((4, NX), f32)
        for r in range(8):
            field_ref[c, 2:18, 256 * r : 256 * r + 256] = own_ref[
                r, 32 + 16 * c : 48 + 16 * c, :
            ]
        field_ref[c, 0:2, :] = before_ref[2 * c : 2 * c + 2, :]
        field_ref[c, 18:20, :] = after_ref[2 * c : 2 * c + 2, :]
    fill_taps(build_ref, state_low, (field_ref[0], field_ref[1]), 1)
    w1 = w1_ref[...]
    turn_ref[...] = w1.T[:160].astype(bf16)
    w1_low = w1[:, :160].astype(bf16)

    def chunk(k, carry):
        cols = pl.ds(pl.multiple_of(k * CHUNK, CHUNK), CHUNK)
        active = jnp.tanh(dot(w1_low, state_low[0:160, cols]))
        acts[:, cols] = active[32:544].astype(bf16)
        acts_turn[:, cols] = (1.0 - active * active).astype(bf16)
        return carry

    lax.fori_loop(0, NX // CHUNK, chunk, 0)
    copies = fetch(
        (w2_ref, acts_turn, turn_ref, state_low.at[0:160], acts, field_ref),
        (w2_far, acts_turn_far, turn_far, state_far, acts_far, field_far),
        sems,
    )
    for copy in copies:
        copy.wait()


def closure_kernel(
    w2_far, acts_turn_far, turn_far, state_far, acts_far, field_far,
    dft_ref, twist_ref, take1_ref, take2_ref, in_ref,
    out_ref,
    w2_ref, acts_turn, turn_ref, state_low, acts, field_ref, sems,
    proj_ref, build_ref, scaled_low, grads,
):
    copies = fetch(
        (w2_far, acts_turn_far, turn_far, state_far, acts_far, field_far),
        (w2_ref, acts_turn, turn_ref, state_low.at[0:160], acts, field_ref),
        sems,
    )
    state_low[160:256, :] = jnp.zeros((96, NX), bf16)
    back_part(in_ref, dft_ref, twist_ref, proj_ref)
    fill_taps(build_ref, scaled_low, (STEP * proj_ref[0], STEP * proj_ref[1]), -1)
    for copy in copies[:3]:
        copy.wait()
    w2_low = w2_ref[:, :160]
    w1_turn = turn_ref[...]

    def chunk(k, carry):
        cols = pl.ds(pl.multiple_of(k * CHUNK, CHUNK), CHUNK)
        back = dot(w2_low, scaled_low[0:160, cols])
        grads[:, cols] = (back * acts_turn[:, cols].astype(f32)).astype(bf16)
        build_ref[:, cols] = dot(w1_turn, grads[:, cols])
        return carry

    lax.fori_loop(0, NX // CHUNK, chunk, 0)
    for copy in copies[3:]:
        copy.wait()
    first_sums = dot(grads[32:544, :], state_low[...], NT)
    second_sums = dot(acts[...], scaled_low[...], NT)
    lane = lax.broadcasted_iota(jnp.int32, (FEATS, 256), 1)
    total1 = total2 = plain = jnp.zeros((FEATS, 256), f32)
    for j in range(16):
        rows = slice(32 * j, 32 * j + 32)
        total1 = total1 + pltpu.roll(first_sums[rows], 255 - j, 1)
        total2 = total2 + pltpu.roll(second_sums[rows], 255 - j, 1)
        plain = plain + first_sums[rows]
    total1 = jnp.where(lane >= 6 * WIDE, plain, total1)
    high1, low1 = split(total1)
    high2, low2 = split(total2)
    packed = (dot(high1, take1_ref[...]) + dot(low1, take1_ref[...])) + (
        dot(high2, take2_ref[...]) + dot(low2, take2_ref[...])
    )
    turned = jnp.concatenate([packed, jnp.zeros((96, 128), f32)], 0).T
    ten = turned[0:10]
    for g in range(1, 4):
        ten = ten + pltpu.roll(turned[10 * g : 10 * g + 10], 32 * g, 1)
    for r in range(8):
        out_ref[r, 32:40, 0:128] = ten[0:8]
        out_ref[r, 32:34, 128:256] = ten[8:10]
        out_ref[r, 34:40, 128:256] = jnp.zeros((6, 128), f32)

    inner, up, down = slice(2, 18), slice(3, 19), slice(1, 17)
    su = field_ref[0, inner, :]
    along_x, along_y = [], []
    for c in range(2):
        mine = field_ref[c, inner, :]
        along_x.append(0.5 * (ahead_of(mine) - behind_of(mine)))
        along_y.append(0.5 * (field_ref[c, up, :] - field_ref[c, down, :]))
    along = (along_x, along_y)
    centre = [STEP * proj_ref[c, inner, :] for c in range(2)]
    for c in range(2):
        mine = centre[c]
        above = STEP * proj_ref[c, up, :]
        below = STEP * proj_ref[c, down, :]
        carried = su * mine
        total = 0.5 * (ahead_of(carried) - behind_of(carried))
        total = total + 0.5 * (field_ref[1, up, :] * above - field_ref[1, down, :] * below)
        total = total - (centre[0] * along[c][0] + centre[1] * along[c][1])
        total = total + (ahead_of(mine) + behind_of(mine) + above + below - 4.0 * mine)
        total = total + proj_ref[c, inner, :]
        for a, move in enumerate((ahead_of, None, behind_of)):
            row = (2 * a + c) * WIDE
            part = build_ref[row + 2 : row + 18, :]
            total = total + (move(part) if move else part)
        for r in range(8):
            out_ref[r, 16 * c : 16 * c + 16, :] = total[:, 256 * r : 256 * r + 256]


def unpack_kernel(in_ref, out_ref, part_ref):
    total = in_ref[0, 32:40, :]
    for r in range(1, 8):
        total = total + in_ref[r, 32:40, :]
    ten = jnp.concatenate([total[:, 0:128], total[0:2, 128:256]], 0)
    for d in range(COLS):
        part_ref[10 * d : 10 * d + 10, :] = ten
    for c in range(2):
        lines = jnp.concatenate([in_ref[r, 16 * c : 16 * c + 16, :] for r in range(8)], 0)
        out_ref[c] = lines.T


def sums_kernel(in_ref, first_ref, second_ref, bias_ref):
    total = in_ref[0:10, :]
    for d in range(1, COLS):
        total = total + in_ref[10 * d : 10 * d + 10, :]
    total = total * (1.0 / math.sqrt(NX * NY))
    moved = [total] + [pltpu.roll(total, 128 - 32 * g, 1) for g in range(1, 4)]
    first_ref[0:10, :] = moved[0][:, 0:32]
    first_ref[10:18, :] = moved[1][0:8, 0:32]
    bias_ref[...] = moved[1][8:9, 0:32]
    second_ref[0:1, :] = moved[1][9:10, 0:32]
    second_ref[1:11, :] = moved[2][:, 0:32]
    second_ref[11:18, :] = moved[3][0:7, 0:32]


def call(kernel, outs, scratch=(), scalars=0, count=0, name=None, remote=0, mib=8, leave=False):
    space = [pl.BlockSpec(memory_space=pltpu.SMEM)] * scalars
    space += [pl.BlockSpec(memory_space=pltpu.HBM)] * remote
    space += [pl.BlockSpec(memory_space=pltpu.VMEM)] * (count - scalars - remote)
    many = isinstance(outs, (list, tuple))
    out_space = pl.BlockSpec(memory_space=pltpu.HBM if leave else pltpu.VMEM)
    return pl.pallas_call(
        kernel,
        out_shape=outs,
        in_specs=space,
        out_specs=[out_space] * len(outs) if many else out_space,
        scratch_shapes=list(scratch),
        compiler_params=pltpu.CompilerParams(vmem_limit_bytes=mib * 2**20),
        name=name,
    )


def shape(*dims, dtype=f32):
    return jax.ShapeDtypeStruct(dims, dtype)


def shards(state, cotangent, first_kernel, first_bias, second_kernel):
    t = tables()
    first_pick, second_pick, first_take, second_take = picks()
    dft, group, twist_y, twist_x = (
        jnp.asarray(t[k]) for k in ("dft", "group", "twist_y", "twist_x")
    )
    dma = lambda count: pltpu.SemaphoreType.DMA((count,))
    every = ("col", "row")
    place = (lax.axis_index("col") * ROWS + lax.axis_index("row")).astype(jnp.int32).reshape(1)
    lanes = lax.broadcasted_iota(jnp.int32, (FEATS, 256), 1)
    bias = jnp.where(lanes >= 6 * WIDE, first_bias[:, None], 0.0)

    def exchange(values, axis):
        return lax.all_to_all(values, axis, 0, 0, tiled=True)

    space = [pltpu.VMEM((4, 256, 128), f32), pltpu.SemaphoreType.DMA((4,))]
    packed = call(pack_kernel, shape(8, 64, 256), space, count=2, name="pack", remote=2)(
        far(cotangent), far(state)
    )
    lines = exchange(packed, "row")
    modes, low, high = call(
        ahead_kernel, [shape(512, 128), shape(4, NX), shape(4, NX)],
        count=3, name="ahead",
    )(dft, twist_x, lines)
    order = [(i % ROWS) * COLS + i // ROWS for i in range(DEV)]
    up = [(order[i], order[(i + 1) % DEV]) for i in range(DEV)]
    before = lax.ppermute(high, ("row", "col"), up)
    after = lax.ppermute(low, ("row", "col"), [(j, i) for i, j in up])
    modes = exchange(modes.reshape(DEV, 2, 128), every).reshape(512, 128)
    keep, mix = call(
        waves_kernel, [shape(256, 128), shape(256, 128)], scalars=1, count=1, name="waves"
    )(place)
    modes, before, after = lax.optimization_barrier((modes, before, after))
    modes = call(middle_kernel, shape(768, 128), scalars=1, count=7, name="middle")(place, dft, twist_y, group, modes, keep, mix)
    modes = exchange(modes.reshape(DEV, 1, 384), every).reshape(768, 128)
    kept = [
        ((576, 256), bf16), ((576, NX), bf16), ((160, 576), bf16), ((256, NX), bf16),
        ((512, NX), bf16), ((2, WIDE, NX), f32),
    ]
    local = [pltpu.VMEM(*k) for k in kept] + [dma(len(kept))]
    kept[3] = ((160, NX), bf16)
    prepared = call(
        state_kernel,
        [pltpu.HBM(*k) for k in kept],
        local + [pltpu.VMEM((160, NX), f32), pltpu.VMEM((576, 256), f32)],
        count=8,
        name="state",
        mib=24,
        leave=True,
    )(lines, before, after, first_kernel, bias, second_kernel, first_pick, second_pick)
    scratch = local + [
        pltpu.VMEM((2, WIDE, NX), f32),
        pltpu.VMEM((160, NX), f32),
        pltpu.VMEM((256, NX), bf16),
        pltpu.VMEM((576, NX), bf16),
    ]
    result = call(
        closure_kernel, shape(8, 40, 256), scratch, count=11, remote=6, name="closure", mib=32
    )(*map(far, prepared), dft, twist_x, first_take, second_take, modes)
    result = exchange(result, "row")
    grad_state, part = call(
        unpack_kernel, [shape(2, 256, 128), shape(320, 128)], count=1, name="unpack"
    )(result)
    part = exchange(part.reshape(COLS, 1, 1280), "col").reshape(320, 128)
    grad_first, grad_second, grad_bias = call(
        sums_kernel, [shape(18, 32), shape(18, 32), shape(1, 32)], count=1, name="sums"
    )(part)
    return grad_state, grad_first, grad_second.T, grad_bias.reshape(32)


def solution(mesh):
    placed = (P(None, "row", "col"), P(None, "row", "col"), P(), P(), P())
    return jax.shard_map(
        shards,
        mesh=mesh,
        in_specs=placed,
        out_specs=(P(None, "row", "col"), P(), P(), P()),
        check_vma=False,
    )
```

```python
import math

import jax
import jax.numpy as jnp
import numpy as np
from jax import lax
from jax.experimental import pallas as pl
from jax.experimental.pallas import tpu as pltpu
from jax.sharding import PartitionSpec as P

NX, NY = 2048, 4096
ROWS, COLS = 8, 32
DEV = ROWS * COLS
FEATS = 32
WIDE = 24
f32, bf16 = jnp.float32, jnp.bfloat16
STEP = 0.1
NT = (((1,), (1,)), ((), ()))
NN = (((1,), (0,)), ((), ()))


def pair(table):
    high = table.astype(jnp.bfloat16)
    low = (table - high.astype(np.float64)).astype(jnp.bfloat16)
    return np.stack([high, low])


def tables():
    index = np.arange(256)
    angle = 2 * np.pi * (np.outer(index, index) % 256) / 256
    dft = np.concatenate([pair(np.cos(angle)), pair(np.sin(angle))])
    small = 2 * np.pi * (np.outer(np.arange(16), np.arange(16)) % 16) / 16
    eye = np.eye(8)
    group = np.concatenate([np.kron(eye, np.cos(small)), np.kron(eye, np.sin(small))], 1)
    twist_y = 2 * np.pi * np.outer(index, np.arange(128) % 16) / NY
    twist_x = 2 * np.pi * np.outer(np.arange(1, 5), index) / NX
    return dict(
        dft=dft,
        group=pair(group),
        twist_y=np.stack([np.cos(twist_y), np.sin(twist_y)]).astype(np.float32),
        twist_x=np.concatenate([np.cos(twist_x), np.sin(twist_x)]).astype(np.float32),
    )


def picks():
    first = np.zeros((18, 256))
    second = np.zeros((18, 256))
    out_first = np.zeros((256, 128))
    out_second = np.zeros((256, 128))
    for a in range(3):
        for b in range(3):
            for c in range(2):
                row = 2 * (3 * a + b) + c
                lane = (2 * a + c) * WIDE
                first[row, lane + b] = 1
                second[row, lane + 2 - b] = 1
                out_first[lane + b, row] = 1
                out_second[lane + 2 - b, 19 + row] = 1
    out_first[6 * WIDE, 18] = 1
    return [x.astype(jnp.bfloat16) for x in (first, second, out_first, out_second)]


def split(values):
    high = values.astype(bf16)
    return high, (values - high.astype(f32)).astype(bf16)


def dot(left, right, dims=NN):
    return lax.dot_general(left, right, dims, preferred_element_type=f32)


def left_dot(table_ref, base, values, dims=NN, keep=None):
    high, low = split(values)
    t_high, t_low = table_ref[base], table_ref[base + 1]
    if keep is not None:
        t_high, t_low = t_high[:, :keep], t_low[:, :keep]
    return dot(t_high, high, dims) + (dot(t_high, low, dims) + dot(t_low, high, dims))


def right_dot(values, table_ref):
    high, low = split(values)
    return dot(high, table_ref[0]) + (dot(low, table_ref[0]) + dot(high, table_ref[1]))


def far(values):
    return pltpu.with_memory_space_constraint(values, pltpu.HBM)


def pack_kernel(cot_ref, state_ref, twist_far, out_ref, twist_ref, buffer_ref, sems):
    copies = []
    twist_copy = pltpu.make_async_copy(twist_far, twist_ref, sems.at[4])
    for f, ref in enumerate((cot_ref, state_ref)):
        for c in range(2):
            k = 2 * f + c
            copies.append(pltpu.make_async_copy(ref.at[c], buffer_ref.at[k], sems.at[k]))
    for copy in copies:
        copy.start()
    twist_copy.start()
    for k, copy in enumerate(copies):
        copy.wait()
        turned = buffer_ref[k].T
        for r in range(ROWS):
            out_ref[r, 16 * k : 16 * k + 16, :] = turned[16 * r : 16 * r + 16]
    twist_copy.wait()


def ahead_kernel(dft_ref, twist_ref, in_ref, out_ref, low_ref, high_ref):
    u = [in_ref[r, 0:32, :] for r in range(8)]
    root = math.sqrt(0.5)
    a, b, c, d = (u[k] - u[k + 4] for k in range(4))
    e0, e1, e2, e3 = (u[k] + u[k + 4] for k in range(4))
    s0, s1 = e0 + e2, e1 + e3
    parts = [
        (a + root * (b - d), -c - root * (b + d)),
        (e0 - e2, e3 - e1),
        (a - root * (b - d), c - root * (b + d)),
    ]
    reals, imags = [], []
    for k, (re, im) in enumerate(parts):
        cos, sin = twist_ref[k : k + 1, :], twist_ref[4 + k : 5 + k, :]
        reals.append(re * cos + im * sin)
        imags.append(im * cos - re * sin)
    even, odd = s0 + s1, s0 - s1
    zero = jnp.zeros_like(even)
    last_re = odd * twist_ref[3:4, :]
    last_im = -odd * twist_ref[7:8, :]
    stack = jnp.concatenate(
        reals + [even] + imags + [zero] + [zero] * 3 + [last_re] + [zero] * 3 + [last_im], 0
    )
    cosine = left_dot(dft_ref, 0, stack, NT)
    sine = left_dot(dft_ref, 2, stack, NT)
    main_re = cosine[:, 0:128] + sine[:, 128:256]
    main_im = cosine[:, 128:256] - sine[:, 0:128]
    odd_re = cosine[:128, 256:384] + sine[:128, 384:512]
    odd_im = cosine[:128, 384:512] - sine[:128, 256:384]
    lane = lax.broadcasted_iota(jnp.int32, (128, 128), 1)
    row = lax.broadcasted_iota(jnp.int32, (128, 128), 0)
    last = lane >= 96
    edge = last & (row == 0)
    top_re = jnp.where(edge, main_re[128:129], main_re[:128])
    top_im = jnp.where(edge, main_re[0:1], main_im[:128])
    out_ref[pl.ds(0, 128, 2), :] = top_re
    out_ref[pl.ds(1, 128, 2), :] = top_im
    out_ref[pl.ds(256, 128, 2), :] = jnp.where(last, odd_re, main_re[128:])
    out_ref[pl.ds(257, 128, 2), :] = jnp.where(last, odd_im, main_im[128:])
    for r in range(8):
        for ch in range(2):
            row0 = 32 + 16 * ch
            low_ref[2 * ch : 2 * ch + 2, 256 * r : 256 * r + 256] = in_ref[r, row0 : row0 + 2, :]
            high_ref[2 * ch : 2 * ch + 2, 256 * r : 256 * r + 256] = in_ref[
                r, row0 + 14 : row0 + 16, :
            ]


def waves_kernel(place_ref, keep_ref, mix_ref):
    place = place_ref[0]
    lane = lax.broadcasted_iota(jnp.int32, (256, 128), 1)
    row = lax.broadcasted_iota(jnp.int32, (256, 128), 0)
    slot = lane // 32
    plain = 8 * place + slot + 1
    last = jnp.where(place == 0, NX // 2, jnp.where(place < 128, 8 * place, 8 * place - 1020))
    mx = jnp.where(slot == 3, last, plain)
    mx = jnp.where(mx >= NX // 2, mx - NX, mx)
    my = row + 256 * (lane % 16)
    my = jnp.where(my >= NY // 2, my - NY, my)
    kx = mx.astype(f32) * (1.0 / NX)
    ky = my.astype(f32) * (1.0 / NY)
    inverse = 1.0 / (kx * kx + ky * ky)
    cross = jnp.where((mx == -(NX // 2)) | (my == -(NY // 2)), 0.0, kx * ky)
    own = jnp.where((lane & 16) == 0, kx * kx, ky * ky)
    keep_ref[...] = 1.0 - own * inverse
    mix_ref[...] = -cross * inverse


def swap16(values, lane):
    return jnp.where((lane & 16) == 0, pltpu.roll(values, 112, 1), pltpu.roll(values, 16, 1))


def middle_kernel(
    place_ref, dft_ref, twist_ref, group_ref, in_ref, keep_ref, mix_ref, out_ref
):
    place = place_ref[0]
    re, im = in_ref[pl.ds(0, 256, 2), :], in_ref[pl.ds(1, 256, 2), :]
    both = jnp.concatenate([re, im], 1)
    cosine, sine = left_dot(dft_ref, 0, both), left_dot(dft_ref, 2, both)
    f_re, f_im = cosine[:, :128] + sine[:, 128:], cosine[:, 128:] - sine[:, :128]
    cos, sin = twist_ref[0], twist_ref[1]
    t_re, t_im = f_re * cos + f_im * sin, f_im * cos - f_re * sin
    g = right_dot(jnp.concatenate([t_re, t_im], 0), group_ref)
    g_re, g_im = g[:256, :128] + g[256:, 128:], g[256:, :128] - g[:256, 128:]
    keep, mix = keep_ref[...], mix_ref[...]
    lane = lax.broadcasted_iota(jnp.int32, (256, 128), 1)
    p_re = keep * g_re + mix * swap16(g_re, lane)
    p_im = keep * g_im + mix * swap16(g_im, lane)
    h = right_dot(jnp.concatenate([p_re, p_im], 0), group_ref)
    h_re, h_im = h[:256, :128] - h[256:, 128:], h[256:, :128] + h[:256, 128:]
    t_re, t_im = h_re * cos - h_im * sin, h_im * cos + h_re * sin
    both = jnp.concatenate([t_re, t_im], 1)
    cosine, sine = left_dot(dft_ref, 0, both), left_dot(dft_ref, 2, both)
    scale = 1.0 / (NX * NY)
    o_re = (cosine[:, :128] - sine[:, 128:]) * scale
    o_im = (cosine[:, 128:] + sine[:, :128]) * scale
    sums = jnp.sum(im, 0, keepdims=True)
    sums = jnp.where(lane[:1] >= 112, sums, 0.0)
    mean = jnp.sum(sums, 1, keepdims=True) * scale
    zeroth = (lane >= 96) & (place == 0)
    o_im = jnp.where(zeroth, jnp.where(lane >= 112, mean, im * (1.0 / NX)), o_im)
    near = (lane & 8) == 0
    outer = ((lane + 2) & 15) < 4

    def beside(values):
        return jnp.where(near, pltpu.roll(values, 255, 0), pltpu.roll(values, 1, 0))

    out_ref[pl.ds(0, 256, 3), :] = o_re
    out_ref[pl.ds(1, 256, 3), :] = o_im
    edge_im = beside(o_im)
    edge_im = jnp.where(near, pltpu.roll(edge_im, 4, 1), pltpu.roll(edge_im, 124, 1))
    out_ref[pl.ds(2, 256, 3), :] = jnp.where(outer, beside(o_re), edge_im)


def back_part(in_ref, dft_ref, twist_ref, out_ref):
    lane = lax.broadcasted_iota(jnp.int32, (128, 128), 1)
    row = lax.broadcasted_iota(jnp.int32, (128, 128), 0)
    last = lane >= 96
    edge = last & (row == 0)
    near = (lane & 8) == 0
    outer = ((lane + 2) & 15) < 4
    top_re, top_im, top_h = (in_ref[pl.ds(k, 128, 3), :] for k in range(3))
    low_re, low_im, low_h = (in_ref[pl.ds(384 + k, 128, 3), :] for k in range(3))
    head = top_h[0:1]
    head_im = jnp.where(near[0:1], pltpu.roll(head, 124, 1), pltpu.roll(head, 4, 1))
    half_im = jnp.where(outer[0:1], 0.5 * head_im, 0.0)
    half_re = jnp.where(outer[0:1], 0.5 * head, 0.0)
    nyquist = jnp.where(edge, 0.5 * top_re[0:1], 0.0)
    mains = [
        jnp.concatenate(
            [jnp.where(edge, 0.5 * top_im, top_re), jnp.where(last, nyquist, low_re)], 0
        ),
        jnp.concatenate([jnp.where(edge, 0.0, top_im), jnp.where(last, 0.0, low_im)], 0),
        jnp.concatenate(
            [
                jnp.where(edge, half_im, top_h),
                jnp.where(last, jnp.where(edge, half_re, 0.0), low_h),
            ],
            0,
        ),
    ]
    m_high, m_low = split(jnp.concatenate(mains, 1).T)
    o_high, o_low = split(jnp.concatenate([low_re, low_im, low_h], 1).T)

    def turn(high, low, base, keep):
        t_high, t_low = dft_ref[base][:keep], dft_ref[base + 1][:keep]
        return dot(high, t_high) + (dot(low, t_high) + dot(high, t_low))

    m_cos, m_sin = turn(m_high, m_low, 0, 256), turn(m_high, m_low, 2, 256)
    o_cos, o_sin = turn(o_high, o_low, 0, 128), turn(o_high, o_low, 2, 128)
    root = math.sqrt(0.5)
    near_row = (lax.broadcasted_iota(jnp.int32, (128, 256), 0) & 8) == 0

    def imag_rows(values):
        return jnp.where(near_row, pltpu.roll(values, 124, 0), pltpu.roll(values, 4, 0))

    for k in (0, 256):
        if k == 0:
            re, im = m_cos[0:128] - m_sin[128:256], m_cos[128:256] + m_sin[0:128]
            last_re, last_im = o_cos[96:128] - o_sin[224:256], o_cos[224:256] + o_sin[96:128]
        else:
            m_c, m_s, o_c, o_s = (v[256:384] for v in (m_cos, m_sin, o_cos, o_sin))
            re, im = m_c - imag_rows(m_s), imag_rows(m_c) + m_s
            last_re, last_im = (o_c - imag_rows(o_s))[96:], (imag_rows(o_c) + o_s)[96:]
        w4 = last_re * twist_ref[3:4, :] - last_im * twist_ref[7:8, :]
        w0 = re[96:128]
        ws = []
        for p in range(3):
            cos, sin = twist_ref[p : p + 1, :], twist_ref[4 + p : 5 + p, :]
            r_p, i_p = re[32 * p : 32 * p + 32], im[32 * p : 32 * p + 32]
            ws.append((r_p * cos - i_p * sin, i_p * cos + r_p * sin))
        for r in range(8):
            total = w0 + w4 if r % 2 == 0 else w0 - w4
            for p in range(3):
                turn_by = (r * (p + 1)) % 8
                cos_r = [1.0, root, 0.0, -root, -1.0, -root, 0.0, root][turn_by]
                sin_r = [0.0, root, 1.0, root, 0.0, -root, -1.0, -root][turn_by]
                if cos_r:
                    total = total + cos_r * ws[p][0]
                if sin_r:
                    total = total - sin_r * ws[p][1]
            total = total + total
            lanes = slice(256 * r, 256 * r + 256)
            for ch in range(2):
                if k == 0:
                    out_ref[ch, 2:18, lanes] = total[16 * ch : 16 * ch + 16]
                else:
                    out_ref[ch, 0:2, lanes] = total[16 * ch + 14 : 16 * ch + 16]
                    out_ref[ch, 18:20, lanes] = total[16 * ch : 16 * ch + 2]
                    if r == 0:
                        out_ref[ch, 20:24, :] = jnp.zeros((4, NX), f32)


def ahead_of(values):
    return pltpu.roll(values, NX - 1, 1)


def behind_of(values):
    return pltpu.roll(values, 1, 1)


def fill_taps(build_ref, target, fields, sign):
    for c in range(2):
        whole = fields[c]
        moves = (behind_of(whole), whole, ahead_of(whole))[::sign]
        for a in range(3):
            row = (2 * a + c) * WIDE
            build_ref[row : row + WIDE, :] = moves[a]
    build_ref[144:152, :] = jnp.ones((8, NX), f32)
    build_ref[152:160, :] = jnp.zeros((8, NX), f32)
    target[0:160, :] = build_ref[...].astype(bf16)


def state_kernel(
    own_ref, before_ref, after_ref, first_ref, bias_ref, second_ref, pick1_ref, pick2_ref,
    w1_out, w2_out, turn_ref, state_low, field_ref,
    build_ref, w1_ref, w2_ref,
):
    lane = lax.broadcasted_iota(jnp.int32, (FEATS, 256), 1)
    bias = bias_ref[...]
    bias_high = bias.astype(bf16).astype(f32)
    bias_part = jnp.where(
        lane == 6 * WIDE, bias_high, jnp.where(lane == 6 * WIDE + 1, bias - bias_high, 0.0)
    )
    base1 = dot(first_ref[...].astype(f32).T.astype(bf16), pick1_ref[...])
    base2 = dot(second_ref[...], pick2_ref[...])
    for j in range(18):
        rows = slice(32 * j, 32 * j + 32)
        moved1 = pltpu.roll(base1, j, 1) if j else base1
        moved2 = pltpu.roll(base2, j, 1) if j else base2
        w1_ref[rows, :] = moved1 + bias_part
        w2_ref[rows, :] = moved2
    for c in range(2):
        field_ref[c, 20:24, :] = jnp.zeros((4, NX), f32)
        for r in range(8):
            field_ref[c, 2:18, 256 * r : 256 * r + 256] = own_ref[
                r, 32 + 16 * c : 48 + 16 * c, :
            ]
        field_ref[c, 0:2, :] = before_ref[2 * c : 2 * c + 2, :]
        field_ref[c, 18:20, :] = after_ref[2 * c : 2 * c + 2, :]
    fill_taps(build_ref, state_low, (field_ref[0], field_ref[1]), 1)
    w1 = w1_ref[...]
    turn_ref[...] = w1.T[:160].astype(bf16)
    w1_out[...] = w1[:, :160].astype(bf16)
    w2_out[...] = w2_ref[:, :160].astype(bf16)


def closure_kernel(
    w1_ref, w2_ref, turn_ref, state_ref, field_ref, dft_ref, twist_ref, take1_ref, take2_ref,
    in_ref,
    out_ref,
    proj_ref, build_ref, state_low, scaled_low, grads, acts,
):
    back_part(in_ref, dft_ref, twist_ref, proj_ref)
    state_low[0:160, :] = state_ref[...]
    state_low[160:256, :] = jnp.zeros((96, NX), bf16)
    scaled_low[160:256, :] = jnp.zeros((96, NX), bf16)
    fill_taps(build_ref, scaled_low, (STEP * proj_ref[0], STEP * proj_ref[1]), -1)
    active = jnp.tanh(dot(w1_ref[...], state_ref[...]))
    acts[...] = active[32:544].astype(bf16)
    back = dot(w2_ref[...], scaled_low[0:160, :])
    grads[...] = (back * (1.0 - active * active)).astype(bf16)
    build_ref[...] = dot(turn_ref[...], grads[...])
    first_sums = dot(grads[32:544, :], state_low[...], NT)
    second_sums = dot(acts[...], scaled_low[...], NT)
    lane = lax.broadcasted_iota(jnp.int32, (FEATS, 256), 1)
    total1 = total2 = plain = jnp.zeros((FEATS, 256), f32)
    for j in range(16):
        rows = slice(32 * j, 32 * j + 32)
        total1 = total1 + pltpu.roll(first_sums[rows], 255 - j, 1)
        total2 = total2 + pltpu.roll(second_sums[rows], 255 - j, 1)
        plain = plain + first_sums[rows]
    total1 = jnp.where(lane >= 6 * WIDE, plain, total1)
    high1, low1 = split(total1)
    high2, low2 = split(total2)
    packed = (dot(high1, take1_ref[...]) + dot(low1, take1_ref[...])) + (
        dot(high2, take2_ref[...]) + dot(low2, take2_ref[...])
    )
    turned = jnp.concatenate([packed, jnp.zeros((96, 128), f32)], 0).T
    ten = turned[0:10]
    for g in range(1, 4):
        ten = ten + pltpu.roll(turned[10 * g : 10 * g + 10], 32 * g, 1)
    for r in range(8):
        out_ref[r, 32:40, 0:128] = ten[0:8]
        out_ref[r, 32:34, 128:256] = ten[8:10]
        out_ref[r, 34:40, 128:256] = jnp.zeros((6, 128), f32)

    inner, up, down = slice(2, 18), slice(3, 19), slice(1, 17)
    su = field_ref[0, inner, :]
    along_x, along_y = [], []
    for c in range(2):
        mine = field_ref[c, inner, :]
        along_x.append(0.5 * (ahead_of(mine) - behind_of(mine)))
        along_y.append(0.5 * (field_ref[c, up, :] - field_ref[c, down, :]))
    along = (along_x, along_y)
    centre = [STEP * proj_ref[c, inner, :] for c in range(2)]
    for c in range(2):
        mine = centre[c]
        above = STEP * proj_ref[c, up, :]
        below = STEP * proj_ref[c, down, :]
        carried = su * mine
        total = 0.5 * (ahead_of(carried) - behind_of(carried))
        total = total + 0.5 * (field_ref[1, up, :] * above - field_ref[1, down, :] * below)
        total = total - (centre[0] * along[c][0] + centre[1] * along[c][1])
        total = total + (ahead_of(mine) + behind_of(mine) + above + below - 4.0 * mine)
        total = total + proj_ref[c, inner, :]
        for a, move in enumerate((ahead_of, None, behind_of)):
            row = (2 * a + c) * WIDE
            part = build_ref[row + 2 : row + 18, :]
            total = total + (move(part) if move else part)
        for r in range(8):
            out_ref[r, 16 * c : 16 * c + 16, :] = total[:, 256 * r : 256 * r + 256]


def unpack_kernel(in_ref, out_ref, part_ref):
    total = in_ref[0, 32:40, :]
    for r in range(1, 8):
        total = total + in_ref[r, 32:40, :]
    ten = jnp.concatenate([total[:, 0:128], total[0:2, 128:256]], 0)
    for d in range(COLS):
        part_ref[10 * d : 10 * d + 10, :] = ten
    for c in range(2):
        lines = jnp.concatenate([in_ref[r, 16 * c : 16 * c + 16, :] for r in range(8)], 0)
        out_ref[c] = lines.T


def sums_kernel(in_ref, first_ref, second_ref, bias_ref):
    total = in_ref[0:10, :]
    for d in range(1, COLS):
        total = total + in_ref[10 * d : 10 * d + 10, :]
    total = total * (1.0 / math.sqrt(NX * NY))
    moved = [total] + [pltpu.roll(total, 128 - 32 * g, 1) for g in range(1, 4)]
    first_ref[0:10, :] = moved[0][:, 0:32]
    first_ref[10:18, :] = moved[1][0:8, 0:32]
    bias_ref[...] = moved[1][8:9, 0:32]
    second_ref[0:1, :] = moved[1][9:10, 0:32]
    second_ref[1:11, :] = moved[2][:, 0:32]
    second_ref[11:18, :] = moved[3][0:7, 0:32]


def call(kernel, outs, scratch=(), scalars=0, count=0, name=None, remote=0, mib=8):
    space = [pl.BlockSpec(memory_space=pltpu.SMEM)] * scalars
    space += [pl.BlockSpec(memory_space=pltpu.HBM)] * remote
    space += [pl.BlockSpec(memory_space=pltpu.VMEM)] * (count - scalars - remote)
    many = isinstance(outs, (list, tuple))
    out_space = pl.BlockSpec(memory_space=pltpu.VMEM)
    return pl.pallas_call(
        kernel,
        out_shape=outs,
        in_specs=space,
        out_specs=[out_space] * len(outs) if many else out_space,
        scratch_shapes=list(scratch),
        compiler_params=pltpu.CompilerParams(vmem_limit_bytes=mib * 2**20),
        name=name,
    )


def shape(*dims, dtype=f32):
    return jax.ShapeDtypeStruct(dims, dtype)


def shards(state, cotangent, first_kernel, first_bias, second_kernel):
    t = tables()
    first_pick, second_pick, first_take, second_take = picks()
    dft, group, twist_y, twist_x = (
        jnp.asarray(t[k]) for k in ("dft", "group", "twist_y", "twist_x")
    )
    every = ("col", "row")
    place = (lax.axis_index("col") * ROWS + lax.axis_index("row")).astype(jnp.int32).reshape(1)
    lanes = lax.broadcasted_iota(jnp.int32, (FEATS, 256), 1)
    bias = jnp.where(lanes >= 6 * WIDE, first_bias[:, None], 0.0)

    def exchange(values, axis):
        return lax.all_to_all(values, axis, 0, 0, tiled=True)

    space = [pltpu.VMEM((4, 256, 128), f32), pltpu.SemaphoreType.DMA((5,))]
    packed, twist_x = call(
        pack_kernel, [shape(8, 64, 256), shape(8, 256)], space, count=3, name="pack", remote=3
    )(far(cotangent), far(state), far(twist_x))
    lines = exchange(packed, "row")
    modes, low, high = call(
        ahead_kernel, [shape(512, 128), shape(4, NX), shape(4, NX)],
        count=3, name="ahead",
    )(dft, twist_x, lines)
    order = [(i % ROWS) * COLS + i // ROWS for i in range(DEV)]
    up = [(order[i], order[(i + 1) % DEV]) for i in range(DEV)]
    before = lax.ppermute(high, ("row", "col"), up)
    after = lax.ppermute(low, ("row", "col"), [(j, i) for i, j in up])
    modes = exchange(modes.reshape(DEV, 2, 128), every).reshape(512, 128)
    keep, mix = call(
        waves_kernel, [shape(256, 128), shape(256, 128)], scalars=1, count=1, name="waves"
    )(place)
    modes, before, after = lax.optimization_barrier((modes, before, after))
    modes = call(middle_kernel, shape(768, 128), scalars=1, count=7, name="middle")(place, dft, twist_y, group, modes, keep, mix)
    modes = exchange(modes.reshape(DEV, 1, 384), every).reshape(768, 128)
    prepared = call(
        state_kernel,
        [
            shape(576, 160, dtype=bf16), shape(576, 160, dtype=bf16),
            shape(160, 576, dtype=bf16), shape(160, NX, dtype=bf16), shape(2, WIDE, NX),
        ],
        [pltpu.VMEM((160, NX), f32), pltpu.VMEM((576, 256), f32), pltpu.VMEM((576, 256), f32)],
        count=8,
        name="state",
    )(lines, before, after, first_kernel, bias, second_kernel, first_pick, second_pick)
    scratch = [
        pltpu.VMEM((2, WIDE, NX), f32),
        pltpu.VMEM((160, NX), f32),
        pltpu.VMEM((256, NX), bf16),
        pltpu.VMEM((256, NX), bf16),
        pltpu.VMEM((576, NX), bf16),
        pltpu.VMEM((512, NX), bf16),
    ]
    result = call(
        closure_kernel, shape(8, 40, 256), scratch, count=10, name="closure", mib=40
    )(*prepared, dft, twist_x, first_take, second_take, modes)
    result = exchange(result, "row")
    grad_state, part = call(
        unpack_kernel, [shape(2, 256, 128), shape(320, 128)], count=1, name="unpack"
    )(result)
    part = exchange(part.reshape(COLS, 1, 1280), "col").reshape(320, 128)
    grad_first, grad_second, grad_bias = call(
        sums_kernel, [shape(18, 32), shape(18, 32), shape(1, 32)], count=1, name="sums"
    )(part)
    return grad_state, grad_first, grad_second.T, grad_bias.reshape(32)


def solution(mesh):
    placed = (P(None, "row", "col"), P(None, "row", "col"), P(), P(), P())
    return jax.shard_map(
        shards,
        mesh=mesh,
        in_specs=placed,
        out_specs=(P(None, "row", "col"), P(), P(), P()),
        check_vma=False,
    )
```

```python
import math

import jax
import jax.numpy as jnp
import numpy as np
from jax import lax
from jax.experimental import pallas as pl
from jax.experimental.pallas import tpu as pltpu
from jax.sharding import PartitionSpec as P

NX, NY = 2048, 4096
ROWS, COLS = 8, 32
DEV = ROWS * COLS
FEATS = 32
WIDE = 24
f32, bf16 = jnp.float32, jnp.bfloat16
STEP = 0.1
NT = (((1,), (1,)), ((), ()))
NN = (((1,), (0,)), ((), ()))


def pair(table):
    high = table.astype(jnp.bfloat16)
    low = (table - high.astype(np.float64)).astype(jnp.bfloat16)
    return np.stack([high, low])


def tables():
    index = np.arange(256)
    angle = 2 * np.pi * (np.outer(index, index) % 256) / 256
    dft = pair(np.concatenate([np.cos(angle), np.sin(angle)]))
    small = 2 * np.pi * (np.outer(np.arange(16), np.arange(16)) % 16) / 16
    eye = np.eye(8)
    group = np.concatenate([np.kron(eye, np.cos(small)), np.kron(eye, np.sin(small))], 1)
    twist_y = 2 * np.pi * np.outer(index, np.arange(128) % 16) / NY
    twist_x = 2 * np.pi * np.outer(np.arange(1, 5), index) / NX
    return dict(
        dft=dft,
        group=pair(group),
        twist_y=np.stack([np.cos(twist_y), np.sin(twist_y)]).astype(np.float32),
        twist_x=np.concatenate([np.cos(twist_x), np.sin(twist_x)]).astype(np.float32),
    )


def picks():
    first = np.zeros((18, 256))
    second = np.zeros((18, 256))
    out_first = np.zeros((256, 128))
    out_second = np.zeros((256, 128))
    for a in range(3):
        for b in range(3):
            for c in range(2):
                row = 2 * (3 * a + b) + c
                lane = (2 * a + c) * WIDE
                first[row, lane + b] = 1
                second[row, lane + 2 - b] = 1
                out_first[lane + b, row] = 1
                out_second[lane + 2 - b, 19 + row] = 1
    out_first[6 * WIDE, 18] = 1
    return [x.astype(jnp.bfloat16) for x in (first, second, out_first, out_second)]


def split(values):
    high = values.astype(bf16)
    return high, (values - high.astype(f32)).astype(bf16)


def dot(left, right, dims=NN):
    return lax.dot_general(left, right, dims, preferred_element_type=f32)


def left_dot(table_ref, values, dims=NN):
    high, low = split(values)
    dim = dims[0][1][0] ^ 1
    size = values.shape[dim]
    wide = dot(table_ref[0], jnp.concatenate([high, low], dim), dims)
    both = wide[:, :size] + (wide[:, size:] + dot(table_ref[1], high, dims))
    return both[:256], both[256:]


def right_dot(values, high_table, low_table, dims=NN):
    high, low = split(values)
    size = values.shape[0]
    tall = dot(jnp.concatenate([high, low], 0), high_table, dims)
    return tall[:size] + (tall[size:] + dot(high, low_table, dims))


def far(values):
    return pltpu.with_memory_space_constraint(values, pltpu.HBM)


def pack_kernel(cot_ref, state_ref, twist_far, out_ref, twist_ref, buffer_ref, sems):
    copies = []
    twist_copy = pltpu.make_async_copy(twist_far, twist_ref, sems.at[4])
    for f, ref in enumerate((cot_ref, state_ref)):
        for c in range(2):
            k = 2 * f + c
            copies.append(pltpu.make_async_copy(ref.at[c], buffer_ref.at[k], sems.at[k]))
    for copy in copies:
        copy.start()
    twist_copy.start()
    for k, copy in enumerate(copies):
        copy.wait()
        turned = buffer_ref[k].T
        for r in range(ROWS):
            out_ref[r, 16 * k : 16 * k + 16, :] = turned[16 * r : 16 * r + 16]
    twist_copy.wait()


def ahead_kernel(dft_ref, twist_ref, in_ref, out_ref, low_ref, high_ref):
    u = [in_ref[r, 0:32, :] for r in range(8)]
    root = math.sqrt(0.5)
    a, b, c, d = (u[k] - u[k + 4] for k in range(4))
    e0, e1, e2, e3 = (u[k] + u[k + 4] for k in range(4))
    s0, s1 = e0 + e2, e1 + e3
    parts = [
        (a + root * (b - d), -c - root * (b + d)),
        (e0 - e2, e3 - e1),
        (a - root * (b - d), c - root * (b + d)),
    ]
    reals, imags = [], []
    for k, (re, im) in enumerate(parts):
        cos, sin = twist_ref[k : k + 1, :], twist_ref[4 + k : 5 + k, :]
        reals.append(re * cos + im * sin)
        imags.append(im * cos - re * sin)
    even, odd = s0 + s1, s0 - s1
    zero = jnp.zeros_like(even)
    last_re = odd * twist_ref[3:4, :]
    last_im = -odd * twist_ref[7:8, :]
    stack = jnp.concatenate(
        reals + [even] + imags + [zero] + [zero] * 3 + [last_re] + [zero] * 3 + [last_im], 0
    )
    cosine, sine = left_dot(dft_ref, stack, NT)
    main_re = cosine[:, 0:128] + sine[:, 128:256]
    main_im = cosine[:, 128:256] - sine[:, 0:128]
    odd_re = cosine[:128, 256:384] + sine[:128, 384:512]
    odd_im = cosine[:128, 384:512] - sine[:128, 256:384]
    lane = lax.broadcasted_iota(jnp.int32, (128, 128), 1)
    row = lax.broadcasted_iota(jnp.int32, (128, 128), 0)
    last = lane >= 96
    edge = last & (row == 0)
    top_re = jnp.where(edge, main_re[128:129], main_re[:128])
    top_im = jnp.where(edge, main_re[0:1], main_im[:128])
    out_ref[pl.ds(0, 128, 2), :] = top_re
    out_ref[pl.ds(1, 128, 2), :] = top_im
    out_ref[pl.ds(256, 128, 2), :] = jnp.where(last, odd_re, main_re[128:])
    out_ref[pl.ds(257, 128, 2), :] = jnp.where(last, odd_im, main_im[128:])
    for r in range(8):
        for ch in range(2):
            row0 = 32 + 16 * ch
            low_ref[2 * ch : 2 * ch + 2, 256 * r : 256 * r + 256] = in_ref[r, row0 : row0 + 2, :]
            high_ref[2 * ch : 2 * ch + 2, 256 * r : 256 * r + 256] = in_ref[
                r, row0 + 14 : row0 + 16, :
            ]


def waves_kernel(place_ref, keep_ref, mix_ref):
    place = place_ref[0]
    lane = lax.broadcasted_iota(jnp.int32, (256, 128), 1)
    row = lax.broadcasted_iota(jnp.int32, (256, 128), 0)
    slot = lane // 32
    plain = 8 * place + slot + 1
    last = jnp.where(place == 0, NX // 2, jnp.where(place < 128, 8 * place, 8 * place - 1020))
    mx = jnp.where(slot == 3, last, plain)
    mx = jnp.where(mx >= NX // 2, mx - NX, mx)
    my = row + 256 * (lane % 16)
    my = jnp.where(my >= NY // 2, my - NY, my)
    kx = mx.astype(f32) * (1.0 / NX)
    ky = my.astype(f32) * (1.0 / NY)
    inverse = 1.0 / (kx * kx + ky * ky)
    cross = jnp.where((mx == -(NX // 2)) | (my == -(NY // 2)), 0.0, kx * ky)
    own = jnp.where((lane & 16) == 0, kx * kx, ky * ky)
    keep_ref[...] = 1.0 - own * inverse
    mix_ref[...] = -cross * inverse


def swap16(values, lane):
    return jnp.where((lane & 16) == 0, pltpu.roll(values, 112, 1), pltpu.roll(values, 16, 1))


def middle_kernel(
    place_ref, dft_ref, twist_ref, group_ref, in_ref, keep_ref, mix_ref, out_ref
):
    place = place_ref[0]
    re, im = in_ref[pl.ds(0, 256, 2), :], in_ref[pl.ds(1, 256, 2), :]
    both = jnp.concatenate([re, im], 1)
    cosine, sine = left_dot(dft_ref, both)
    f_re, f_im = cosine[:, :128] + sine[:, 128:], cosine[:, 128:] - sine[:, :128]
    cos, sin = twist_ref[0], twist_ref[1]
    t_re, t_im = f_re * cos + f_im * sin, f_im * cos - f_re * sin
    g = right_dot(jnp.concatenate([t_re, t_im], 0), group_ref[0], group_ref[1])
    g_re, g_im = g[:256, :128] + g[256:, 128:], g[256:, :128] - g[:256, 128:]
    keep, mix = keep_ref[...], mix_ref[...]
    lane = lax.broadcasted_iota(jnp.int32, (256, 128), 1)
    p_re = keep * g_re + mix * swap16(g_re, lane)
    p_im = keep * g_im + mix * swap16(g_im, lane)
    h = right_dot(jnp.concatenate([p_re, p_im], 0), group_ref[0], group_ref[1])
    h_re, h_im = h[:256, :128] - h[256:, 128:], h[256:, :128] + h[:256, 128:]
    t_re, t_im = h_re * cos - h_im * sin, h_im * cos + h_re * sin
    both = jnp.concatenate([t_re, t_im], 1)
    cosine, sine = left_dot(dft_ref, both)
    scale = 1.0 / (NX * NY)
    o_re = (cosine[:, :128] - sine[:, 128:]) * scale
    o_im = (cosine[:, 128:] + sine[:, :128]) * scale
    sums = jnp.sum(im, 0, keepdims=True)
    sums = jnp.where(lane[:1] >= 112, sums, 0.0)
    mean = jnp.sum(sums, 1, keepdims=True) * scale
    zeroth = (lane >= 96) & (place == 0)
    o_im = jnp.where(zeroth, jnp.where(lane >= 112, mean, im * (1.0 / NX)), o_im)
    near = (lane & 8) == 0
    outer = ((lane + 2) & 15) < 4

    def beside(values):
        return jnp.where(near, pltpu.roll(values, 255, 0), pltpu.roll(values, 1, 0))

    out_ref[pl.ds(0, 256, 3), :] = o_re
    out_ref[pl.ds(1, 256, 3), :] = o_im
    edge_im = beside(o_im)
    edge_im = jnp.where(near, pltpu.roll(edge_im, 4, 1), pltpu.roll(edge_im, 124, 1))
    out_ref[pl.ds(2, 256, 3), :] = jnp.where(outer, beside(o_re), edge_im)


def back_part(in_ref, dft_ref, twist_ref, out_ref):
    lane = lax.broadcasted_iota(jnp.int32, (128, 128), 1)
    row = lax.broadcasted_iota(jnp.int32, (128, 128), 0)
    last = lane >= 96
    edge = last & (row == 0)
    near = (lane & 8) == 0
    outer = ((lane + 2) & 15) < 4
    top_re, top_im, top_h = (in_ref[pl.ds(k, 128, 3), :] for k in range(3))
    low_re, low_im, low_h = (in_ref[pl.ds(384 + k, 128, 3), :] for k in range(3))
    head = top_h[0:1]
    head_im = jnp.where(near[0:1], pltpu.roll(head, 124, 1), pltpu.roll(head, 4, 1))
    half_im = jnp.where(outer[0:1], 0.5 * head_im, 0.0)
    half_re = jnp.where(outer[0:1], 0.5 * head, 0.0)
    nyquist = jnp.where(edge, 0.5 * top_re[0:1], 0.0)
    mains = [
        jnp.concatenate(
            [jnp.where(edge, 0.5 * top_im, top_re), jnp.where(last, nyquist, low_re)], 0
        ),
        jnp.concatenate([jnp.where(edge, 0.0, top_im), jnp.where(last, 0.0, low_im)], 0),
        jnp.concatenate(
            [
                jnp.where(edge, half_im, top_h),
                jnp.where(last, jnp.where(edge, half_re, 0.0), low_h),
            ],
            0,
        ),
    ]
    main = right_dot(jnp.concatenate(mains, 1).T, dft_ref[0], dft_ref[1], NT)
    odd = jnp.concatenate([low_re, low_im, low_h], 1).T
    odd = jnp.concatenate([odd[128 * k + 96 : 128 * k + 128] for k in range(3)], 0)
    odd = right_dot(odd, dft_ref[0][:, :128], dft_ref[1][:, :128], NT)
    m_cos, m_sin, o_cos, o_sin = main[:, :256], main[:, 256:], odd[:, :256], odd[:, 256:]
    root = math.sqrt(0.5)

    def imag_rows(values):
        rows = values.shape[0]
        near_row = (lax.broadcasted_iota(jnp.int32, values.shape, 0) & 8) == 0
        return jnp.where(near_row, pltpu.roll(values, rows - 4, 0), pltpu.roll(values, 4, 0))

    for k in (0, 256):
        if k == 0:
            re, im = m_cos[0:128] - m_sin[128:256], m_cos[128:256] + m_sin[0:128]
            last_re, last_im = o_cos[0:32] - o_sin[32:64], o_cos[32:64] + o_sin[0:32]
        else:
            m_c, m_s, o_c, o_s = m_cos[256:384], m_sin[256:384], o_cos[64:96], o_sin[64:96]
            re, im = m_c - imag_rows(m_s), imag_rows(m_c) + m_s
            last_re, last_im = o_c - imag_rows(o_s), imag_rows(o_c) + o_s
        w4 = last_re * twist_ref[3:4, :] - last_im * twist_ref[7:8, :]
        w0 = re[96:128]
        ws = []
        for p in range(3):
            cos, sin = twist_ref[p : p + 1, :], twist_ref[4 + p : 5 + p, :]
            r_p, i_p = re[32 * p : 32 * p + 32], im[32 * p : 32 * p + 32]
            ws.append((r_p * cos - i_p * sin, i_p * cos + r_p * sin))
        for r in range(8):
            total = w0 + w4 if r % 2 == 0 else w0 - w4
            for p in range(3):
                turn_by = (r * (p + 1)) % 8
                cos_r = [1.0, root, 0.0, -root, -1.0, -root, 0.0, root][turn_by]
                sin_r = [0.0, root, 1.0, root, 0.0, -root, -1.0, -root][turn_by]
                if cos_r:
                    total = total + cos_r * ws[p][0]
                if sin_r:
                    total = total - sin_r * ws[p][1]
            total = total + total
            lanes = slice(256 * r, 256 * r + 256)
            for ch in range(2):
                if k == 0:
                    out_ref[ch, 2:18, lanes] = total[16 * ch : 16 * ch + 16]
                else:
                    out_ref[ch, 0:2, lanes] = total[16 * ch + 14 : 16 * ch + 16]
                    out_ref[ch, 18:20, lanes] = total[16 * ch : 16 * ch + 2]
                    if r == 0:
                        out_ref[ch, 20:24, :] = jnp.zeros((4, NX), f32)


def ahead_of(values):
    return pltpu.roll(values, NX - 1, 1)


def behind_of(values):
    return pltpu.roll(values, 1, 1)


def fill_taps(build_ref, target, fields, sign):
    for c in range(2):
        whole = fields[c]
        moves = (behind_of(whole), whole, ahead_of(whole))[::sign]
        for a in range(3):
            row = (2 * a + c) * WIDE
            build_ref[row : row + WIDE, :] = moves[a]
    build_ref[144:152, :] = jnp.ones((8, NX), f32)
    build_ref[152:160, :] = jnp.zeros((8, NX), f32)
    target[0:160, :] = build_ref[...].astype(bf16)


def state_kernel(
    own_ref, before_ref, after_ref, first_ref, bias_ref, second_ref, pick1_ref, pick2_ref,
    w1_out, w2_out, turn_ref, state_low, field_ref,
    build_ref, w1_ref, w2_ref,
):
    lane = lax.broadcasted_iota(jnp.int32, (FEATS, 256), 1)
    bias = bias_ref[...]
    bias_high = bias.astype(bf16).astype(f32)
    bias_part = jnp.where(
        lane == 6 * WIDE, bias_high, jnp.where(lane == 6 * WIDE + 1, bias - bias_high, 0.0)
    )
    base1 = dot(first_ref[...].astype(f32).T.astype(bf16), pick1_ref[...])
    base2 = dot(second_ref[...], pick2_ref[...])
    for j in range(18):
        rows = slice(32 * j, 32 * j + 32)
        moved1 = pltpu.roll(base1, j, 1) if j else base1
        moved2 = pltpu.roll(base2, j, 1) if j else base2
        w1_ref[rows, :] = moved1 + bias_part
        w2_ref[rows, :] = moved2
    for c in range(2):
        field_ref[c, 20:24, :] = jnp.zeros((4, NX), f32)
        for r in range(8):
            field_ref[c, 2:18, 256 * r : 256 * r + 256] = own_ref[
                r, 32 + 16 * c : 48 + 16 * c, :
            ]
        field_ref[c, 0:2, :] = before_ref[2 * c : 2 * c + 2, :]
        field_ref[c, 18:20, :] = after_ref[2 * c : 2 * c + 2, :]
    fill_taps(build_ref, state_low, (field_ref[0], field_ref[1]), 1)
    w1 = w1_ref[...]
    turn_ref[...] = w1.T[:160].astype(bf16)
    w1_out[...] = w1[:, :160].astype(bf16)
    w2_out[...] = w2_ref[:, :160].astype(bf16)


def closure_kernel(
    w1_ref, w2_ref, turn_ref, state_ref, field_ref, dft_ref, twist_ref, take1_ref, take2_ref,
    in_ref,
    out_ref,
    proj_ref, build_ref, state_low, scaled_low, grads, acts,
):
    back_part(in_ref, dft_ref, twist_ref, proj_ref)
    state_low[0:160, :] = state_ref[...]
    state_low[160:256, :] = jnp.zeros((96, NX), bf16)
    scaled_low[160:256, :] = jnp.zeros((96, NX), bf16)
    fill_taps(build_ref, scaled_low, (STEP * proj_ref[0], STEP * proj_ref[1]), -1)
    active = jnp.tanh(dot(w1_ref[...], state_ref[...]))
    acts[...] = active[32:544].astype(bf16)
    back = dot(w2_ref[...], scaled_low[0:160, :])
    grads[...] = (back * (1.0 - active * active)).astype(bf16)
    build_ref[...] = dot(turn_ref[...], grads[...])
    first_sums = dot(grads[32:544, :], state_low[...], NT)
    second_sums = dot(acts[...], scaled_low[...], NT)
    lane = lax.broadcasted_iota(jnp.int32, (FEATS, 256), 1)
    total1 = total2 = plain = jnp.zeros((FEATS, 256), f32)
    for j in range(16):
        rows = slice(32 * j, 32 * j + 32)
        total1 = total1 + pltpu.roll(first_sums[rows], 255 - j, 1)
        total2 = total2 + pltpu.roll(second_sums[rows], 255 - j, 1)
        plain = plain + first_sums[rows]
    total1 = jnp.where(lane >= 6 * WIDE, plain, total1)
    high1, low1 = split(total1)
    high2, low2 = split(total2)
    packed = (dot(high1, take1_ref[...]) + dot(low1, take1_ref[...])) + (
        dot(high2, take2_ref[...]) + dot(low2, take2_ref[...])
    )
    turned = jnp.concatenate([packed, jnp.zeros((96, 128), f32)], 0).T
    ten = turned[0:10]
    for g in range(1, 4):
        ten = ten + pltpu.roll(turned[10 * g : 10 * g + 10], 32 * g, 1)
    for r in range(8):
        out_ref[r, 32:40, 0:128] = ten[0:8]
        out_ref[r, 32:34, 128:256] = ten[8:10]
        out_ref[r, 34:40, 128:256] = jnp.zeros((6, 128), f32)

    inner, up, down = slice(2, 18), slice(3, 19), slice(1, 17)
    su = field_ref[0, inner, :]
    along_x, along_y = [], []
    for c in range(2):
        mine = field_ref[c, inner, :]
        along_x.append(0.5 * (ahead_of(mine) - behind_of(mine)))
        along_y.append(0.5 * (field_ref[c, up, :] - field_ref[c, down, :]))
    along = (along_x, along_y)
    centre = [STEP * proj_ref[c, inner, :] for c in range(2)]
    for c in range(2):
        mine = centre[c]
        above = STEP * proj_ref[c, up, :]
        below = STEP * proj_ref[c, down, :]
        carried = su * mine
        total = 0.5 * (ahead_of(carried) - behind_of(carried))
        total = total + 0.5 * (field_ref[1, up, :] * above - field_ref[1, down, :] * below)
        total = total - (centre[0] * along[c][0] + centre[1] * along[c][1])
        total = total + (ahead_of(mine) + behind_of(mine) + above + below - 4.0 * mine)
        total = total + proj_ref[c, inner, :]
        for a, move in enumerate((ahead_of, None, behind_of)):
            row = (2 * a + c) * WIDE
            part = build_ref[row + 2 : row + 18, :]
            total = total + (move(part) if move else part)
        for r in range(8):
            out_ref[r, 16 * c : 16 * c + 16, :] = total[:, 256 * r : 256 * r + 256]


def unpack_kernel(in_ref, out_ref, part_ref):
    total = in_ref[0, 32:40, :]
    for r in range(1, 8):
        total = total + in_ref[r, 32:40, :]
    ten = jnp.concatenate([total[:, 0:128], total[0:2, 128:256]], 0)
    for d in range(COLS):
        part_ref[10 * d : 10 * d + 10, :] = ten
    for c in range(2):
        lines = jnp.concatenate([in_ref[r, 16 * c : 16 * c + 16, :] for r in range(8)], 0)
        out_ref[c] = lines.T


def sums_kernel(in_ref, first_ref, second_ref, bias_ref):
    total = in_ref[0:10, :]
    for d in range(1, COLS):
        total = total + in_ref[10 * d : 10 * d + 10, :]
    total = total * (1.0 / math.sqrt(NX * NY))
    moved = [total] + [pltpu.roll(total, 128 - 32 * g, 1) for g in range(1, 4)]
    first_ref[0:10, :] = moved[0][:, 0:32]
    first_ref[10:18, :] = moved[1][0:8, 0:32]
    bias_ref[...] = moved[1][8:9, 0:32]
    second_ref[0:1, :] = moved[1][9:10, 0:32]
    second_ref[1:11, :] = moved[2][:, 0:32]
    second_ref[11:18, :] = moved[3][0:7, 0:32]


def call(kernel, outs, scratch=(), scalars=0, count=0, name=None, remote=0, mib=8):
    space = [pl.BlockSpec(memory_space=pltpu.SMEM)] * scalars
    space += [pl.BlockSpec(memory_space=pltpu.HBM)] * remote
    space += [pl.BlockSpec(memory_space=pltpu.VMEM)] * (count - scalars - remote)
    many = isinstance(outs, (list, tuple))
    out_space = pl.BlockSpec(memory_space=pltpu.VMEM)
    return pl.pallas_call(
        kernel,
        out_shape=outs,
        in_specs=space,
        out_specs=[out_space] * len(outs) if many else out_space,
        scratch_shapes=list(scratch),
        compiler_params=pltpu.CompilerParams(vmem_limit_bytes=mib * 2**20),
        name=name,
    )


def shape(*dims, dtype=f32):
    return jax.ShapeDtypeStruct(dims, dtype)


def shards(state, cotangent, first_kernel, first_bias, second_kernel):
    t = tables()
    first_pick, second_pick, first_take, second_take = picks()
    dft, group, twist_y, twist_x = (
        jnp.asarray(t[k]) for k in ("dft", "group", "twist_y", "twist_x")
    )
    every = ("col", "row")
    place = (lax.axis_index("col") * ROWS + lax.axis_index("row")).astype(jnp.int32).reshape(1)
    lanes = lax.broadcasted_iota(jnp.int32, (FEATS, 256), 1)
    bias = jnp.where(lanes >= 6 * WIDE, first_bias[:, None], 0.0)

    def exchange(values, axis):
        return lax.all_to_all(values, axis, 0, 0, tiled=True)

    space = [pltpu.VMEM((4, 256, 128), f32), pltpu.SemaphoreType.DMA((5,))]
    packed, twist_x = call(
        pack_kernel, [shape(8, 64, 256), shape(8, 256)], space, count=3, name="pack", remote=3
    )(far(cotangent), far(state), far(twist_x))
    lines = exchange(packed, "row")
    modes, low, high = call(
        ahead_kernel, [shape(512, 128), shape(4, NX), shape(4, NX)],
        count=3, name="ahead",
    )(dft, twist_x, lines)
    order = [(i % ROWS) * COLS + i // ROWS for i in range(DEV)]
    up = [(order[i], order[(i + 1) % DEV]) for i in range(DEV)]
    before = lax.ppermute(high, ("row", "col"), up)
    after = lax.ppermute(low, ("row", "col"), [(j, i) for i, j in up])
    modes = exchange(modes.reshape(DEV, 1, 256), every).reshape(512, 128)
    keep, mix = call(
        waves_kernel, [shape(256, 128), shape(256, 128)], scalars=1, count=1, name="waves"
    )(place)
    modes, before, after = lax.optimization_barrier((modes, before, after))
    modes = call(middle_kernel, shape(768, 128), scalars=1, count=7, name="middle")(place, dft, twist_y, group, modes, keep, mix)
    modes = exchange(modes.reshape(DEV, 1, 384), every).reshape(768, 128)
    prepared = call(
        state_kernel,
        [
            shape(576, 160, dtype=bf16), shape(576, 160, dtype=bf16),
            shape(160, 576, dtype=bf16), shape(160, NX, dtype=bf16), shape(2, WIDE, NX),
        ],
        [pltpu.VMEM((160, NX), f32), pltpu.VMEM((576, 256), f32), pltpu.VMEM((576, 256), f32)],
        count=8,
        name="state",
    )(lines, before, after, first_kernel, bias, second_kernel, first_pick, second_pick)
    scratch = [
        pltpu.VMEM((2, WIDE, NX), f32),
        pltpu.VMEM((160, NX), f32),
        pltpu.VMEM((256, NX), bf16),
        pltpu.VMEM((256, NX), bf16),
        pltpu.VMEM((576, NX), bf16),
        pltpu.VMEM((512, NX), bf16),
    ]
    result = call(
        closure_kernel, shape(8, 40, 256), scratch, count=10, name="closure", mib=40
    )(*prepared, dft, twist_x, first_take, second_take, modes)
    result = exchange(result, "row")
    grad_state, part = call(
        unpack_kernel, [shape(2, 256, 128), shape(320, 128)], count=1, name="unpack"
    )(result)
    part = exchange(part.reshape(COLS, 1, 1280), "col").reshape(320, 128)
    grad_first, grad_second, grad_bias = call(
        sums_kernel, [shape(18, 32), shape(18, 32), shape(1, 32)], count=1, name="sums"
    )(part)
    return grad_state, grad_first, grad_second.T, grad_bias.reshape(32)


def solution(mesh):
    placed = (P(None, "row", "col"), P(None, "row", "col"), P(), P(), P())
    return jax.shard_map(
        shards,
        mesh=mesh,
        in_specs=placed,
        out_specs=(P(None, "row", "col"), P(), P(), P()),
        check_vma=False,
    )
```

```python
import math

import jax
import jax.numpy as jnp
import numpy as np
from jax import lax
from jax.experimental import pallas as pl
from jax.experimental.pallas import tpu as pltpu
from jax.sharding import PartitionSpec as P

NX, NY = 2048, 4096
ROWS, COLS = 8, 32
DEV = ROWS * COLS
FEATS = 32
WIDE = 24
f32, bf16 = jnp.float32, jnp.bfloat16
STEP = 0.1
NT = (((1,), (1,)), ((), ()))
NN = (((1,), (0,)), ((), ()))


def pair(table):
    high = table.astype(jnp.bfloat16)
    low = (table - high.astype(np.float64)).astype(jnp.bfloat16)
    return np.stack([high, low])


def tables():
    index = np.arange(256)
    angle = 2 * np.pi * (np.outer(index, index) % 256) / 256
    dft = pair(np.concatenate([np.cos(angle), np.sin(angle)]))
    small = 2 * np.pi * (np.outer(np.arange(16), np.arange(16)) % 16) / 16
    eye = np.eye(8)
    group = np.concatenate([np.kron(eye, np.cos(small)), np.kron(eye, np.sin(small))], 1)
    twist_y = 2 * np.pi * np.outer(index, np.arange(128) % 16) / NY
    twist_x = 2 * np.pi * np.outer(np.arange(1, 5), index) / NX
    return dict(
        dft=dft,
        group=pair(group),
        twist_y=np.stack([np.cos(twist_y), np.sin(twist_y)]).astype(np.float32),
        twist_x=np.concatenate([np.cos(twist_x), np.sin(twist_x)]).astype(np.float32),
    )


def picks():
    first = np.zeros((18, 256))
    second = np.zeros((18, 256))
    out_first = np.zeros((256, 128))
    out_second = np.zeros((256, 128))
    for a in range(3):
        for b in range(3):
            for c in range(2):
                row = 2 * (3 * a + b) + c
                lane = (2 * a + c) * WIDE
                first[row, lane + b] = 1
                second[row, lane + 2 - b] = 1
                out_first[lane + b, row] = 1
                out_second[lane + 2 - b, 19 + row] = 1
    out_first[6 * WIDE, 18] = 1
    return [x.astype(jnp.bfloat16) for x in (first, second, out_first, out_second)]


def split(values):
    high = values.astype(bf16)
    return high, (values - high.astype(f32)).astype(bf16)


def dot(left, right, dims=NN):
    return lax.dot_general(left, right, dims, preferred_element_type=f32)


def left_dot(table_ref, values, dims=NN):
    high, low = split(values)
    dim = dims[0][1][0] ^ 1
    size = values.shape[dim]
    wide = dot(table_ref[0], jnp.concatenate([high, low], dim), dims)
    both = wide[:, :size] + (wide[:, size:] + dot(table_ref[1], high, dims))
    return both[:256], both[256:]


def apart_dot(table_ref, values):
    high, low = split(values)
    parts = []
    for k in (0, 256):
        t_high, t_low = table_ref[0, k : k + 256, :], table_ref[1, k : k + 256, :]
        parts.append(dot(t_high, high) + (dot(t_high, low) + dot(t_low, high)))
    return parts


def right_apart(values, table_ref):
    high, low = split(values)
    return dot(high, table_ref[0]) + (dot(low, table_ref[0]) + dot(high, table_ref[1]))


def right_dot(values, high_table, low_table, dims=NN):
    high, low = split(values)
    size = values.shape[0]
    tall = dot(jnp.concatenate([high, low], 0), high_table, dims)
    return tall[:size] + (tall[size:] + dot(high, low_table, dims))


def far(values):
    return pltpu.with_memory_space_constraint(values, pltpu.HBM)


def pack_kernel(cot_ref, state_ref, twist_far, out_ref, twist_ref, buffer_ref, sems):
    copies = []
    twist_copy = pltpu.make_async_copy(twist_far, twist_ref, sems.at[4])
    for f, ref in enumerate((cot_ref, state_ref)):
        for c in range(2):
            k = 2 * f + c
            copies.append(pltpu.make_async_copy(ref.at[c], buffer_ref.at[k], sems.at[k]))
    for copy in copies:
        copy.start()
    twist_copy.start()
    for k, copy in enumerate(copies):
        copy.wait()
        turned = buffer_ref[k].T
        for r in range(ROWS):
            out_ref[r, 16 * k : 16 * k + 16, :] = turned[16 * r : 16 * r + 16]
    twist_copy.wait()


def ahead_kernel(dft_ref, twist_ref, in_ref, out_ref, low_ref, high_ref):
    u = [in_ref[r, 0:32, :] for r in range(8)]
    root = math.sqrt(0.5)
    a, b, c, d = (u[k] - u[k + 4] for k in range(4))
    e0, e1, e2, e3 = (u[k] + u[k + 4] for k in range(4))
    s0, s1 = e0 + e2, e1 + e3
    parts = [
        (a + root * (b - d), -c - root * (b + d)),
        (e0 - e2, e3 - e1),
        (a - root * (b - d), c - root * (b + d)),
    ]
    reals, imags = [], []
    for k, (re, im) in enumerate(parts):
        cos, sin = twist_ref[k : k + 1, :], twist_ref[4 + k : 5 + k, :]
        reals.append(re * cos + im * sin)
        imags.append(im * cos - re * sin)
    even, odd = s0 + s1, s0 - s1
    zero = jnp.zeros_like(even)
    last_re = odd * twist_ref[3:4, :]
    last_im = -odd * twist_ref[7:8, :]
    stack = jnp.concatenate(
        reals + [even] + imags + [zero] + [zero] * 3 + [last_re] + [zero] * 3 + [last_im], 0
    )
    cosine, sine = left_dot(dft_ref, stack, NT)
    main_re = cosine[:, 0:128] + sine[:, 128:256]
    main_im = cosine[:, 128:256] - sine[:, 0:128]
    odd_re = cosine[:128, 256:384] + sine[:128, 384:512]
    odd_im = cosine[:128, 384:512] - sine[:128, 256:384]
    lane = lax.broadcasted_iota(jnp.int32, (128, 128), 1)
    row = lax.broadcasted_iota(jnp.int32, (128, 128), 0)
    last = lane >= 96
    edge = last & (row == 0)
    top_re = jnp.where(edge, main_re[128:129], main_re[:128])
    top_im = jnp.where(edge, main_re[0:1], main_im[:128])
    out_ref[pl.ds(0, 128, 2), :] = top_re
    out_ref[pl.ds(1, 128, 2), :] = top_im
    out_ref[pl.ds(256, 128, 2), :] = jnp.where(last, odd_re, main_re[128:])
    out_ref[pl.ds(257, 128, 2), :] = jnp.where(last, odd_im, main_im[128:])
    for r in range(8):
        for ch in range(2):
            row0 = 32 + 16 * ch
            low_ref[2 * ch : 2 * ch + 2, 256 * r : 256 * r + 256] = in_ref[r, row0 : row0 + 2, :]
            high_ref[2 * ch : 2 * ch + 2, 256 * r : 256 * r + 256] = in_ref[
                r, row0 + 14 : row0 + 16, :
            ]


def waves(place):
    lane = lax.broadcasted_iota(jnp.int32, (256, 128), 1)
    row = lax.broadcasted_iota(jnp.int32, (256, 128), 0)
    slot = lane // 32
    plain = 8 * place + slot + 1
    last = jnp.where(place == 0, NX // 2, jnp.where(place < 128, 8 * place, 8 * place - 1020))
    mx = jnp.where(slot == 3, last, plain)
    mx = jnp.where(mx >= NX // 2, mx - NX, mx)
    my = row + 256 * (lane % 16)
    my = jnp.where(my >= NY // 2, my - NY, my)
    kx = mx.astype(f32) * (1.0 / NX)
    ky = my.astype(f32) * (1.0 / NY)
    inverse = 1.0 / (kx * kx + ky * ky)
    cross = jnp.where((mx == -(NX // 2)) | (my == -(NY // 2)), 0.0, kx * ky)
    own = jnp.where((lane & 16) == 0, kx * kx, ky * ky)
    return 1.0 - own * inverse, -cross * inverse, lane


def swap16(values, lane):
    return jnp.where((lane & 16) == 0, pltpu.roll(values, 112, 1), pltpu.roll(values, 16, 1))


def middle_kernel(
    place_ref, dft_ref, twist_ref, group_ref, in_ref, out_ref
):
    place = place_ref[0]
    re, im = in_ref[pl.ds(0, 256, 2), :], in_ref[pl.ds(1, 256, 2), :]
    both = jnp.concatenate([re, im], 1)
    cosine, sine = apart_dot(dft_ref, both)
    f_re, f_im = cosine[:, :128] + sine[:, 128:], cosine[:, 128:] - sine[:, :128]
    cos, sin = twist_ref[0], twist_ref[1]
    t_re, t_im = f_re * cos + f_im * sin, f_im * cos - f_re * sin
    g = right_apart(jnp.concatenate([t_re, t_im], 0), group_ref)
    g_re, g_im = g[:256, :128] + g[256:, 128:], g[256:, :128] - g[:256, 128:]
    keep, mix, lane = waves(place)
    p_re = keep * g_re + mix * swap16(g_re, lane)
    p_im = keep * g_im + mix * swap16(g_im, lane)
    h = right_apart(jnp.concatenate([p_re, p_im], 0), group_ref)
    h_re, h_im = h[:256, :128] - h[256:, 128:], h[256:, :128] + h[:256, 128:]
    t_re, t_im = h_re * cos - h_im * sin, h_im * cos + h_re * sin
    both = jnp.concatenate([t_re, t_im], 1)
    cosine, sine = apart_dot(dft_ref, both)
    scale = 1.0 / (NX * NY)
    o_re = (cosine[:, :128] - sine[:, 128:]) * scale
    o_im = (cosine[:, 128:] + sine[:, :128]) * scale
    sums = jnp.sum(im, 0, keepdims=True)
    sums = jnp.where(lane[:1] >= 112, sums, 0.0)
    mean = jnp.sum(sums, 1, keepdims=True) * scale
    zeroth = (lane >= 96) & (place == 0)
    o_im = jnp.where(zeroth, jnp.where(lane >= 112, mean, im * (1.0 / NX)), o_im)
    near = (lane & 8) == 0
    outer = ((lane + 2) & 15) < 4

    def beside(values):
        return jnp.where(near, pltpu.roll(values, 255, 0), pltpu.roll(values, 1, 0))

    out_ref[pl.ds(0, 256, 3), :] = o_re
    out_ref[pl.ds(1, 256, 3), :] = o_im
    edge_im = beside(o_im)
    edge_im = jnp.where(near, pltpu.roll(edge_im, 4, 1), pltpu.roll(edge_im, 124, 1))
    out_ref[pl.ds(2, 256, 3), :] = jnp.where(outer, beside(o_re), edge_im)


def back_part(in_ref, dft_ref, twist_ref, out_ref):
    lane = lax.broadcasted_iota(jnp.int32, (128, 128), 1)
    row = lax.broadcasted_iota(jnp.int32, (128, 128), 0)
    last = lane >= 96
    edge = last & (row == 0)
    near = (lane & 8) == 0
    outer = ((lane + 2) & 15) < 4
    top_re, top_im, top_h = (in_ref[pl.ds(k, 128, 3), :] for k in range(3))
    low_re, low_im, low_h = (in_ref[pl.ds(384 + k, 128, 3), :] for k in range(3))
    head = top_h[0:1]
    head_im = jnp.where(near[0:1], pltpu.roll(head, 124, 1), pltpu.roll(head, 4, 1))
    half_im = jnp.where(outer[0:1], 0.5 * head_im, 0.0)
    half_re = jnp.where(outer[0:1], 0.5 * head, 0.0)
    nyquist = jnp.where(edge, 0.5 * top_re[0:1], 0.0)
    mains = [
        jnp.concatenate(
            [jnp.where(edge, 0.5 * top_im, top_re), jnp.where(last, nyquist, low_re)], 0
        ),
        jnp.concatenate([jnp.where(edge, 0.0, top_im), jnp.where(last, 0.0, low_im)], 0),
        jnp.concatenate(
            [
                jnp.where(edge, half_im, top_h),
                jnp.where(last, jnp.where(edge, half_re, 0.0), low_h),
            ],
            0,
        ),
    ]
    main = right_dot(jnp.concatenate(mains, 1).T, dft_ref[0], dft_ref[1], NT)
    odd = jnp.concatenate([low_re, low_im, low_h], 1).T
    odd = jnp.concatenate([odd[128 * k + 96 : 128 * k + 128] for k in range(3)], 0)
    odd = right_dot(odd, dft_ref[0][:, :128], dft_ref[1][:, :128], NT)
    m_cos, m_sin, o_cos, o_sin = main[:, :256], main[:, 256:], odd[:, :256], odd[:, 256:]
    root = math.sqrt(0.5)

    def imag_rows(values):
        rows = values.shape[0]
        near_row = (lax.broadcasted_iota(jnp.int32, values.shape, 0) & 8) == 0
        return jnp.where(near_row, pltpu.roll(values, rows - 4, 0), pltpu.roll(values, 4, 0))

    for k in (0, 256):
        if k == 0:
            re, im = m_cos[0:128] - m_sin[128:256], m_cos[128:256] + m_sin[0:128]
            last_re, last_im = o_cos[0:32] - o_sin[32:64], o_cos[32:64] + o_sin[0:32]
        else:
            m_c, m_s, o_c, o_s = m_cos[256:384], m_sin[256:384], o_cos[64:96], o_sin[64:96]
            re, im = m_c - imag_rows(m_s), imag_rows(m_c) + m_s
            last_re, last_im = o_c - imag_rows(o_s), imag_rows(o_c) + o_s
        w4 = last_re * twist_ref[3:4, :] - last_im * twist_ref[7:8, :]
        w0 = re[96:128]
        ws = []
        for p in range(3):
            cos, sin = twist_ref[p : p + 1, :], twist_ref[4 + p : 5 + p, :]
            r_p, i_p = re[32 * p : 32 * p + 32], im[32 * p : 32 * p + 32]
            ws.append((r_p * cos - i_p * sin, i_p * cos + r_p * sin))
        for r in range(8):
            total = w0 + w4 if r % 2 == 0 else w0 - w4
            for p in range(3):
                turn_by = (r * (p + 1)) % 8
                cos_r = [1.0, root, 0.0, -root, -1.0, -root, 0.0, root][turn_by]
                sin_r = [0.0, root, 1.0, root, 0.0, -root, -1.0, -root][turn_by]
                if cos_r:
                    total = total + cos_r * ws[p][0]
                if sin_r:
                    total = total - sin_r * ws[p][1]
            total = total + total
            lanes = slice(256 * r, 256 * r + 256)
            for ch in range(2):
                if k == 0:
                    out_ref[ch, 2:18, lanes] = total[16 * ch : 16 * ch + 16]
                else:
                    out_ref[ch, 0:2, lanes] = total[16 * ch + 14 : 16 * ch + 16]
                    out_ref[ch, 18:20, lanes] = total[16 * ch : 16 * ch + 2]
                    if r == 0:
                        out_ref[ch, 20:24, :] = jnp.zeros((4, NX), f32)


def ahead_of(values):
    return pltpu.roll(values, NX - 1, 1)


def behind_of(values):
    return pltpu.roll(values, 1, 1)


def fill_taps(build_ref, target, fields, sign):
    for c in range(2):
        whole = fields[c]
        moves = (behind_of(whole), whole, ahead_of(whole))[::sign]
        for a in range(3):
            row = (2 * a + c) * WIDE
            build_ref[row : row + WIDE, :] = moves[a]
    build_ref[144:152, :] = jnp.ones((8, NX), f32)
    build_ref[152:160, :] = jnp.zeros((8, NX), f32)
    target[0:160, :] = build_ref[...].astype(bf16)


def state_kernel(
    first_far, second_far, bias_far, pick_far, before_far, after_far, own_ref,
    w1_out, w2_out, turn_ref, state_low, field_ref,
    build_ref, w1_ref, w2_ref, first_ref, second_ref, bias_ref, pick_ref,
    before_ref, after_ref, sems,
):
    copies = [
        pltpu.make_async_copy(source, target, sems.at[k])
        for k, (source, target) in enumerate(
            (
                (first_far, first_ref), (second_far, second_ref),
                (bias_far, bias_ref), (pick_far, pick_ref),
                (before_far, before_ref), (after_far, after_ref),
            )
        )
    ]
    for copy in copies:
        copy.start()
    for copy in copies:
        copy.wait()
    lane = lax.broadcasted_iota(jnp.int32, (FEATS, 256), 1)
    square = lax.broadcasted_iota(jnp.int32, (FEATS, FEATS), 0)
    own = square == lax.broadcasted_iota(jnp.int32, (FEATS, FEATS), 1)
    bias = jnp.sum(jnp.where(own, bias_ref[...], 0.0), 1, keepdims=True)
    bias_high = bias.astype(bf16).astype(f32)
    bias_part = jnp.where(
        lane == 6 * WIDE, bias_high, jnp.where(lane == 6 * WIDE + 1, bias - bias_high, 0.0)
    )
    base1 = dot(first_ref[...].astype(f32).T.astype(bf16), pick_ref[0])
    base2 = dot(second_ref[...].astype(f32).T.astype(bf16), pick_ref[1])
    for j in range(18):
        rows = slice(32 * j, 32 * j + 32)
        moved1 = pltpu.roll(base1, j, 1) if j else base1
        moved2 = pltpu.roll(base2, j, 1) if j else base2
        w1_ref[rows, :] = moved1 + bias_part
        w2_ref[rows, :] = moved2
    for c in range(2):
        field_ref[c, 20:24, :] = jnp.zeros((4, NX), f32)
        for r in range(8):
            field_ref[c, 2:18, 256 * r : 256 * r + 256] = own_ref[
                r, 32 + 16 * c : 48 + 16 * c, :
            ]
        field_ref[c, 0:2, :] = before_ref[2 * c : 2 * c + 2, :]
        field_ref[c, 18:20, :] = after_ref[2 * c : 2 * c + 2, :]
    fill_taps(build_ref, state_low, (field_ref[0], field_ref[1]), 1)
    w1 = w1_ref[...]
    turn_ref[...] = w1.T[:160].astype(bf16)
    w1_out[...] = w1[:, :160].astype(bf16)
    w2_out[...] = w2_ref[:, :160].astype(bf16)


def closure_kernel(
    w1_ref, w2_ref, turn_ref, state_ref, field_ref, dft_ref, twist_ref, take1_ref, take2_ref,
    in_ref,
    out_ref,
    proj_ref, build_ref, state_low, scaled_low, grads, acts,
):
    back_part(in_ref, dft_ref, twist_ref, proj_ref)
    state_low[0:160, :] = state_ref[...]
    state_low[160:256, :] = jnp.zeros((96, NX), bf16)
    scaled_low[160:256, :] = jnp.zeros((96, NX), bf16)
    fill_taps(build_ref, scaled_low, (STEP * proj_ref[0], STEP * proj_ref[1]), -1)
    active = jnp.tanh(dot(w1_ref[...], state_ref[...]))
    acts[...] = active[32:544].astype(bf16)
    back = dot(w2_ref[...], scaled_low[0:160, :])
    grads[...] = (back * (1.0 - active * active)).astype(bf16)
    build_ref[...] = dot(turn_ref[...], grads[...])
    first_sums = dot(grads[32:544, :], state_low[...], NT)
    second_sums = dot(acts[...], scaled_low[...], NT)
    lane = lax.broadcasted_iota(jnp.int32, (FEATS, 256), 1)
    total1 = total2 = plain = jnp.zeros((FEATS, 256), f32)
    for j in range(16):
        rows = slice(32 * j, 32 * j + 32)
        total1 = total1 + pltpu.roll(first_sums[rows], 255 - j, 1)
        total2 = total2 + pltpu.roll(second_sums[rows], 255 - j, 1)
        plain = plain + first_sums[rows]
    total1 = jnp.where(lane >= 6 * WIDE, plain, total1)
    high1, low1 = split(total1)
    high2, low2 = split(total2)
    packed = (dot(high1, take1_ref[...]) + dot(low1, take1_ref[...])) + (
        dot(high2, take2_ref[...]) + dot(low2, take2_ref[...])
    )
    turned = jnp.concatenate([packed, jnp.zeros((96, 128), f32)], 0).T
    ten = turned[0:10]
    for g in range(1, 4):
        ten = ten + pltpu.roll(turned[10 * g : 10 * g + 10], 32 * g, 1)
    for r in range(8):
        out_ref[r, 32:40, 0:128] = ten[0:8]
        out_ref[r, 32:34, 128:256] = ten[8:10]
        out_ref[r, 34:40, 128:256] = jnp.zeros((6, 128), f32)

    inner, up, down = slice(2, 18), slice(3, 19), slice(1, 17)
    su = field_ref[0, inner, :]
    along_x, along_y = [], []
    for c in range(2):
        mine = field_ref[c, inner, :]
        along_x.append(0.5 * (ahead_of(mine) - behind_of(mine)))
        along_y.append(0.5 * (field_ref[c, up, :] - field_ref[c, down, :]))
    along = (along_x, along_y)
    centre = [STEP * proj_ref[c, inner, :] for c in range(2)]
    for c in range(2):
        mine = centre[c]
        above = STEP * proj_ref[c, up, :]
        below = STEP * proj_ref[c, down, :]
        carried = su * mine
        total = 0.5 * (ahead_of(carried) - behind_of(carried))
        total = total + 0.5 * (field_ref[1, up, :] * above - field_ref[1, down, :] * below)
        total = total - (centre[0] * along[c][0] + centre[1] * along[c][1])
        total = total + (ahead_of(mine) + behind_of(mine) + above + below - 4.0 * mine)
        total = total + proj_ref[c, inner, :]
        for a, move in enumerate((ahead_of, None, behind_of)):
            row = (2 * a + c) * WIDE
            part = build_ref[row + 2 : row + 18, :]
            total = total + (move(part) if move else part)
        for r in range(8):
            out_ref[r, 16 * c : 16 * c + 16, :] = total[:, 256 * r : 256 * r + 256]


def unpack_kernel(in_ref, out_ref, part_ref):
    total = in_ref[0, 32:40, :]
    for r in range(1, 8):
        total = total + in_ref[r, 32:40, :]
    ten = jnp.concatenate([total[:, 0:128], total[0:2, 128:256]], 0)
    for d in range(COLS):
        part_ref[10 * d : 10 * d + 10, :] = ten
    for c in range(2):
        lines = jnp.concatenate([in_ref[r, 16 * c : 16 * c + 16, :] for r in range(8)], 0)
        out_ref[c] = lines.T


def sums_kernel(in_ref, first_ref, second_ref, bias_ref):
    total = in_ref[0:10, :]
    for d in range(1, COLS):
        total = total + in_ref[10 * d : 10 * d + 10, :]
    total = total * (1.0 / math.sqrt(NX * NY))
    moved = [total] + [pltpu.roll(total, 128 - 32 * g, 1) for g in range(1, 4)]
    first_ref[0:10, :] = moved[0][:, 0:32]
    first_ref[10:18, :] = moved[1][0:8, 0:32]
    bias_ref[...] = moved[1][8:9, 0:32]
    second_ref[0:1, :] = moved[1][9:10, 0:32]
    second_ref[1:11, :] = moved[2][:, 0:32]
    second_ref[11:18, :] = moved[3][0:7, 0:32]


def call(kernel, outs, scratch=(), scalars=0, count=0, name=None, remote=0, mib=8):
    space = [pl.BlockSpec(memory_space=pltpu.SMEM)] * scalars
    space += [pl.BlockSpec(memory_space=pltpu.HBM)] * remote
    space += [pl.BlockSpec(memory_space=pltpu.VMEM)] * (count - scalars - remote)
    many = isinstance(outs, (list, tuple))
    out_space = pl.BlockSpec(memory_space=pltpu.VMEM)
    return pl.pallas_call(
        kernel,
        out_shape=outs,
        in_specs=space,
        out_specs=[out_space] * len(outs) if many else out_space,
        scratch_shapes=list(scratch),
        compiler_params=pltpu.CompilerParams(vmem_limit_bytes=mib * 2**20),
        name=name,
    )


def shape(*dims, dtype=f32):
    return jax.ShapeDtypeStruct(dims, dtype)


def shards(state, cotangent, first_kernel, first_bias, second_kernel):
    t = tables()
    first_pick, second_pick, first_take, second_take = picks()
    dft, group, twist_y, twist_x = (
        jnp.asarray(t[k]) for k in ("dft", "group", "twist_y", "twist_x")
    )
    every = ("col", "row")
    place = (lax.axis_index("col") * ROWS + lax.axis_index("row")).astype(jnp.int32).reshape(1)

    def exchange(values, axis):
        return lax.all_to_all(values, axis, 0, 0, tiled=True)

    space = [pltpu.VMEM((4, 256, 128), f32), pltpu.SemaphoreType.DMA((5,))]
    packed, twist_x = call(
        pack_kernel, [shape(8, 64, 256), shape(8, 256)], space, count=3, name="pack", remote=3
    )(far(cotangent), far(state), far(twist_x))
    lines = exchange(packed, "row")
    modes, low, high = call(
        ahead_kernel, [shape(512, 128), shape(4, NX), shape(4, NX)],
        count=3, name="ahead",
    )(dft, twist_x, lines)
    order = [(i % ROWS) * COLS + i // ROWS for i in range(DEV)]
    up = [(order[i], order[(i + 1) % DEV]) for i in range(DEV)]
    before = lax.ppermute(high, ("row", "col"), up)
    after = lax.ppermute(low, ("row", "col"), [(j, i) for i, j in up])
    modes = exchange(modes.reshape(DEV, 1, 256), every).reshape(512, 128)
    prepared = call(
        state_kernel,
        [
            shape(576, 160, dtype=bf16), shape(576, 160, dtype=bf16),
            shape(160, 576, dtype=bf16), shape(160, NX, dtype=bf16), shape(2, WIDE, NX),
        ],
        [
            pltpu.VMEM((160, NX), f32), pltpu.VMEM((576, 256), f32), pltpu.VMEM((576, 256), f32),
            pltpu.VMEM((18, FEATS), bf16), pltpu.VMEM((18, FEATS), bf16),
            pltpu.VMEM((1, FEATS), f32), pltpu.VMEM((2, 18, 256), bf16),
            pltpu.VMEM((4, NX), f32), pltpu.VMEM((4, NX), f32),
            pltpu.SemaphoreType.DMA((6,)),
        ],
        count=7,
        remote=6,
        name="state",
    )(
        far(first_kernel), far(second_kernel.T), far(first_bias.reshape(1, FEATS)),
        far(jnp.asarray(np.stack([first_pick, second_pick]))), far(before), far(after), lines,
    )
    modes, prepared = lax.optimization_barrier((modes, prepared))
    modes = call(middle_kernel, shape(768, 128), scalars=1, count=5, name="middle")(place, dft, twist_y, group, modes)
    modes = exchange(modes.reshape(DEV, 1, 384), every).reshape(768, 128)
    scratch = [
        pltpu.VMEM((2, WIDE, NX), f32),
        pltpu.VMEM((160, NX), f32),
        pltpu.VMEM((256, NX), bf16),
        pltpu.VMEM((256, NX), bf16),
        pltpu.VMEM((576, NX), bf16),
        pltpu.VMEM((512, NX), bf16),
    ]
    result = call(
        closure_kernel, shape(8, 40, 256), scratch, count=10, name="closure", mib=40
    )(*prepared, dft, twist_x, first_take, second_take, modes)
    result = exchange(result, "row")
    grad_state, part = call(
        unpack_kernel, [shape(2, 256, 128), shape(320, 128)], count=1, name="unpack"
    )(result)
    part = exchange(part.reshape(COLS, 1, 1280), "col").reshape(320, 128)
    grad_first, grad_second, grad_bias = call(
        sums_kernel, [shape(18, 32), shape(18, 32), shape(1, 32)], count=1, name="sums"
    )(part)
    return grad_state, grad_first, grad_second.T, grad_bias.reshape(32)


def solution(mesh):
    placed = (P(None, "row", "col"), P(None, "row", "col"), P(), P(), P())
    return jax.shard_map(
        shards,
        mesh=mesh,
        in_specs=placed,
        out_specs=(P(None, "row", "col"), P(), P(), P()),
        check_vma=False,
    )
```

```python
import math

import jax
import jax.numpy as jnp
import numpy as np
from jax import lax
from jax.experimental import pallas as pl
from jax.experimental.pallas import tpu as pltpu
from jax.sharding import PartitionSpec as P

NX, NY = 2048, 4096
ROWS, COLS = 8, 32
DEV = ROWS * COLS
FEATS = 32
WIDE = 24
f32, bf16 = jnp.float32, jnp.bfloat16
STEP = 0.1
NT = (((1,), (1,)), ((), ()))
NN = (((1,), (0,)), ((), ()))


def pair(table):
    high = table.astype(jnp.bfloat16)
    low = (table - high.astype(np.float64)).astype(jnp.bfloat16)
    return np.stack([high, low])


def tables():
    index = np.arange(256)
    angle = 2 * np.pi * (np.outer(index, index) % 256) / 256
    dft = pair(np.concatenate([np.cos(angle), np.sin(angle)]))
    small = 2 * np.pi * (np.outer(np.arange(16), np.arange(16)) % 16) / 16
    eye = np.eye(8)
    group = np.concatenate([np.kron(eye, np.cos(small)), np.kron(eye, np.sin(small))], 1)
    twist_y = 2 * np.pi * np.outer(index, np.arange(128) % 16) / NY
    twist_x = 2 * np.pi * np.outer(np.arange(1, 5), index) / NX
    return dict(
        dft=dft,
        group=pair(group),
        twist_y=np.stack([np.cos(twist_y), np.sin(twist_y)]).astype(np.float32),
        twist_x=np.concatenate([np.cos(twist_x), np.sin(twist_x)]).astype(np.float32),
    )


def picks():
    first = np.zeros((18, 256))
    second = np.zeros((18, 256))
    out_first = np.zeros((256, 128))
    out_second = np.zeros((256, 128))
    for a in range(3):
        for b in range(3):
            for c in range(2):
                row = 2 * (3 * a + b) + c
                lane = (2 * a + c) * WIDE
                first[row, lane + b] = 1
                second[row, lane + 2 - b] = 1
                out_first[lane + b, row] = 1
                out_second[lane + 2 - b, 19 + row] = 1
    out_first[6 * WIDE, 18] = 1
    return [x.astype(jnp.bfloat16) for x in (first, second, out_first, out_second)]


def split(values):
    high = values.astype(bf16)
    return high, (values - high.astype(f32)).astype(bf16)


def dot(left, right, dims=NN):
    return lax.dot_general(left, right, dims, preferred_element_type=f32)


def left_dot(table_ref, values, dims=NN):
    high, low = split(values)
    dim = dims[0][1][0] ^ 1
    size = values.shape[dim]
    wide = dot(table_ref[0], jnp.concatenate([high, low], dim), dims)
    both = wide[:, :size] + (wide[:, size:] + dot(table_ref[1], high, dims))
    return both[:256], both[256:]


def apart_dot(table_ref, values):
    high, low = split(values)
    parts = []
    for k in (0, 256):
        t_high, t_low = table_ref[0, k : k + 256, :], table_ref[1, k : k + 256, :]
        parts.append(dot(t_high, high) + (dot(t_high, low) + dot(t_low, high)))
    return parts


def right_apart(values, table_ref):
    high, low = split(values)
    return dot(high, table_ref[0]) + (dot(low, table_ref[0]) + dot(high, table_ref[1]))


def right_dot(values, high_table, low_table, dims=NN):
    high, low = split(values)
    size = values.shape[0]
    tall = dot(jnp.concatenate([high, low], 0), high_table, dims)
    return tall[:size] + (tall[size:] + dot(high, low_table, dims))


def far(values):
    return pltpu.with_memory_space_constraint(values, pltpu.HBM)


def pack_kernel(cot_ref, state_ref, twist_far, out_ref, twist_ref, buffer_ref, sems):
    copies = []
    twist_copy = pltpu.make_async_copy(twist_far, twist_ref, sems.at[4])
    for f, ref in enumerate((cot_ref, state_ref)):
        for c in range(2):
            k = 2 * f + c
            copies.append(pltpu.make_async_copy(ref.at[c], buffer_ref.at[k], sems.at[k]))
    for copy in copies:
        copy.start()
    twist_copy.start()
    for k, copy in enumerate(copies):
        copy.wait()
        turned = buffer_ref[k].T
        for r in range(ROWS):
            out_ref[r, 16 * k : 16 * k + 16, :] = turned[16 * r : 16 * r + 16]
    twist_copy.wait()


def ahead_kernel(dft_ref, twist_ref, in_ref, out_ref, low_ref, high_ref):
    u = [in_ref[r, 0:32, :] for r in range(8)]
    root = math.sqrt(0.5)
    a, b, c, d = (u[k] - u[k + 4] for k in range(4))
    e0, e1, e2, e3 = (u[k] + u[k + 4] for k in range(4))
    s0, s1 = e0 + e2, e1 + e3
    parts = [
        (a + root * (b - d), -c - root * (b + d)),
        (e0 - e2, e3 - e1),
        (a - root * (b - d), c - root * (b + d)),
    ]
    reals, imags = [], []
    for k, (re, im) in enumerate(parts):
        cos, sin = twist_ref[k : k + 1, :], twist_ref[4 + k : 5 + k, :]
        reals.append(re * cos + im * sin)
        imags.append(im * cos - re * sin)
    even, odd = s0 + s1, s0 - s1
    zero = jnp.zeros_like(even)
    last_re = odd * twist_ref[3:4, :]
    last_im = -odd * twist_ref[7:8, :]
    stack = jnp.concatenate(
        reals + [even] + imags + [zero] + [zero] * 3 + [last_re] + [zero] * 3 + [last_im], 0
    )
    cosine, sine = left_dot(dft_ref, stack, NT)
    main_re = cosine[:, 0:128] + sine[:, 128:256]
    main_im = cosine[:, 128:256] - sine[:, 0:128]
    odd_re = cosine[:128, 256:384] + sine[:128, 384:512]
    odd_im = cosine[:128, 384:512] - sine[:128, 256:384]
    lane = lax.broadcasted_iota(jnp.int32, (128, 128), 1)
    row = lax.broadcasted_iota(jnp.int32, (128, 128), 0)
    last = lane >= 96
    edge = last & (row == 0)
    top_re = jnp.where(edge, main_re[128:129], main_re[:128])
    top_im = jnp.where(edge, main_re[0:1], main_im[:128])
    out_ref[pl.ds(0, 128, 2), :] = top_re
    out_ref[pl.ds(1, 128, 2), :] = top_im
    out_ref[pl.ds(256, 128, 2), :] = jnp.where(last, odd_re, main_re[128:])
    out_ref[pl.ds(257, 128, 2), :] = jnp.where(last, odd_im, main_im[128:])
    for r in range(8):
        for ch in range(2):
            row0 = 32 + 16 * ch
            low_ref[2 * ch : 2 * ch + 2, 256 * r : 256 * r + 256] = in_ref[r, row0 : row0 + 2, :]
            high_ref[2 * ch : 2 * ch + 2, 256 * r : 256 * r + 256] = in_ref[
                r, row0 + 14 : row0 + 16, :
            ]


def waves(place):
    lane = lax.broadcasted_iota(jnp.int32, (256, 128), 1)
    row = lax.broadcasted_iota(jnp.int32, (256, 128), 0)
    slot = lane // 32
    plain = 8 * place + slot + 1
    last = jnp.where(place == 0, NX // 2, jnp.where(place < 128, 8 * place, 8 * place - 1020))
    mx = jnp.where(slot == 3, last, plain)
    mx = jnp.where(mx >= NX // 2, mx - NX, mx)
    my = row + 256 * (lane % 16)
    my = jnp.where(my >= NY // 2, my - NY, my)
    kx = mx.astype(f32) * (1.0 / NX)
    ky = my.astype(f32) * (1.0 / NY)
    inverse = 1.0 / (kx * kx + ky * ky)
    cross = jnp.where((mx == -(NX // 2)) | (my == -(NY // 2)), 0.0, kx * ky)
    own = jnp.where((lane & 16) == 0, kx * kx, ky * ky)
    return 1.0 - own * inverse, -cross * inverse, lane


def swap16(values, lane):
    return jnp.where((lane & 16) == 0, pltpu.roll(values, 112, 1), pltpu.roll(values, 16, 1))


def middle_kernel(
    place_ref, dft_ref, twist_ref, group_ref, in_ref, out_ref
):
    place = place_ref[0]
    re, im = in_ref[pl.ds(0, 256, 2), :], in_ref[pl.ds(1, 256, 2), :]
    both = jnp.concatenate([re, im], 1)
    cosine, sine = apart_dot(dft_ref, both)
    f_re, f_im = cosine[:, :128] + sine[:, 128:], cosine[:, 128:] - sine[:, :128]
    cos, sin = twist_ref[0], twist_ref[1]
    t_re, t_im = f_re * cos + f_im * sin, f_im * cos - f_re * sin
    g = right_apart(jnp.concatenate([t_re, t_im], 0), group_ref)
    g_re, g_im = g[:256, :128] + g[256:, 128:], g[256:, :128] - g[:256, 128:]
    keep, mix, lane = waves(place)
    p_re = keep * g_re + mix * swap16(g_re, lane)
    p_im = keep * g_im + mix * swap16(g_im, lane)
    h = right_apart(jnp.concatenate([p_re, p_im], 0), group_ref)
    h_re, h_im = h[:256, :128] - h[256:, 128:], h[256:, :128] + h[:256, 128:]
    t_re, t_im = h_re * cos - h_im * sin, h_im * cos + h_re * sin
    both = jnp.concatenate([t_re, t_im], 1)
    cosine, sine = apart_dot(dft_ref, both)
    scale = 1.0 / (NX * NY)
    o_re = (cosine[:, :128] - sine[:, 128:]) * scale
    o_im = (cosine[:, 128:] + sine[:, :128]) * scale
    sums = jnp.sum(im, 0, keepdims=True)
    sums = jnp.where(lane[:1] >= 112, sums, 0.0)
    mean = jnp.sum(sums, 1, keepdims=True) * scale
    zeroth = (lane >= 96) & (place == 0)
    o_im = jnp.where(zeroth, jnp.where(lane >= 112, mean, im * (1.0 / NX)), o_im)
    near = (lane & 8) == 0
    outer = ((lane + 2) & 15) < 4

    def beside(values):
        return jnp.where(near, pltpu.roll(values, 255, 0), pltpu.roll(values, 1, 0))

    out_ref[pl.ds(0, 256, 3), :] = o_re
    out_ref[pl.ds(1, 256, 3), :] = o_im
    edge_im = beside(o_im)
    edge_im = jnp.where(near, pltpu.roll(edge_im, 4, 1), pltpu.roll(edge_im, 124, 1))
    out_ref[pl.ds(2, 256, 3), :] = jnp.where(outer, beside(o_re), edge_im)


def back_part(in_ref, dft_ref, twist_ref, out_ref):
    lane = lax.broadcasted_iota(jnp.int32, (128, 128), 1)
    row = lax.broadcasted_iota(jnp.int32, (128, 128), 0)
    last = lane >= 96
    edge = last & (row == 0)
    near = (lane & 8) == 0
    outer = ((lane + 2) & 15) < 4
    top_re, top_im, top_h = (in_ref[pl.ds(k, 128, 3), :] for k in range(3))
    low_re, low_im, low_h = (in_ref[pl.ds(384 + k, 128, 3), :] for k in range(3))
    head = top_h[0:1]
    head_im = jnp.where(near[0:1], pltpu.roll(head, 124, 1), pltpu.roll(head, 4, 1))
    half_im = jnp.where(outer[0:1], 0.5 * head_im, 0.0)
    half_re = jnp.where(outer[0:1], 0.5 * head, 0.0)
    nyquist = jnp.where(edge, 0.5 * top_re[0:1], 0.0)
    mains = [
        jnp.concatenate(
            [jnp.where(edge, 0.5 * top_im, top_re), jnp.where(last, nyquist, low_re)], 0
        ),
        jnp.concatenate([jnp.where(edge, 0.0, top_im), jnp.where(last, 0.0, low_im)], 0),
        jnp.concatenate(
            [
                jnp.where(edge, half_im, top_h),
                jnp.where(last, jnp.where(edge, half_re, 0.0), low_h),
            ],
            0,
        ),
    ]
    main = right_dot(jnp.concatenate(mains, 1).T, dft_ref[0], dft_ref[1], NT)
    odd = jnp.concatenate([low_re, low_im, low_h], 1).T
    odd = jnp.concatenate([odd[128 * k + 96 : 128 * k + 128] for k in range(3)], 0)
    odd = right_dot(odd, dft_ref[0][:, :128], dft_ref[1][:, :128], NT)
    m_cos, m_sin, o_cos, o_sin = main[:, :256], main[:, 256:], odd[:, :256], odd[:, 256:]
    root = math.sqrt(0.5)

    def imag_rows(values):
        rows = values.shape[0]
        near_row = (lax.broadcasted_iota(jnp.int32, values.shape, 0) & 8) == 0
        return jnp.where(near_row, pltpu.roll(values, rows - 4, 0), pltpu.roll(values, 4, 0))

    for k in (0, 256):
        if k == 0:
            re, im = m_cos[0:128] - m_sin[128:256], m_cos[128:256] + m_sin[0:128]
            last_re, last_im = o_cos[0:32] - o_sin[32:64], o_cos[32:64] + o_sin[0:32]
        else:
            m_c, m_s, o_c, o_s = m_cos[256:384], m_sin[256:384], o_cos[64:96], o_sin[64:96]
            re, im = m_c - imag_rows(m_s), imag_rows(m_c) + m_s
            last_re, last_im = o_c - imag_rows(o_s), imag_rows(o_c) + o_s
        w4 = last_re * twist_ref[3:4, :] - last_im * twist_ref[7:8, :]
        w0 = re[96:128]
        ws = []
        for p in range(3):
            cos, sin = twist_ref[p : p + 1, :], twist_ref[4 + p : 5 + p, :]
            r_p, i_p = re[32 * p : 32 * p + 32], im[32 * p : 32 * p + 32]
            ws.append((r_p * cos - i_p * sin, i_p * cos + r_p * sin))
        for r in range(8):
            total = w0 + w4 if r % 2 == 0 else w0 - w4
            for p in range(3):
                turn_by = (r * (p + 1)) % 8
                cos_r = [1.0, root, 0.0, -root, -1.0, -root, 0.0, root][turn_by]
                sin_r = [0.0, root, 1.0, root, 0.0, -root, -1.0, -root][turn_by]
                if cos_r:
                    total = total + cos_r * ws[p][0]
                if sin_r:
                    total = total - sin_r * ws[p][1]
            total = total + total
            lanes = slice(256 * r, 256 * r + 256)
            for ch in range(2):
                if k == 0:
                    out_ref[ch, 2:18, lanes] = total[16 * ch : 16 * ch + 16]
                else:
                    out_ref[ch, 0:2, lanes] = total[16 * ch + 14 : 16 * ch + 16]
                    out_ref[ch, 18:20, lanes] = total[16 * ch : 16 * ch + 2]
                    if r == 0:
                        out_ref[ch, 20:24, :] = jnp.zeros((4, NX), f32)


def ahead_of(values):
    return pltpu.roll(values, NX - 1, 1)


def behind_of(values):
    return pltpu.roll(values, 1, 1)


def fill_taps(build_ref, target, fields, sign):
    for c in range(2):
        whole = fields[c]
        moves = (behind_of(whole), whole, ahead_of(whole))[::sign]
        for a in range(3):
            row = (2 * a + c) * WIDE
            build_ref[row : row + WIDE, :] = moves[a]
    build_ref[144:152, :] = jnp.ones((8, NX), f32)
    build_ref[152:160, :] = jnp.zeros((8, NX), f32)
    target[0:160, :] = build_ref[...].astype(bf16)


def bands_kernel(
    first_far, second_far, bias_far, pick_far,
    w1_out, w2_out, turn_ref,
    w1_ref, w2_ref, first_ref, second_ref, bias_ref, pick_ref, sems,
):
    copies = [
        pltpu.make_async_copy(source, target, sems.at[k])
        for k, (source, target) in enumerate(
            (
                (first_far, first_ref), (second_far, second_ref),
                (bias_far, bias_ref), (pick_far, pick_ref),
            )
        )
    ]
    for copy in copies:
        copy.start()
    for copy in copies:
        copy.wait()
    lane = lax.broadcasted_iota(jnp.int32, (FEATS, 256), 1)
    square = lax.broadcasted_iota(jnp.int32, (FEATS, FEATS), 0)
    own = square == lax.broadcasted_iota(jnp.int32, (FEATS, FEATS), 1)
    bias = jnp.sum(jnp.where(own, bias_ref[...], 0.0), 1, keepdims=True)
    bias_high = bias.astype(bf16).astype(f32)
    bias_part = jnp.where(
        lane == 6 * WIDE, bias_high, jnp.where(lane == 6 * WIDE + 1, bias - bias_high, 0.0)
    )
    base1 = dot(first_ref[...].astype(f32).T.astype(bf16), pick_ref[0])
    base2 = dot(second_ref[...].astype(f32).T.astype(bf16), pick_ref[1])
    for j in range(18):
        rows = slice(32 * j, 32 * j + 32)
        moved1 = pltpu.roll(base1, j, 1) if j else base1
        moved2 = pltpu.roll(base2, j, 1) if j else base2
        w1_ref[rows, :] = moved1 + bias_part
        w2_ref[rows, :] = moved2
    w1 = w1_ref[...]
    turn_ref[...] = w1.T[:160].astype(bf16)
    w1_out[...] = w1[:, :160].astype(bf16)
    w2_out[...] = w2_ref[:, :160].astype(bf16)


def closure_kernel(
    w1_ref, w2_ref, turn_ref, own_ref, before_ref, after_ref,
    dft_ref, twist_ref, take1_ref, take2_ref, in_ref,
    out_ref,
    field_ref, proj_ref, build_ref, state_low, scaled_low, grads, acts,
):
    for c in range(2):
        field_ref[c, 20:24, :] = jnp.zeros((4, NX), f32)
        for r in range(8):
            field_ref[c, 2:18, 256 * r : 256 * r + 256] = own_ref[
                r, 32 + 16 * c : 48 + 16 * c, :
            ]
        field_ref[c, 0:2, :] = before_ref[2 * c : 2 * c + 2, :]
        field_ref[c, 18:20, :] = after_ref[2 * c : 2 * c + 2, :]
    fill_taps(build_ref, state_low, (field_ref[0], field_ref[1]), 1)
    back_part(in_ref, dft_ref, twist_ref, proj_ref)
    state_low[160:256, :] = jnp.zeros((96, NX), bf16)
    scaled_low[160:256, :] = jnp.zeros((96, NX), bf16)
    fill_taps(build_ref, scaled_low, (STEP * proj_ref[0], STEP * proj_ref[1]), -1)
    active = jnp.tanh(dot(w1_ref[...], state_low[0:160, :]))
    acts[...] = active[32:544].astype(bf16)
    back = dot(w2_ref[...], scaled_low[0:160, :])
    grads[...] = (back * (1.0 - active * active)).astype(bf16)
    build_ref[...] = dot(turn_ref[...], grads[...])
    first_sums = dot(grads[32:544, :], state_low[...], NT)
    second_sums = dot(acts[...], scaled_low[...], NT)
    lane = lax.broadcasted_iota(jnp.int32, (FEATS, 256), 1)
    total1 = total2 = plain = jnp.zeros((FEATS, 256), f32)
    for j in range(16):
        rows = slice(32 * j, 32 * j + 32)
        total1 = total1 + pltpu.roll(first_sums[rows], 255 - j, 1)
        total2 = total2 + pltpu.roll(second_sums[rows], 255 - j, 1)
        plain = plain + first_sums[rows]
    total1 = jnp.where(lane >= 6 * WIDE, plain, total1)
    high1, low1 = split(total1)
    high2, low2 = split(total2)
    packed = (dot(high1, take1_ref[...]) + dot(low1, take1_ref[...])) + (
        dot(high2, take2_ref[...]) + dot(low2, take2_ref[...])
    )
    turned = jnp.concatenate([packed, jnp.zeros((96, 128), f32)], 0).T
    ten = turned[0:10]
    for g in range(1, 4):
        ten = ten + pltpu.roll(turned[10 * g : 10 * g + 10], 32 * g, 1)
    for r in range(8):
        out_ref[r, 32:40, 0:128] = ten[0:8]
        out_ref[r, 32:34, 128:256] = ten[8:10]
        out_ref[r, 34:40, 128:256] = jnp.zeros((6, 128), f32)

    inner, up, down = slice(2, 18), slice(3, 19), slice(1, 17)
    su = field_ref[0, inner, :]
    along_x, along_y = [], []
    for c in range(2):
        mine = field_ref[c, inner, :]
        along_x.append(0.5 * (ahead_of(mine) - behind_of(mine)))
        along_y.append(0.5 * (field_ref[c, up, :] - field_ref[c, down, :]))
    along = (along_x, along_y)
    centre = [STEP * proj_ref[c, inner, :] for c in range(2)]
    for c in range(2):
        mine = centre[c]
        above = STEP * proj_ref[c, up, :]
        below = STEP * proj_ref[c, down, :]
        carried = su * mine
        total = 0.5 * (ahead_of(carried) - behind_of(carried))
        total = total + 0.5 * (field_ref[1, up, :] * above - field_ref[1, down, :] * below)
        total = total - (centre[0] * along[c][0] + centre[1] * along[c][1])
        total = total + (ahead_of(mine) + behind_of(mine) + above + below - 4.0 * mine)
        total = total + proj_ref[c, inner, :]
        for a, move in enumerate((ahead_of, None, behind_of)):
            row = (2 * a + c) * WIDE
            part = build_ref[row + 2 : row + 18, :]
            total = total + (move(part) if move else part)
        for r in range(8):
            out_ref[r, 16 * c : 16 * c + 16, :] = total[:, 256 * r : 256 * r + 256]


def unpack_kernel(in_ref, out_ref, part_ref):
    total = in_ref[0, 32:40, :]
    for r in range(1, 8):
        total = total + in_ref[r, 32:40, :]
    ten = jnp.concatenate([total[:, 0:128], total[0:2, 128:256]], 0)
    for d in range(COLS):
        part_ref[10 * d : 10 * d + 10, :] = ten
    for c in range(2):
        lines = jnp.concatenate([in_ref[r, 16 * c : 16 * c + 16, :] for r in range(8)], 0)
        out_ref[c] = lines.T


def sums_kernel(in_ref, first_ref, second_ref, bias_ref):
    total = in_ref[0:10, :]
    for d in range(1, COLS):
        total = total + in_ref[10 * d : 10 * d + 10, :]
    total = total * (1.0 / math.sqrt(NX * NY))
    moved = [total] + [pltpu.roll(total, 128 - 32 * g, 1) for g in range(1, 4)]
    first_ref[0:10, :] = moved[0][:, 0:32]
    first_ref[10:18, :] = moved[1][0:8, 0:32]
    bias_ref[...] = moved[1][8:9, 0:32]
    second_ref[0:1, :] = moved[1][9:10, 0:32]
    second_ref[1:11, :] = moved[2][:, 0:32]
    second_ref[11:18, :] = moved[3][0:7, 0:32]


def call(kernel, outs, scratch=(), scalars=0, count=0, name=None, remote=0, mib=8):
    space = [pl.BlockSpec(memory_space=pltpu.SMEM)] * scalars
    space += [pl.BlockSpec(memory_space=pltpu.HBM)] * remote
    space += [pl.BlockSpec(memory_space=pltpu.VMEM)] * (count - scalars - remote)
    many = isinstance(outs, (list, tuple))
    out_space = pl.BlockSpec(memory_space=pltpu.VMEM)
    return pl.pallas_call(
        kernel,
        out_shape=outs,
        in_specs=space,
        out_specs=[out_space] * len(outs) if many else out_space,
        scratch_shapes=list(scratch),
        compiler_params=pltpu.CompilerParams(vmem_limit_bytes=mib * 2**20),
        name=name,
    )


def shape(*dims, dtype=f32):
    return jax.ShapeDtypeStruct(dims, dtype)


def shards(state, cotangent, first_kernel, first_bias, second_kernel):
    t = tables()
    first_pick, second_pick, first_take, second_take = picks()
    dft, group, twist_y, twist_x = (
        jnp.asarray(t[k]) for k in ("dft", "group", "twist_y", "twist_x")
    )
    every = ("col", "row")
    place = (lax.axis_index("col") * ROWS + lax.axis_index("row")).astype(jnp.int32).reshape(1)

    def exchange(values, axis):
        return lax.all_to_all(values, axis, 0, 0, tiled=True)

    space = [pltpu.VMEM((4, 256, 128), f32), pltpu.SemaphoreType.DMA((5,))]
    packed, twist_x = call(
        pack_kernel, [shape(8, 64, 256), shape(8, 256)], space, count=3, name="pack", remote=3
    )(far(cotangent), far(state), far(twist_x))
    lines = exchange(packed, "row")
    modes, low, high = call(
        ahead_kernel, [shape(512, 128), shape(4, NX), shape(4, NX)],
        count=3, name="ahead",
    )(dft, twist_x, lines)
    order = [(i % ROWS) * COLS + i // ROWS for i in range(DEV)]
    up = [(order[i], order[(i + 1) % DEV]) for i in range(DEV)]
    before = lax.ppermute(high, ("row", "col"), up)
    after = lax.ppermute(low, ("row", "col"), [(j, i) for i, j in up])
    modes = exchange(modes.reshape(DEV, 1, 256), every).reshape(512, 128)
    prepared = call(
        bands_kernel,
        [
            shape(576, 160, dtype=bf16), shape(576, 160, dtype=bf16), shape(160, 576, dtype=bf16),
        ],
        [
            pltpu.VMEM((576, 256), f32), pltpu.VMEM((576, 256), f32),
            pltpu.VMEM((18, FEATS), bf16), pltpu.VMEM((18, FEATS), bf16),
            pltpu.VMEM((1, FEATS), f32), pltpu.VMEM((2, 18, 256), bf16),
            pltpu.SemaphoreType.DMA((4,)),
        ],
        count=4,
        remote=4,
        name="bands",
    )(
        far(first_kernel), far(second_kernel.T), far(first_bias.reshape(1, FEATS)),
        far(jnp.asarray(np.stack([first_pick, second_pick]))),
    )
    modes, prepared, before, after = lax.optimization_barrier((modes, prepared, before, after))
    modes = call(middle_kernel, shape(768, 128), scalars=1, count=5, name="middle")(place, dft, twist_y, group, modes)
    modes = exchange(modes.reshape(DEV, 1, 384), every).reshape(768, 128)
    scratch = [
        pltpu.VMEM((2, WIDE, NX), f32),
        pltpu.VMEM((2, WIDE, NX), f32),
        pltpu.VMEM((160, NX), f32),
        pltpu.VMEM((256, NX), bf16),
        pltpu.VMEM((256, NX), bf16),
        pltpu.VMEM((576, NX), bf16),
        pltpu.VMEM((512, NX), bf16),
    ]
    result = call(
        closure_kernel, shape(8, 40, 256), scratch, count=11, name="closure", mib=40
    )(*prepared, lines, before, after, dft, twist_x, first_take, second_take, modes)
    result = exchange(result, "row")
    grad_state, part = call(
        unpack_kernel, [shape(2, 256, 128), shape(320, 128)], count=1, name="unpack"
    )(result)
    part = exchange(part.reshape(COLS, 1, 1280), "col").reshape(320, 128)
    grad_first, grad_second, grad_bias = call(
        sums_kernel, [shape(18, 32), shape(18, 32), shape(1, 32)], count=1, name="sums"
    )(part)
    return grad_state, grad_first, grad_second.T, grad_bias.reshape(32)


def solution(mesh):
    placed = (P(None, "row", "col"), P(None, "row", "col"), P(), P(), P())
    return jax.shard_map(
        shards,
        mesh=mesh,
        in_specs=placed,
        out_specs=(P(None, "row", "col"), P(), P(), P()),
        check_vma=False,
    )
```

```python
import math

import jax
import jax.numpy as jnp
import numpy as np
from jax import lax
from jax.experimental import pallas as pl
from jax.experimental.pallas import tpu as pltpu
from jax.sharding import PartitionSpec as P

NX, NY = 2048, 4096
ROWS, COLS = 8, 32
DEV = ROWS * COLS
FEATS = 32
WIDE = 24
f32, bf16 = jnp.float32, jnp.bfloat16
STEP = 0.1
NT = (((1,), (1,)), ((), ()))
NN = (((1,), (0,)), ((), ()))


def pair(table):
    high = table.astype(jnp.bfloat16)
    low = (table - high.astype(np.float64)).astype(jnp.bfloat16)
    return np.stack([high, low])


def tables():
    index = np.arange(256)
    angle = 2 * np.pi * (np.outer(index, index) % 256) / 256
    dft = pair(np.concatenate([np.cos(angle), np.sin(angle)]))
    small = 2 * np.pi * (np.outer(np.arange(16), np.arange(16)) % 16) / 16
    eye = np.eye(8)
    group = np.concatenate([np.kron(eye, np.cos(small)), np.kron(eye, np.sin(small))], 1)
    twist_y = 2 * np.pi * np.outer(index, np.arange(128) % 16) / NY
    twist_x = 2 * np.pi * np.outer(np.arange(1, 5), index) / NX
    return dict(
        dft=dft,
        group=pair(group),
        twist_y=np.stack([np.cos(twist_y), np.sin(twist_y)]).astype(np.float32),
        twist_x=np.concatenate([np.cos(twist_x), np.sin(twist_x)]).astype(np.float32),
    )


def picks():
    first = np.zeros((18, 256))
    second = np.zeros((18, 256))
    out_first = np.zeros((256, 128))
    out_second = np.zeros((256, 128))
    for a in range(3):
        for b in range(3):
            for c in range(2):
                row = 2 * (3 * a + b) + c
                lane = (2 * a + c) * WIDE
                first[row, lane + b] = 1
                second[row, lane + 2 - b] = 1
                out_first[lane + b, row] = 1
                out_second[lane + 2 - b, 19 + row] = 1
    out_first[6 * WIDE, 18] = 1
    return [x.astype(jnp.bfloat16) for x in (first, second, out_first, out_second)]


def split(values):
    high = values.astype(bf16)
    return high, (values - high.astype(f32)).astype(bf16)


def dot(left, right, dims=NN):
    return lax.dot_general(left, right, dims, preferred_element_type=f32)


def left_dot(table_ref, values, dims=NN):
    high, low = split(values)
    dim = dims[0][1][0] ^ 1
    size = values.shape[dim]
    wide = dot(table_ref[0], jnp.concatenate([high, low], dim), dims)
    both = wide[:, :size] + (wide[:, size:] + dot(table_ref[1], high, dims))
    return both[:256], both[256:]


def apart_dot(table_ref, values):
    high, low = split(values)
    parts = []
    for k in (0, 256):
        t_high, t_low = table_ref[0, k : k + 256, :], table_ref[1, k : k + 256, :]
        parts.append(dot(t_high, high) + (dot(t_high, low) + dot(t_low, high)))
    return parts


def right_apart(values, table_ref):
    high, low = split(values)
    return dot(high, table_ref[0]) + (dot(low, table_ref[0]) + dot(high, table_ref[1]))


def right_dot(values, high_table, low_table, dims=NN):
    high, low = split(values)
    size = values.shape[0]
    tall = dot(jnp.concatenate([high, low], 0), high_table, dims)
    return tall[:size] + (tall[size:] + dot(high, low_table, dims))


def far(values):
    return pltpu.with_memory_space_constraint(values, pltpu.HBM)


def pack_kernel(cot_ref, state_ref, twist_far, out_ref, twist_ref, buffer_ref, sems):
    copies = []
    twist_copy = pltpu.make_async_copy(twist_far, twist_ref, sems.at[4])
    for f, ref in enumerate((cot_ref, state_ref)):
        for c in range(2):
            k = 2 * f + c
            copies.append(pltpu.make_async_copy(ref.at[c], buffer_ref.at[k], sems.at[k]))
    for copy in copies:
        copy.start()
    twist_copy.start()
    for k, copy in enumerate(copies):
        copy.wait()
        turned = buffer_ref[k].T
        for r in range(ROWS):
            out_ref[r, 16 * k : 16 * k + 16, :] = turned[16 * r : 16 * r + 16]
    twist_copy.wait()


def ahead_kernel(dft_ref, twist_ref, in_ref, out_ref, low_ref, high_ref):
    u = [in_ref[r, 0:32, :] for r in range(8)]
    root = math.sqrt(0.5)
    a, b, c, d = (u[k] - u[k + 4] for k in range(4))
    e0, e1, e2, e3 = (u[k] + u[k + 4] for k in range(4))
    s0, s1 = e0 + e2, e1 + e3
    parts = [
        (a + root * (b - d), -c - root * (b + d)),
        (e0 - e2, e3 - e1),
        (a - root * (b - d), c - root * (b + d)),
    ]
    reals, imags = [], []
    for k, (re, im) in enumerate(parts):
        cos, sin = twist_ref[k : k + 1, :], twist_ref[4 + k : 5 + k, :]
        reals.append(re * cos + im * sin)
        imags.append(im * cos - re * sin)
    even, odd = s0 + s1, s0 - s1
    zero = jnp.zeros_like(even)
    last_re = odd * twist_ref[3:4, :]
    last_im = -odd * twist_ref[7:8, :]
    stack = jnp.concatenate(
        reals + [even] + imags + [zero] + [zero] * 3 + [last_re] + [zero] * 3 + [last_im], 0
    )
    cosine, sine = left_dot(dft_ref, stack, NT)
    main_re = cosine[:, 0:128] + sine[:, 128:256]
    main_im = cosine[:, 128:256] - sine[:, 0:128]
    odd_re = cosine[:128, 256:384] + sine[:128, 384:512]
    odd_im = cosine[:128, 384:512] - sine[:128, 256:384]
    lane = lax.broadcasted_iota(jnp.int32, (128, 128), 1)
    row = lax.broadcasted_iota(jnp.int32, (128, 128), 0)
    last = lane >= 96
    edge = last & (row == 0)
    top_re = jnp.where(edge, main_re[128:129], main_re[:128])
    top_im = jnp.where(edge, main_re[0:1], main_im[:128])
    out_ref[pl.ds(0, 128, 2), :] = top_re
    out_ref[pl.ds(1, 128, 2), :] = top_im
    out_ref[pl.ds(256, 128, 2), :] = jnp.where(last, odd_re, main_re[128:])
    out_ref[pl.ds(257, 128, 2), :] = jnp.where(last, odd_im, main_im[128:])
    for r in range(8):
        for ch in range(2):
            row0 = 32 + 16 * ch
            low_ref[2 * ch : 2 * ch + 2, 256 * r : 256 * r + 256] = in_ref[r, row0 : row0 + 2, :]
            high_ref[2 * ch : 2 * ch + 2, 256 * r : 256 * r + 256] = in_ref[
                r, row0 + 14 : row0 + 16, :
            ]


def waves(place):
    lane = lax.broadcasted_iota(jnp.int32, (256, 128), 1)
    row = lax.broadcasted_iota(jnp.int32, (256, 128), 0)
    slot = lane // 32
    plain = 8 * place + slot + 1
    last = jnp.where(place == 0, NX // 2, jnp.where(place < 128, 8 * place, 8 * place - 1020))
    mx = jnp.where(slot == 3, last, plain)
    mx = jnp.where(mx >= NX // 2, mx - NX, mx)
    my = row + 256 * (lane % 16)
    my = jnp.where(my >= NY // 2, my - NY, my)
    kx = mx.astype(f32) * (1.0 / NX)
    ky = my.astype(f32) * (1.0 / NY)
    inverse = 1.0 / (kx * kx + ky * ky)
    cross = jnp.where((mx == -(NX // 2)) | (my == -(NY // 2)), 0.0, kx * ky)
    own = jnp.where((lane & 16) == 0, kx * kx, ky * ky)
    return 1.0 - own * inverse, -cross * inverse, lane


def swap16(values, lane):
    return jnp.where((lane & 16) == 0, pltpu.roll(values, 112, 1), pltpu.roll(values, 16, 1))


def middle_kernel(
    place_ref, dft_ref, twist_ref, group_ref, in_ref, out_ref
):
    place = place_ref[0]
    re, im = in_ref[pl.ds(0, 256, 2), :], in_ref[pl.ds(1, 256, 2), :]
    both = jnp.concatenate([re, im], 1)
    cosine, sine = apart_dot(dft_ref, both)
    f_re, f_im = cosine[:, :128] + sine[:, 128:], cosine[:, 128:] - sine[:, :128]
    cos, sin = twist_ref[0], twist_ref[1]
    t_re, t_im = f_re * cos + f_im * sin, f_im * cos - f_re * sin
    g = right_apart(jnp.concatenate([t_re, t_im], 0), group_ref)
    g_re, g_im = g[:256, :128] + g[256:, 128:], g[256:, :128] - g[:256, 128:]
    keep, mix, lane = waves(place)
    p_re = keep * g_re + mix * swap16(g_re, lane)
    p_im = keep * g_im + mix * swap16(g_im, lane)
    h = right_apart(jnp.concatenate([p_re, p_im], 0), group_ref)
    h_re, h_im = h[:256, :128] - h[256:, 128:], h[256:, :128] + h[:256, 128:]
    t_re, t_im = h_re * cos - h_im * sin, h_im * cos + h_re * sin
    both = jnp.concatenate([t_re, t_im], 1)
    cosine, sine = apart_dot(dft_ref, both)
    scale = 1.0 / (NX * NY)
    o_re = (cosine[:, :128] - sine[:, 128:]) * scale
    o_im = (cosine[:, 128:] + sine[:, :128]) * scale
    sums = jnp.sum(im, 0, keepdims=True)
    sums = jnp.where(lane[:1] >= 112, sums, 0.0)
    mean = jnp.sum(sums, 1, keepdims=True) * scale
    zeroth = (lane >= 96) & (place == 0)
    o_im = jnp.where(zeroth, jnp.where(lane >= 112, mean, im * (1.0 / NX)), o_im)
    near = (lane & 8) == 0
    outer = ((lane + 2) & 15) < 4

    def beside(values):
        return jnp.where(near, pltpu.roll(values, 255, 0), pltpu.roll(values, 1, 0))

    out_ref[pl.ds(0, 256, 3), :] = o_re
    out_ref[pl.ds(1, 256, 3), :] = o_im
    edge_im = beside(o_im)
    edge_im = jnp.where(near, pltpu.roll(edge_im, 4, 1), pltpu.roll(edge_im, 124, 1))
    out_ref[pl.ds(2, 256, 3), :] = jnp.where(outer, beside(o_re), edge_im)


def back_part(in_ref, dft_ref, twist_ref, out_ref):
    lane = lax.broadcasted_iota(jnp.int32, (128, 128), 1)
    row = lax.broadcasted_iota(jnp.int32, (128, 128), 0)
    last = lane >= 96
    edge = last & (row == 0)
    near = (lane & 8) == 0
    outer = ((lane + 2) & 15) < 4
    top_re, top_im, top_h = (in_ref[pl.ds(k, 128, 3), :] for k in range(3))
    low_re, low_im, low_h = (in_ref[pl.ds(384 + k, 128, 3), :] for k in range(3))
    head = top_h[0:1]
    head_im = jnp.where(near[0:1], pltpu.roll(head, 124, 1), pltpu.roll(head, 4, 1))
    half_im = jnp.where(outer[0:1], 0.5 * head_im, 0.0)
    half_re = jnp.where(outer[0:1], 0.5 * head, 0.0)
    nyquist = jnp.where(edge, 0.5 * top_re[0:1], 0.0)
    mains = [
        jnp.concatenate(
            [jnp.where(edge, 0.5 * top_im, top_re), jnp.where(last, nyquist, low_re)], 0
        ),
        jnp.concatenate([jnp.where(edge, 0.0, top_im), jnp.where(last, 0.0, low_im)], 0),
        jnp.concatenate(
            [
                jnp.where(edge, half_im, top_h),
                jnp.where(last, jnp.where(edge, half_re, 0.0), low_h),
            ],
            0,
        ),
    ]
    main = right_dot(jnp.concatenate(mains, 1).T, dft_ref[0], dft_ref[1], NT)
    odd = jnp.concatenate([low_re, low_im, low_h], 1).T
    odd = jnp.concatenate([odd[128 * k + 96 : 128 * k + 128] for k in range(3)], 0)
    odd = right_dot(odd, dft_ref[0][:, :128], dft_ref[1][:, :128], NT)
    m_cos, m_sin, o_cos, o_sin = main[:, :256], main[:, 256:], odd[:, :256], odd[:, 256:]
    root = math.sqrt(0.5)

    def imag_rows(values):
        rows = values.shape[0]
        near_row = (lax.broadcasted_iota(jnp.int32, values.shape, 0) & 8) == 0
        return jnp.where(near_row, pltpu.roll(values, rows - 4, 0), pltpu.roll(values, 4, 0))

    for k in (0, 256):
        if k == 0:
            re, im = m_cos[0:128] - m_sin[128:256], m_cos[128:256] + m_sin[0:128]
            last_re, last_im = o_cos[0:32] - o_sin[32:64], o_cos[32:64] + o_sin[0:32]
        else:
            m_c, m_s, o_c, o_s = m_cos[256:384], m_sin[256:384], o_cos[64:96], o_sin[64:96]
            re, im = m_c - imag_rows(m_s), imag_rows(m_c) + m_s
            last_re, last_im = o_c - imag_rows(o_s), imag_rows(o_c) + o_s
        w4 = last_re * twist_ref[3:4, :] - last_im * twist_ref[7:8, :]
        w0 = re[96:128]
        ws = []
        for p in range(3):
            cos, sin = twist_ref[p : p + 1, :], twist_ref[4 + p : 5 + p, :]
            r_p, i_p = re[32 * p : 32 * p + 32], im[32 * p : 32 * p + 32]
            ws.append((r_p * cos - i_p * sin, i_p * cos + r_p * sin))
        for r in range(8):
            total = w0 + w4 if r % 2 == 0 else w0 - w4
            for p in range(3):
                turn_by = (r * (p + 1)) % 8
                cos_r = [1.0, root, 0.0, -root, -1.0, -root, 0.0, root][turn_by]
                sin_r = [0.0, root, 1.0, root, 0.0, -root, -1.0, -root][turn_by]
                if cos_r:
                    total = total + cos_r * ws[p][0]
                if sin_r:
                    total = total - sin_r * ws[p][1]
            total = total + total
            lanes = slice(256 * r, 256 * r + 256)
            for ch in range(2):
                if k == 0:
                    out_ref[ch, 2:18, lanes] = total[16 * ch : 16 * ch + 16]
                else:
                    out_ref[ch, 0:2, lanes] = total[16 * ch + 14 : 16 * ch + 16]
                    out_ref[ch, 18:20, lanes] = total[16 * ch : 16 * ch + 2]
                    if r == 0:
                        out_ref[ch, 20:24, :] = jnp.zeros((4, NX), f32)


def ahead_of(values):
    return pltpu.roll(values, NX - 1, 1)


def behind_of(values):
    return pltpu.roll(values, 1, 1)


def fill_taps(build_ref, target, fields, sign):
    for c in range(2):
        whole = fields[c]
        moves = (behind_of(whole), whole, ahead_of(whole))[::sign]
        for a in range(3):
            row = (2 * a + c) * WIDE
            build_ref[row : row + WIDE, :] = moves[a]
    build_ref[144:152, :] = jnp.ones((8, NX), f32)
    build_ref[152:160, :] = jnp.zeros((8, NX), f32)
    target[0:160, :] = build_ref[...].astype(bf16)


def bands_kernel(
    first_far, second_far, bias_far, pick_far,
    w1_out, w2_out, turn_ref,
    w1_ref, w2_ref, first_ref, second_ref, bias_ref, pick_ref, sems,
):
    copies = [
        pltpu.make_async_copy(source, target, sems.at[k])
        for k, (source, target) in enumerate(
            (
                (first_far, first_ref), (second_far, second_ref),
                (bias_far, bias_ref), (pick_far, pick_ref),
            )
        )
    ]
    for copy in copies:
        copy.start()
    for copy in copies:
        copy.wait()
    lane = lax.broadcasted_iota(jnp.int32, (FEATS, 256), 1)
    square = lax.broadcasted_iota(jnp.int32, (FEATS, FEATS), 0)
    own = square == lax.broadcasted_iota(jnp.int32, (FEATS, FEATS), 1)
    bias = jnp.sum(jnp.where(own, bias_ref[...], 0.0), 1, keepdims=True)
    bias_high = bias.astype(bf16).astype(f32)
    bias_part = jnp.where(
        lane == 6 * WIDE, bias_high, jnp.where(lane == 6 * WIDE + 1, bias - bias_high, 0.0)
    )
    base1 = dot(first_ref[...].astype(f32).T.astype(bf16), pick_ref[0])
    base2 = dot(second_ref[...].astype(f32).T.astype(bf16), pick_ref[1])
    for j in range(18):
        rows = slice(32 * j, 32 * j + 32)
        moved1 = pltpu.roll(base1, j, 1) if j else base1
        moved2 = pltpu.roll(base2, j, 1) if j else base2
        w1_ref[rows, :] = moved1 + bias_part
        w2_ref[rows, :] = moved2
    w1 = w1_ref[...]
    turn_ref[...] = w1.T[:160].astype(bf16)
    w1_out[...] = w1[:, :160].astype(bf16)
    w2_out[...] = w2_ref[:, :160].astype(bf16)


def closure_kernel(
    w1_ref, w2_ref, turn_ref, own_ref, before_ref, after_ref,
    dft_ref, twist_ref, take1_ref, take2_ref, in_ref,
    out_ref,
    field_ref, proj_ref, build_ref, state_low, scaled_low, grads, acts,
):
    for c in range(2):
        field_ref[c, 20:24, :] = jnp.zeros((4, NX), f32)
        for r in range(8):
            field_ref[c, 2:18, 256 * r : 256 * r + 256] = own_ref[
                r, 32 + 16 * c : 48 + 16 * c, :
            ]
        field_ref[c, 0:2, :] = before_ref[2 * c : 2 * c + 2, :]
        field_ref[c, 18:20, :] = after_ref[2 * c : 2 * c + 2, :]
    fill_taps(build_ref, state_low, (field_ref[0], field_ref[1]), 1)
    back_part(in_ref, dft_ref, twist_ref, proj_ref)
    state_low[160:256, :] = jnp.zeros((96, NX), bf16)
    scaled_low[160:256, :] = jnp.zeros((96, NX), bf16)
    fill_taps(build_ref, scaled_low, (STEP * proj_ref[0], STEP * proj_ref[1]), -1)
    active = jnp.tanh(dot(w1_ref[...], state_low[0:160, :]))
    acts[...] = active[32:544].astype(bf16)
    back = dot(w2_ref[...], scaled_low[0:160, :])
    grads[...] = (back * (1.0 - active * active)).astype(bf16)
    build_ref[...] = dot(turn_ref[...], grads[...])
    first_sums = dot(grads[32:544, :], state_low[...], NT)
    second_sums = dot(acts[...], scaled_low[...], NT)
    lane = lax.broadcasted_iota(jnp.int32, (FEATS, 256), 1)
    total1 = total2 = plain = jnp.zeros((FEATS, 256), f32)
    for j in range(16):
        rows = slice(32 * j, 32 * j + 32)
        total1 = total1 + pltpu.roll(first_sums[rows], 255 - j, 1)
        total2 = total2 + pltpu.roll(second_sums[rows], 255 - j, 1)
        plain = plain + first_sums[rows]
    total1 = jnp.where(lane >= 6 * WIDE, plain, total1)
    high1, low1 = split(total1)
    high2, low2 = split(total2)
    packed = (dot(high1, take1_ref[...]) + dot(low1, take1_ref[...])) + (
        dot(high2, take2_ref[...]) + dot(low2, take2_ref[...])
    )
    turned = jnp.concatenate([packed, jnp.zeros((96, 128), f32)], 0).T
    ten = turned[0:10]
    for g in range(1, 4):
        ten = ten + pltpu.roll(turned[10 * g : 10 * g + 10], 32 * g, 1)
    for r in range(8):
        out_ref[r, 32:40, 0:128] = ten[0:8]
        out_ref[r, 32:34, 128:256] = ten[8:10]
        out_ref[r, 34:40, 128:256] = jnp.zeros((6, 128), f32)

    inner, up, down = slice(2, 18), slice(3, 19), slice(1, 17)
    su = field_ref[0, inner, :]
    along_x, along_y = [], []
    for c in range(2):
        mine = field_ref[c, inner, :]
        along_x.append(0.5 * (ahead_of(mine) - behind_of(mine)))
        along_y.append(0.5 * (field_ref[c, up, :] - field_ref[c, down, :]))
    along = (along_x, along_y)
    centre = [STEP * proj_ref[c, inner, :] for c in range(2)]
    for c in range(2):
        mine = centre[c]
        above = STEP * proj_ref[c, up, :]
        below = STEP * proj_ref[c, down, :]
        carried = su * mine
        total = 0.5 * (ahead_of(carried) - behind_of(carried))
        total = total + 0.5 * (field_ref[1, up, :] * above - field_ref[1, down, :] * below)
        total = total - (centre[0] * along[c][0] + centre[1] * along[c][1])
        total = total + (ahead_of(mine) + behind_of(mine) + above + below - 4.0 * mine)
        total = total + proj_ref[c, inner, :]
        for a, move in enumerate((ahead_of, None, behind_of)):
            row = (2 * a + c) * WIDE
            part = build_ref[row + 2 : row + 18, :]
            total = total + (move(part) if move else part)
        for r in range(8):
            out_ref[r, 16 * c : 16 * c + 16, :] = total[:, 256 * r : 256 * r + 256]


def part_kernel(in_ref, part_ref):
    total = in_ref[0, 32:40, :]
    for r in range(1, 8):
        total = total + in_ref[r, 32:40, :]
    ten = jnp.concatenate([total[:, 0:128], total[0:2, 128:256]], 0)
    for d in range(COLS):
        part_ref[10 * d : 10 * d + 10, :] = ten


def unpack_kernel(in_ref, out_ref):
    for c in range(2):
        lines = jnp.concatenate([in_ref[r, 16 * c : 16 * c + 16, :] for r in range(8)], 0)
        out_ref[c] = lines.T


def sums_kernel(in_ref, first_ref, second_ref, bias_ref):
    total = in_ref[0:10, :]
    for d in range(1, COLS):
        total = total + in_ref[10 * d : 10 * d + 10, :]
    total = total * (1.0 / math.sqrt(NX * NY))
    moved = [total] + [pltpu.roll(total, 128 - 32 * g, 1) for g in range(1, 4)]
    first_ref[0:10, :] = moved[0][:, 0:32]
    first_ref[10:18, :] = moved[1][0:8, 0:32]
    bias_ref[...] = moved[1][8:9, 0:32]
    second_ref[0:1, :] = moved[1][9:10, 0:32]
    second_ref[1:11, :] = moved[2][:, 0:32]
    second_ref[11:18, :] = moved[3][0:7, 0:32]


def call(kernel, outs, scratch=(), scalars=0, count=0, name=None, remote=0, mib=8):
    space = [pl.BlockSpec(memory_space=pltpu.SMEM)] * scalars
    space += [pl.BlockSpec(memory_space=pltpu.HBM)] * remote
    space += [pl.BlockSpec(memory_space=pltpu.VMEM)] * (count - scalars - remote)
    many = isinstance(outs, (list, tuple))
    out_space = pl.BlockSpec(memory_space=pltpu.VMEM)
    return pl.pallas_call(
        kernel,
        out_shape=outs,
        in_specs=space,
        out_specs=[out_space] * len(outs) if many else out_space,
        scratch_shapes=list(scratch),
        compiler_params=pltpu.CompilerParams(vmem_limit_bytes=mib * 2**20),
        name=name,
    )


def shape(*dims, dtype=f32):
    return jax.ShapeDtypeStruct(dims, dtype)


def shards(state, cotangent, first_kernel, first_bias, second_kernel):
    t = tables()
    first_pick, second_pick, first_take, second_take = picks()
    dft, group, twist_y, twist_x = (
        jnp.asarray(t[k]) for k in ("dft", "group", "twist_y", "twist_x")
    )
    every = ("col", "row")
    place = (lax.axis_index("col") * ROWS + lax.axis_index("row")).astype(jnp.int32).reshape(1)

    def exchange(values, axis):
        return lax.all_to_all(values, axis, 0, 0, tiled=True)

    space = [pltpu.VMEM((4, 256, 128), f32), pltpu.SemaphoreType.DMA((5,))]
    packed, twist_x = call(
        pack_kernel, [shape(8, 64, 256), shape(8, 256)], space, count=3, name="pack", remote=3
    )(far(cotangent), far(state), far(twist_x))
    lines = exchange(packed, "row")
    modes, low, high = call(
        ahead_kernel, [shape(512, 128), shape(4, NX), shape(4, NX)],
        count=3, name="ahead",
    )(dft, twist_x, lines)
    order = [(i % ROWS) * COLS + i // ROWS for i in range(DEV)]
    up = [(order[i], order[(i + 1) % DEV]) for i in range(DEV)]
    before = lax.ppermute(high, ("row", "col"), up)
    after = lax.ppermute(low, ("row", "col"), [(j, i) for i, j in up])
    modes = exchange(modes.reshape(DEV, 1, 256), every).reshape(512, 128)
    prepared = call(
        bands_kernel,
        [
            shape(576, 160, dtype=bf16), shape(576, 160, dtype=bf16), shape(160, 576, dtype=bf16),
        ],
        [
            pltpu.VMEM((576, 256), f32), pltpu.VMEM((576, 256), f32),
            pltpu.VMEM((18, FEATS), bf16), pltpu.VMEM((18, FEATS), bf16),
            pltpu.VMEM((1, FEATS), f32), pltpu.VMEM((2, 18, 256), bf16),
            pltpu.SemaphoreType.DMA((4,)),
        ],
        count=4,
        remote=4,
        name="bands",
    )(
        far(first_kernel), far(second_kernel.T), far(first_bias.reshape(1, FEATS)),
        far(jnp.asarray(np.stack([first_pick, second_pick]))),
    )
    modes, prepared, before, after = lax.optimization_barrier((modes, prepared, before, after))
    modes = call(middle_kernel, shape(768, 128), scalars=1, count=5, name="middle")(place, dft, twist_y, group, modes)
    modes = exchange(modes.reshape(DEV, 1, 384), every).reshape(768, 128)
    scratch = [
        pltpu.VMEM((2, WIDE, NX), f32),
        pltpu.VMEM((2, WIDE, NX), f32),
        pltpu.VMEM((160, NX), f32),
        pltpu.VMEM((256, NX), bf16),
        pltpu.VMEM((256, NX), bf16),
        pltpu.VMEM((576, NX), bf16),
        pltpu.VMEM((512, NX), bf16),
    ]
    result = call(
        closure_kernel, shape(8, 40, 256), scratch, count=11, name="closure", mib=40
    )(*prepared, lines, before, after, dft, twist_x, first_take, second_take, modes)
    result = exchange(result, "row")
    part = call(part_kernel, shape(320, 128), count=1, name="part")(result)
    part = exchange(part.reshape(COLS, 1, 1280), "col").reshape(320, 128)
    grad_first, grad_second, grad_bias = call(
        sums_kernel, [shape(18, 32), shape(18, 32), shape(1, 32)], count=1, name="sums"
    )(part)
    grad_state = call(unpack_kernel, shape(2, 256, 128), count=1, name="unpack")(result)
    return grad_state, grad_first, grad_second.T, grad_bias.reshape(32)


def solution(mesh):
    placed = (P(None, "row", "col"), P(None, "row", "col"), P(), P(), P())
    return jax.shard_map(
        shards,
        mesh=mesh,
        in_specs=placed,
        out_specs=(P(None, "row", "col"), P(), P(), P()),
        check_vma=False,
    )
```

```python
import math

import jax
import jax.numpy as jnp
import numpy as np
from jax import lax
from jax.experimental import pallas as pl
from jax.experimental.pallas import tpu as pltpu
from jax.sharding import PartitionSpec as P

NX, NY = 2048, 4096
ROWS, COLS = 8, 32
DEV = ROWS * COLS
FEATS = 32
WIDE = 24
f32, bf16 = jnp.float32, jnp.bfloat16
STEP = 0.1
NT = (((1,), (1,)), ((), ()))
NN = (((1,), (0,)), ((), ()))


def pair(table):
    high = table.astype(jnp.bfloat16)
    low = (table - high.astype(np.float64)).astype(jnp.bfloat16)
    return np.stack([high, low])


def tables():
    index = np.arange(256)
    angle = 2 * np.pi * (np.outer(index, index) % 256) / 256
    dft = pair(np.concatenate([np.cos(angle), np.sin(angle)]))
    small = 2 * np.pi * (np.outer(np.arange(16), np.arange(16)) % 16) / 16
    eye = np.eye(8)
    group = np.concatenate([np.kron(eye, np.cos(small)), np.kron(eye, np.sin(small))], 1)
    twist_y = 2 * np.pi * np.outer(index, np.arange(128) % 16) / NY
    twist_x = 2 * np.pi * np.outer(np.arange(1, 5), index) / NX
    return dict(
        dft=dft,
        group=pair(group),
        twist_y=np.stack([np.cos(twist_y), np.sin(twist_y)]).astype(np.float32),
        twist_x=np.concatenate([np.cos(twist_x), np.sin(twist_x)]).astype(np.float32),
    )


def picks():
    first = np.zeros((18, 256))
    second = np.zeros((18, 256))
    out_first = np.zeros((256, 128))
    out_second = np.zeros((256, 128))
    for a in range(3):
        for b in range(3):
            for c in range(2):
                row = 2 * (3 * a + b) + c
                lane = (2 * a + c) * WIDE
                first[row, lane + b] = 1
                second[row, lane + 2 - b] = 1
                out_first[lane + b, row] = 1
                out_second[lane + 2 - b, 19 + row] = 1
    out_first[6 * WIDE, 18] = 1
    return [x.astype(jnp.bfloat16) for x in (first, second, out_first, out_second)]


def split(values):
    high = values.astype(bf16)
    return high, (values - high.astype(f32)).astype(bf16)


def dot(left, right, dims=NN):
    return lax.dot_general(left, right, dims, preferred_element_type=f32)


def left_dot(table_ref, values, dims=NN):
    high, low = split(values)
    dim = dims[0][1][0] ^ 1
    size = values.shape[dim]
    wide = dot(table_ref[0], jnp.concatenate([high, low], dim), dims)
    both = wide[:, :size] + (wide[:, size:] + dot(table_ref[1], high, dims))
    return both[:256], both[256:]


def apart_dot(table_ref, values):
    high, low = split(values)
    parts = []
    for k in (0, 256):
        t_high, t_low = table_ref[0, k : k + 256, :], table_ref[1, k : k + 256, :]
        parts.append(dot(t_high, high) + (dot(t_high, low) + dot(t_low, high)))
    return parts


def right_apart(values, table_ref):
    high, low = split(values)
    return dot(high, table_ref[0]) + (dot(low, table_ref[0]) + dot(high, table_ref[1]))


def right_dot(values, high_table, low_table, dims=NN):
    high, low = split(values)
    size = values.shape[0]
    tall = dot(jnp.concatenate([high, low], 0), high_table, dims)
    return tall[:size] + (tall[size:] + dot(high, low_table, dims))


def far(values):
    return pltpu.with_memory_space_constraint(values, pltpu.HBM)


def pack_kernel(cot_ref, state_ref, twist_far, out_ref, twist_ref, buffer_ref, sems):
    copies = []
    twist_copy = pltpu.make_async_copy(twist_far, twist_ref, sems.at[4])
    for f, ref in enumerate((cot_ref, state_ref)):
        for c in range(2):
            k = 2 * f + c
            copies.append(pltpu.make_async_copy(ref.at[c], buffer_ref.at[k], sems.at[k]))
    for copy in copies:
        copy.start()
    twist_copy.start()
    for k, copy in enumerate(copies):
        copy.wait()
        turned = buffer_ref[k].T
        for r in range(ROWS):
            out_ref[r, 16 * k : 16 * k + 16, :] = turned[16 * r : 16 * r + 16]
    twist_copy.wait()


def ahead_kernel(dft_ref, twist_ref, in_ref, out_ref, low_ref, high_ref):
    u = [in_ref[r, 0:32, :] for r in range(8)]
    root = math.sqrt(0.5)
    a, b, c, d = (u[k] - u[k + 4] for k in range(4))
    e0, e1, e2, e3 = (u[k] + u[k + 4] for k in range(4))
    s0, s1 = e0 + e2, e1 + e3
    parts = [
        (a + root * (b - d), -c - root * (b + d)),
        (e0 - e2, e3 - e1),
        (a - root * (b - d), c - root * (b + d)),
    ]
    reals, imags = [], []
    for k, (re, im) in enumerate(parts):
        cos, sin = twist_ref[k : k + 1, :], twist_ref[4 + k : 5 + k, :]
        reals.append(re * cos + im * sin)
        imags.append(im * cos - re * sin)
    even, odd = s0 + s1, s0 - s1
    zero = jnp.zeros_like(even)
    last_re = odd * twist_ref[3:4, :]
    last_im = -odd * twist_ref[7:8, :]
    stack = jnp.concatenate(
        reals + [even] + imags + [zero] + [zero] * 3 + [last_re] + [zero] * 3 + [last_im], 0
    )
    cosine, sine = left_dot(dft_ref, stack, NT)
    main_re = cosine[:, 0:128] + sine[:, 128:256]
    main_im = cosine[:, 128:256] - sine[:, 0:128]
    odd_re = cosine[:128, 256:384] + sine[:128, 384:512]
    odd_im = cosine[:128, 384:512] - sine[:128, 256:384]
    lane = lax.broadcasted_iota(jnp.int32, (128, 128), 1)
    row = lax.broadcasted_iota(jnp.int32, (128, 128), 0)
    last = lane >= 96
    edge = last & (row == 0)
    top_re = jnp.where(edge, main_re[128:129], main_re[:128])
    top_im = jnp.where(edge, main_re[0:1], main_im[:128])
    out_ref[pl.ds(0, 128, 2), :] = top_re
    out_ref[pl.ds(1, 128, 2), :] = top_im
    out_ref[pl.ds(256, 128, 2), :] = jnp.where(last, odd_re, main_re[128:])
    out_ref[pl.ds(257, 128, 2), :] = jnp.where(last, odd_im, main_im[128:])
    for r in range(8):
        for ch in range(2):
            row0 = 32 + 16 * ch
            low_ref[2 * ch : 2 * ch + 2, 256 * r : 256 * r + 256] = in_ref[r, row0 : row0 + 2, :]
            high_ref[2 * ch : 2 * ch + 2, 256 * r : 256 * r + 256] = in_ref[
                r, row0 + 14 : row0 + 16, :
            ]


def waves(place):
    lane = lax.broadcasted_iota(jnp.int32, (256, 128), 1)
    row = lax.broadcasted_iota(jnp.int32, (256, 128), 0)
    slot = lane // 32
    plain = 8 * place + slot + 1
    last = jnp.where(place == 0, NX // 2, jnp.where(place < 128, 8 * place, 8 * place - 1020))
    mx = jnp.where(slot == 3, last, plain)
    mx = jnp.where(mx >= NX // 2, mx - NX, mx)
    my = row + 256 * (lane % 16)
    my = jnp.where(my >= NY // 2, my - NY, my)
    kx = mx.astype(f32) * (1.0 / NX)
    ky = my.astype(f32) * (1.0 / NY)
    inverse = 1.0 / (kx * kx + ky * ky)
    cross = jnp.where((mx == -(NX // 2)) | (my == -(NY // 2)), 0.0, kx * ky)
    own = jnp.where((lane & 16) == 0, kx * kx, ky * ky)
    return 1.0 - own * inverse, -cross * inverse, lane


def swap16(values, lane):
    return jnp.where((lane & 16) == 0, pltpu.roll(values, 112, 1), pltpu.roll(values, 16, 1))


def middle_kernel(
    place_ref, dft_ref, twist_ref, group_ref, in_ref, out_ref
):
    place = place_ref[0]
    re, im = in_ref[pl.ds(0, 256, 2), :], in_ref[pl.ds(1, 256, 2), :]
    both = jnp.concatenate([re, im], 1)
    cosine, sine = apart_dot(dft_ref, both)
    f_re, f_im = cosine[:, :128] + sine[:, 128:], cosine[:, 128:] - sine[:, :128]
    cos, sin = twist_ref[0], twist_ref[1]
    t_re, t_im = f_re * cos + f_im * sin, f_im * cos - f_re * sin
    g = right_apart(jnp.concatenate([t_re, t_im], 0), group_ref)
    g_re, g_im = g[:256, :128] + g[256:, 128:], g[256:, :128] - g[:256, 128:]
    keep, mix, lane = waves(place)
    p_re = keep * g_re + mix * swap16(g_re, lane)
    p_im = keep * g_im + mix * swap16(g_im, lane)
    h = right_apart(jnp.concatenate([p_re, p_im], 0), group_ref)
    h_re, h_im = h[:256, :128] - h[256:, 128:], h[256:, :128] + h[:256, 128:]
    t_re, t_im = h_re * cos - h_im * sin, h_im * cos + h_re * sin
    both = jnp.concatenate([t_re, t_im], 1)
    cosine, sine = apart_dot(dft_ref, both)
    scale = 1.0 / (NX * NY)
    o_re = (cosine[:, :128] - sine[:, 128:]) * scale
    o_im = (cosine[:, 128:] + sine[:, :128]) * scale
    sums = jnp.sum(im, 0, keepdims=True)
    sums = jnp.where(lane[:1] >= 112, sums, 0.0)
    mean = jnp.sum(sums, 1, keepdims=True) * scale
    zeroth = (lane >= 96) & (place == 0)
    o_im = jnp.where(zeroth, jnp.where(lane >= 112, mean, im * (1.0 / NX)), o_im)
    near = (lane & 8) == 0
    outer = ((lane + 2) & 15) < 4

    def beside(values):
        return jnp.where(near, pltpu.roll(values, 255, 0), pltpu.roll(values, 1, 0))

    out_ref[pl.ds(0, 256, 3), :] = o_re
    out_ref[pl.ds(1, 256, 3), :] = o_im
    edge_im = beside(o_im)
    edge_im = jnp.where(near, pltpu.roll(edge_im, 4, 1), pltpu.roll(edge_im, 124, 1))
    out_ref[pl.ds(2, 256, 3), :] = jnp.where(outer, beside(o_re), edge_im)


def back_part(in_ref, dft_ref, twist_ref, out_ref):
    lane = lax.broadcasted_iota(jnp.int32, (128, 128), 1)
    row = lax.broadcasted_iota(jnp.int32, (128, 128), 0)
    last = lane >= 96
    edge = last & (row == 0)
    near = (lane & 8) == 0
    outer = ((lane + 2) & 15) < 4
    top_re, top_im, top_h = (in_ref[pl.ds(k, 128, 3), :] for k in range(3))
    low_re, low_im, low_h = (in_ref[pl.ds(384 + k, 128, 3), :] for k in range(3))
    head = top_h[0:1]
    head_im = jnp.where(near[0:1], pltpu.roll(head, 124, 1), pltpu.roll(head, 4, 1))
    half_im = jnp.where(outer[0:1], 0.5 * head_im, 0.0)
    half_re = jnp.where(outer[0:1], 0.5 * head, 0.0)
    nyquist = jnp.where(edge, 0.5 * top_re[0:1], 0.0)
    mains = [
        jnp.concatenate(
            [jnp.where(edge, 0.5 * top_im, top_re), jnp.where(last, nyquist, low_re)], 0
        ),
        jnp.concatenate([jnp.where(edge, 0.0, top_im), jnp.where(last, 0.0, low_im)], 0),
        jnp.concatenate(
            [
                jnp.where(edge, half_im, top_h),
                jnp.where(last, jnp.where(edge, half_re, 0.0), low_h),
            ],
            0,
        ),
    ]
    main = right_dot(jnp.concatenate(mains, 1).T, dft_ref[0], dft_ref[1], NT)
    odd = jnp.concatenate([low_re, low_im, low_h], 1).T
    odd = jnp.concatenate([odd[128 * k + 96 : 128 * k + 128] for k in range(3)], 0)
    odd = right_dot(odd, dft_ref[0][:, :128], dft_ref[1][:, :128], NT)
    m_cos, m_sin, o_cos, o_sin = main[:, :256], main[:, 256:], odd[:, :256], odd[:, 256:]
    root = math.sqrt(0.5)

    def imag_rows(values):
        rows = values.shape[0]
        near_row = (lax.broadcasted_iota(jnp.int32, values.shape, 0) & 8) == 0
        return jnp.where(near_row, pltpu.roll(values, rows - 4, 0), pltpu.roll(values, 4, 0))

    for k in (0, 256):
        if k == 0:
            re, im = m_cos[0:128] - m_sin[128:256], m_cos[128:256] + m_sin[0:128]
            last_re, last_im = o_cos[0:32] - o_sin[32:64], o_cos[32:64] + o_sin[0:32]
        else:
            m_c, m_s, o_c, o_s = m_cos[256:384], m_sin[256:384], o_cos[64:96], o_sin[64:96]
            re, im = m_c - imag_rows(m_s), imag_rows(m_c) + m_s
            last_re, last_im = o_c - imag_rows(o_s), imag_rows(o_c) + o_s
        w4 = last_re * twist_ref[3:4, :] - last_im * twist_ref[7:8, :]
        w0 = re[96:128]
        ws = []
        for p in range(3):
            cos, sin = twist_ref[p : p + 1, :], twist_ref[4 + p : 5 + p, :]
            r_p, i_p = re[32 * p : 32 * p + 32], im[32 * p : 32 * p + 32]
            ws.append((r_p * cos - i_p * sin, i_p * cos + r_p * sin))
        for r in range(8):
            total = w0 + w4 if r % 2 == 0 else w0 - w4
            for p in range(3):
                turn_by = (r * (p + 1)) % 8
                cos_r = [1.0, root, 0.0, -root, -1.0, -root, 0.0, root][turn_by]
                sin_r = [0.0, root, 1.0, root, 0.0, -root, -1.0, -root][turn_by]
                if cos_r:
                    total = total + cos_r * ws[p][0]
                if sin_r:
                    total = total - sin_r * ws[p][1]
            total = total + total
            lanes = slice(256 * r, 256 * r + 256)
            for ch in range(2):
                if k == 0:
                    out_ref[ch, 2:18, lanes] = total[16 * ch : 16 * ch + 16]
                else:
                    out_ref[ch, 0:2, lanes] = total[16 * ch + 14 : 16 * ch + 16]
                    out_ref[ch, 18:20, lanes] = total[16 * ch : 16 * ch + 2]
                    if r == 0:
                        out_ref[ch, 20:24, :] = jnp.zeros((4, NX), f32)


def ahead_of(values):
    return pltpu.roll(values, NX - 1, 1)


def behind_of(values):
    return pltpu.roll(values, 1, 1)


def fill_taps(build_ref, target, fields, sign):
    for c in range(2):
        whole = fields[c]
        moves = (behind_of(whole), whole, ahead_of(whole))[::sign]
        for a in range(3):
            row = (2 * a + c) * WIDE
            build_ref[row : row + WIDE, :] = moves[a]
    build_ref[144:152, :] = jnp.ones((8, NX), f32)
    build_ref[152:160, :] = jnp.zeros((8, NX), f32)
    target[0:160, :] = build_ref[...].astype(bf16)


def bands_kernel(
    first_far, second_far, bias_far, pick_far,
    w1_out, w2_out, turn_ref,
    w1_ref, w2_ref, first_ref, second_ref, bias_ref, pick_ref, sems,
):
    copies = [
        pltpu.make_async_copy(source, target, sems.at[k])
        for k, (source, target) in enumerate(
            (
                (first_far, first_ref), (second_far, second_ref),
                (bias_far, bias_ref), (pick_far, pick_ref),
            )
        )
    ]
    for copy in copies:
        copy.start()
    for copy in copies:
        copy.wait()
    lane = lax.broadcasted_iota(jnp.int32, (FEATS, 256), 1)
    square = lax.broadcasted_iota(jnp.int32, (FEATS, FEATS), 0)
    own = square == lax.broadcasted_iota(jnp.int32, (FEATS, FEATS), 1)
    bias = jnp.sum(jnp.where(own, bias_ref[...], 0.0), 1, keepdims=True)
    bias_high = bias.astype(bf16).astype(f32)
    bias_part = jnp.where(
        lane == 6 * WIDE, bias_high, jnp.where(lane == 6 * WIDE + 1, bias - bias_high, 0.0)
    )
    base1 = dot(first_ref[...].astype(f32).T.astype(bf16), pick_ref[0])
    base2 = dot(second_ref[...].astype(f32).T.astype(bf16), pick_ref[1])
    for j in range(18):
        rows = slice(32 * j, 32 * j + 32)
        moved1 = pltpu.roll(base1, j, 1) if j else base1
        moved2 = pltpu.roll(base2, j, 1) if j else base2
        w1_ref[rows, :] = moved1 + bias_part
        w2_ref[rows, :] = moved2
    w1 = w1_ref[...]
    turn_ref[...] = w1.T[:160].astype(bf16)
    w1_out[...] = w1[:, :160].astype(bf16)
    w2_out[...] = w2_ref[:, :160].astype(bf16)


def closure_kernel(
    w1_ref, w2_ref, turn_ref, own_ref, before_ref, after_ref,
    dft_ref, twist_ref, take1_ref, take2_ref, in_ref,
    out_ref,
    field_ref, proj_ref, build_ref, state_low, scaled_low, grads, acts,
):
    for c in range(2):
        field_ref[c, 20:24, :] = jnp.zeros((4, NX), f32)
        for r in range(8):
            field_ref[c, 2:18, 256 * r : 256 * r + 256] = own_ref[
                r, 32 + 16 * c : 48 + 16 * c, :
            ]
        field_ref[c, 0:2, :] = before_ref[2 * c : 2 * c + 2, :]
        field_ref[c, 18:20, :] = after_ref[2 * c : 2 * c + 2, :]
    fill_taps(build_ref, state_low, (field_ref[0], field_ref[1]), 1)
    back_part(in_ref, dft_ref, twist_ref, proj_ref)
    state_low[160:256, :] = jnp.zeros((96, NX), bf16)
    scaled_low[160:256, :] = jnp.zeros((96, NX), bf16)
    fill_taps(build_ref, scaled_low, (STEP * proj_ref[0], STEP * proj_ref[1]), -1)
    active = jnp.tanh(dot(w1_ref[...], state_low[0:160, :]))
    acts[...] = active[32:544].astype(bf16)
    back = dot(w2_ref[...], scaled_low[0:160, :])
    grads[...] = (back * (1.0 - active * active)).astype(bf16)
    build_ref[...] = dot(turn_ref[...], grads[...])
    first_sums = dot(grads[32:544, :], state_low[...], NT)
    second_sums = dot(acts[...], scaled_low[...], NT)
    lane = lax.broadcasted_iota(jnp.int32, (FEATS, 256), 1)
    total1 = total2 = plain = jnp.zeros((FEATS, 256), f32)
    for j in range(16):
        rows = slice(32 * j, 32 * j + 32)
        total1 = total1 + pltpu.roll(first_sums[rows], 255 - j, 1)
        total2 = total2 + pltpu.roll(second_sums[rows], 255 - j, 1)
        plain = plain + first_sums[rows]
    total1 = jnp.where(lane >= 6 * WIDE, plain, total1)
    high1, low1 = split(total1)
    high2, low2 = split(total2)
    packed = (dot(high1, take1_ref[...]) + dot(low1, take1_ref[...])) + (
        dot(high2, take2_ref[...]) + dot(low2, take2_ref[...])
    )
    turned = jnp.concatenate([packed, jnp.zeros((96, 128), f32)], 0).T
    ten = turned[0:10]
    for g in range(1, 4):
        ten = ten + pltpu.roll(turned[10 * g : 10 * g + 10], 32 * g, 1)
    for r in range(8):
        out_ref[r, 32:40, 0:128] = ten[0:8]
        out_ref[r, 32:34, 128:256] = ten[8:10]
        out_ref[r, 34:40, 128:256] = jnp.zeros((6, 128), f32)

    inner, up, down = slice(2, 18), slice(3, 19), slice(1, 17)
    su = field_ref[0, inner, :]
    along_x, along_y = [], []
    for c in range(2):
        mine = field_ref[c, inner, :]
        along_x.append(0.5 * (ahead_of(mine) - behind_of(mine)))
        along_y.append(0.5 * (field_ref[c, up, :] - field_ref[c, down, :]))
    along = (along_x, along_y)
    centre = [STEP * proj_ref[c, inner, :] for c in range(2)]
    for c in range(2):
        mine = centre[c]
        above = STEP * proj_ref[c, up, :]
        below = STEP * proj_ref[c, down, :]
        carried = su * mine
        total = 0.5 * (ahead_of(carried) - behind_of(carried))
        total = total + 0.5 * (field_ref[1, up, :] * above - field_ref[1, down, :] * below)
        total = total - (centre[0] * along[c][0] + centre[1] * along[c][1])
        total = total + (ahead_of(mine) + behind_of(mine) + above + below - 4.0 * mine)
        total = total + proj_ref[c, inner, :]
        for a, move in enumerate((ahead_of, None, behind_of)):
            row = (2 * a + c) * WIDE
            part = build_ref[row + 2 : row + 18, :]
            total = total + (move(part) if move else part)
        for r in range(8):
            out_ref[r, 16 * c : 16 * c + 16, :] = total[:, 256 * r : 256 * r + 256]


def part_kernel(in_ref, part_ref):
    total = in_ref[0, 32:40, :]
    for r in range(1, 8):
        total = total + in_ref[r, 32:40, :]
    ten = jnp.concatenate([total[:, 0:128], total[0:2, 128:256]], 0)
    for d in range(COLS):
        part_ref[10 * d : 10 * d + 10, :] = ten


def final_kernel(result_ref, in_ref, out_ref, first_ref, second_ref, bias_ref):
    total = in_ref[0:10, :]
    for d in range(1, COLS):
        total = total + in_ref[10 * d : 10 * d + 10, :]
    total = total * (1.0 / math.sqrt(NX * NY))
    moved = [total] + [pltpu.roll(total, 128 - 32 * g, 1) for g in range(1, 4)]
    first_ref[0:10, :] = moved[0][:, 0:32]
    first_ref[10:18, :] = moved[1][0:8, 0:32]
    bias_ref[...] = moved[1][8:9, 0:32]
    second_ref[0:1, :] = moved[1][9:10, 0:32]
    second_ref[1:11, :] = moved[2][:, 0:32]
    second_ref[11:18, :] = moved[3][0:7, 0:32]
    for c in range(2):
        lines = jnp.concatenate([result_ref[r, 16 * c : 16 * c + 16, :] for r in range(8)], 0)
        out_ref[c] = lines.T


def call(kernel, outs, scratch=(), scalars=0, count=0, name=None, remote=0, mib=8):
    space = [pl.BlockSpec(memory_space=pltpu.SMEM)] * scalars
    space += [pl.BlockSpec(memory_space=pltpu.HBM)] * remote
    space += [pl.BlockSpec(memory_space=pltpu.VMEM)] * (count - scalars - remote)
    many = isinstance(outs, (list, tuple))
    out_space = pl.BlockSpec(memory_space=pltpu.VMEM)
    return pl.pallas_call(
        kernel,
        out_shape=outs,
        in_specs=space,
        out_specs=[out_space] * len(outs) if many else out_space,
        scratch_shapes=list(scratch),
        compiler_params=pltpu.CompilerParams(vmem_limit_bytes=mib * 2**20),
        name=name,
    )


def shape(*dims, dtype=f32):
    return jax.ShapeDtypeStruct(dims, dtype)


def shards(state, cotangent, first_kernel, first_bias, second_kernel):
    t = tables()
    first_pick, second_pick, first_take, second_take = picks()
    dft, group, twist_y, twist_x = (
        jnp.asarray(t[k]) for k in ("dft", "group", "twist_y", "twist_x")
    )
    every = ("col", "row")
    place = (lax.axis_index("col") * ROWS + lax.axis_index("row")).astype(jnp.int32).reshape(1)

    def exchange(values, axis):
        return lax.all_to_all(values, axis, 0, 0, tiled=True)

    space = [pltpu.VMEM((4, 256, 128), f32), pltpu.SemaphoreType.DMA((5,))]
    packed, twist_x = call(
        pack_kernel, [shape(8, 64, 256), shape(8, 256)], space, count=3, name="pack", remote=3
    )(far(cotangent), far(state), far(twist_x))
    lines = exchange(packed, "row")
    modes, low, high = call(
        ahead_kernel, [shape(512, 128), shape(4, NX), shape(4, NX)],
        count=3, name="ahead",
    )(dft, twist_x, lines)
    order = [(i % ROWS) * COLS + i // ROWS for i in range(DEV)]
    up = [(order[i], order[(i + 1) % DEV]) for i in range(DEV)]
    before = lax.ppermute(high, ("row", "col"), up)
    after = lax.ppermute(low, ("row", "col"), [(j, i) for i, j in up])
    modes = exchange(modes.reshape(DEV, 1, 256), every).reshape(512, 128)
    prepared = call(
        bands_kernel,
        [
            shape(576, 160, dtype=bf16), shape(576, 160, dtype=bf16), shape(160, 576, dtype=bf16),
        ],
        [
            pltpu.VMEM((576, 256), f32), pltpu.VMEM((576, 256), f32),
            pltpu.VMEM((18, FEATS), bf16), pltpu.VMEM((18, FEATS), bf16),
            pltpu.VMEM((1, FEATS), f32), pltpu.VMEM((2, 18, 256), bf16),
            pltpu.SemaphoreType.DMA((4,)),
        ],
        count=4,
        remote=4,
        name="bands",
    )(
        far(first_kernel), far(second_kernel.T), far(first_bias.reshape(1, FEATS)),
        far(jnp.asarray(np.stack([first_pick, second_pick]))),
    )
    modes, prepared, before, after = lax.optimization_barrier((modes, prepared, before, after))
    modes = call(middle_kernel, shape(768, 128), scalars=1, count=5, name="middle")(place, dft, twist_y, group, modes)
    modes = exchange(modes.reshape(DEV, 1, 384), every).reshape(768, 128)
    scratch = [
        pltpu.VMEM((2, WIDE, NX), f32),
        pltpu.VMEM((2, WIDE, NX), f32),
        pltpu.VMEM((160, NX), f32),
        pltpu.VMEM((256, NX), bf16),
        pltpu.VMEM((256, NX), bf16),
        pltpu.VMEM((576, NX), bf16),
        pltpu.VMEM((512, NX), bf16),
    ]
    result = call(
        closure_kernel, shape(8, 40, 256), scratch, count=11, name="closure", mib=40
    )(*prepared, lines, before, after, dft, twist_x, first_take, second_take, modes)
    result = exchange(result, "row")
    part = call(part_kernel, shape(320, 128), count=1, name="part")(result)
    part = exchange(part.reshape(COLS, 1, 1280), "col").reshape(320, 128)
    grad_state, grad_first, grad_second, grad_bias = call(
        final_kernel,
        [shape(2, 256, 128), shape(18, 32), shape(18, 32), shape(1, 32)],
        count=2,
        name="final",
    )(result, part)
    return grad_state, grad_first, grad_second.T, grad_bias.reshape(32)


def solution(mesh):
    placed = (P(None, "row", "col"), P(None, "row", "col"), P(), P(), P())
    return jax.shard_map(
        shards,
        mesh=mesh,
        in_specs=placed,
        out_specs=(P(None, "row", "col"), P(), P(), P()),
        check_vma=False,
    )
```

```python
import math

import jax
import jax.numpy as jnp
import numpy as np
from jax import lax
from jax.experimental import pallas as pl
from jax.experimental.pallas import tpu as pltpu
from jax.sharding import PartitionSpec as P


NX, NY = 2048, 4096
ROWS, COLS = 8, 32
DEV = ROWS * COLS
FEATS = 32
WIDE = 24
f32, bf16 = jnp.float32, jnp.bfloat16
STEP = 0.1
NT = (((1,), (1,)), ((), ()))
NN = (((1,), (0,)), ((), ()))


def pair(table):
    high = table.astype(jnp.bfloat16)
    low = (table - high.astype(np.float64)).astype(jnp.bfloat16)
    return np.stack([high, low])


def tables():
    index = np.arange(256)
    angle = 2 * np.pi * (np.outer(index, index) % 256) / 256
    dft = pair(np.concatenate([np.cos(angle), np.sin(angle)]))
    small = 2 * np.pi * (np.outer(np.arange(16), np.arange(16)) % 16) / 16
    eye = np.eye(8)
    group = np.concatenate([np.kron(eye, np.cos(small)), np.kron(eye, np.sin(small))], 1)
    twist_y = 2 * np.pi * np.outer(index, np.arange(128) % 16) / NY
    twist_x = 2 * np.pi * np.outer(np.arange(1, 5), index) / NX
    return dict(
        dft=dft,
        group=pair(group),
        twist_y=np.stack([np.cos(twist_y), np.sin(twist_y)]).astype(np.float32),
        twist_x=np.concatenate([np.cos(twist_x), np.sin(twist_x)]).astype(np.float32),
    )


def picks():
    first = np.zeros((18, 256))
    second = np.zeros((18, 256))
    out_first = np.zeros((256, 128))
    out_second = np.zeros((256, 128))
    for a in range(3):
        for b in range(3):
            for c in range(2):
                row = 2 * (3 * a + b) + c
                lane = (2 * a + c) * WIDE
                first[row, lane + b] = 1
                second[row, lane + 2 - b] = 1
                out_first[lane + b, row] = 1
                out_second[lane + 2 - b, 19 + row] = 1
    out_first[6 * WIDE, 18] = 1
    return [x.astype(jnp.bfloat16) for x in (first, second, out_first, out_second)]


def split(values):
    high = values.astype(bf16)
    return high, (values - high.astype(f32)).astype(bf16)


def dot(left, right, dims=NN):
    return lax.dot_general(left, right, dims, preferred_element_type=f32)


def left_dot(table_ref, values, dims=NN):
    high, low = split(values)
    dim = dims[0][1][0] ^ 1
    size = values.shape[dim]
    wide = dot(table_ref[0], jnp.concatenate([high, low], dim), dims)
    both = wide[:, :size] + (wide[:, size:] + dot(table_ref[1], high, dims))
    return both[:256], both[256:]


def apart_dot(table_ref, values):
    high, low = split(values)
    parts = []
    for k in (0, 256):
        t_high, t_low = table_ref[0, k : k + 256, :], table_ref[1, k : k + 256, :]
        parts.append(dot(t_high, high) + (dot(t_high, low) + dot(t_low, high)))
    return parts


def right_apart(values, table_ref):
    high, low = split(values)
    return dot(high, table_ref[0]) + (dot(low, table_ref[0]) + dot(high, table_ref[1]))


def right_dot(values, high_table, low_table, dims=NN):
    high, low = split(values)
    size = values.shape[0]
    tall = dot(jnp.concatenate([high, low], 0), high_table, dims)
    return tall[:size] + (tall[size:] + dot(high, low_table, dims))


def far(values):
    return pltpu.with_memory_space_constraint(values, pltpu.HBM)


def pack_kernel(cot_ref, state_ref, twist_far, out_ref, twist_ref, buffer_ref, sems):
    copies = []
    twist_copy = pltpu.make_async_copy(twist_far, twist_ref, sems.at[4])
    for f, ref in enumerate((cot_ref, state_ref)):
        for c in range(2):
            k = 2 * f + c
            copies.append(pltpu.make_async_copy(ref.at[c], buffer_ref.at[k], sems.at[k]))
    for copy in copies:
        copy.start()
    twist_copy.start()
    for k, copy in enumerate(copies):
        copy.wait()
        turned = buffer_ref[k].T
        for r in range(ROWS):
            out_ref[r, 16 * k : 16 * k + 16, :] = turned[16 * r : 16 * r + 16]
    twist_copy.wait()


def ahead_kernel(dft_ref, twist_ref, in_ref, out_ref, low_ref, high_ref):
    u = [in_ref[r, 0:32, :] for r in range(8)]
    root = math.sqrt(0.5)
    a, b, c, d = (u[k] - u[k + 4] for k in range(4))
    e0, e1, e2, e3 = (u[k] + u[k + 4] for k in range(4))
    s0, s1 = e0 + e2, e1 + e3
    parts = [
        (a + root * (b - d), -c - root * (b + d)),
        (e0 - e2, e3 - e1),
        (a - root * (b - d), c - root * (b + d)),
    ]
    reals, imags = [], []
    for k, (re, im) in enumerate(parts):
        cos, sin = twist_ref[k : k + 1, :], twist_ref[4 + k : 5 + k, :]
        reals.append(re * cos + im * sin)
        imags.append(im * cos - re * sin)
    even, odd = s0 + s1, s0 - s1
    zero = jnp.zeros_like(even)
    last_re = odd * twist_ref[3:4, :]
    last_im = -odd * twist_ref[7:8, :]
    stack = jnp.concatenate(
        reals + [even] + imags + [zero] + [zero] * 3 + [last_re] + [zero] * 3 + [last_im], 0
    )
    cosine, sine = left_dot(dft_ref, stack, NT)
    main_re = cosine[:, 0:128] + sine[:, 128:256]
    main_im = cosine[:, 128:256] - sine[:, 0:128]
    odd_re = cosine[:128, 256:384] + sine[:128, 384:512]
    odd_im = cosine[:128, 384:512] - sine[:128, 256:384]
    lane = lax.broadcasted_iota(jnp.int32, (128, 128), 1)
    row = lax.broadcasted_iota(jnp.int32, (128, 128), 0)
    last = lane >= 96
    edge = last & (row == 0)
    top_re = jnp.where(edge, main_re[128:129], main_re[:128])
    top_im = jnp.where(edge, main_re[0:1], main_im[:128])
    out_ref[pl.ds(0, 128, 2), :] = top_re
    out_ref[pl.ds(1, 128, 2), :] = top_im
    out_ref[pl.ds(256, 128, 2), :] = jnp.where(last, odd_re, main_re[128:])
    out_ref[pl.ds(257, 128, 2), :] = jnp.where(last, odd_im, main_im[128:])
    for r in range(8):
        for ch in range(2):
            row0 = 32 + 16 * ch
            low_ref[2 * ch : 2 * ch + 2, 256 * r : 256 * r + 256] = in_ref[r, row0 : row0 + 2, :]
            high_ref[2 * ch : 2 * ch + 2, 256 * r : 256 * r + 256] = in_ref[
                r, row0 + 14 : row0 + 16, :
            ]


def waves(place):
    lane = lax.broadcasted_iota(jnp.int32, (256, 128), 1)
    row = lax.broadcasted_iota(jnp.int32, (256, 128), 0)
    slot = lane // 32
    plain = 8 * place + slot + 1
    last = jnp.where(place == 0, NX // 2, jnp.where(place < 128, 8 * place, 8 * place - 1020))
    mx = jnp.where(slot == 3, last, plain)
    mx = jnp.where(mx >= NX // 2, mx - NX, mx)
    my = row + 256 * (lane % 16)
    my = jnp.where(my >= NY // 2, my - NY, my)
    kx = mx.astype(f32) * (1.0 / NX)
    ky = my.astype(f32) * (1.0 / NY)
    inverse = 1.0 / (kx * kx + ky * ky)
    cross = jnp.where((mx == -(NX // 2)) | (my == -(NY // 2)), 0.0, kx * ky)
    own = jnp.where((lane & 16) == 0, kx * kx, ky * ky)
    return 1.0 - own * inverse, -cross * inverse, lane


def swap16(values, lane):
    return jnp.where((lane & 16) == 0, pltpu.roll(values, 112, 1), pltpu.roll(values, 16, 1))


def middle_kernel(
    place_ref, dft_ref, twist_ref, group_ref, in_ref, out_ref
):
    place = place_ref[0]
    re, im = in_ref[pl.ds(0, 256, 2), :], in_ref[pl.ds(1, 256, 2), :]
    both = jnp.concatenate([re, im], 1)
    cosine, sine = apart_dot(dft_ref, both)
    f_re, f_im = cosine[:, :128] + sine[:, 128:], cosine[:, 128:] - sine[:, :128]
    cos, sin = twist_ref[0], twist_ref[1]
    t_re, t_im = f_re * cos + f_im * sin, f_im * cos - f_re * sin
    g = right_apart(jnp.concatenate([t_re, t_im], 0), group_ref)
    g_re, g_im = g[:256, :128] + g[256:, 128:], g[256:, :128] - g[:256, 128:]
    keep, mix, lane = waves(place)
    p_re = keep * g_re + mix * swap16(g_re, lane)
    p_im = keep * g_im + mix * swap16(g_im, lane)
    h = right_apart(jnp.concatenate([p_re, p_im], 0), group_ref)
    h_re, h_im = h[:256, :128] - h[256:, 128:], h[256:, :128] + h[:256, 128:]
    t_re, t_im = h_re * cos - h_im * sin, h_im * cos + h_re * sin
    both = jnp.concatenate([t_re, t_im], 1)
    cosine, sine = apart_dot(dft_ref, both)
    scale = 1.0 / (NX * NY)
    o_re = (cosine[:, :128] - sine[:, 128:]) * scale
    o_im = (cosine[:, 128:] + sine[:, :128]) * scale
    sums = jnp.sum(im, 0, keepdims=True)
    sums = jnp.where(lane[:1] >= 112, sums, 0.0)
    mean = jnp.sum(sums, 1, keepdims=True) * scale
    zeroth = (lane >= 96) & (place == 0)
    o_im = jnp.where(zeroth, jnp.where(lane >= 112, mean, im * (1.0 / NX)), o_im)
    near = (lane & 8) == 0
    outer = ((lane + 2) & 15) < 4

    def beside(values):
        return jnp.where(near, pltpu.roll(values, 255, 0), pltpu.roll(values, 1, 0))

    out_ref[pl.ds(0, 256, 3), :] = o_re
    out_ref[pl.ds(1, 256, 3), :] = o_im
    edge_im = beside(o_im)
    edge_im = jnp.where(near, pltpu.roll(edge_im, 4, 1), pltpu.roll(edge_im, 124, 1))
    out_ref[pl.ds(2, 256, 3), :] = jnp.where(outer, beside(o_re), edge_im)


def back_part(in_ref, dft_ref, twist_ref, out_ref):
    lane = lax.broadcasted_iota(jnp.int32, (128, 128), 1)
    row = lax.broadcasted_iota(jnp.int32, (128, 128), 0)
    last = lane >= 96
    edge = last & (row == 0)
    near = (lane & 8) == 0
    outer = ((lane + 2) & 15) < 4
    top_re, top_im, top_h = (in_ref[pl.ds(k, 128, 3), :] for k in range(3))
    low_re, low_im, low_h = (in_ref[pl.ds(384 + k, 128, 3), :] for k in range(3))
    head = top_h[0:1]
    head_im = jnp.where(near[0:1], pltpu.roll(head, 124, 1), pltpu.roll(head, 4, 1))
    half_im = jnp.where(outer[0:1], 0.5 * head_im, 0.0)
    half_re = jnp.where(outer[0:1], 0.5 * head, 0.0)
    nyquist = jnp.where(edge, 0.5 * top_re[0:1], 0.0)
    mains = [
        jnp.concatenate(
            [jnp.where(edge, 0.5 * top_im, top_re), jnp.where(last, nyquist, low_re)], 0
        ),
        jnp.concatenate([jnp.where(edge, 0.0, top_im), jnp.where(last, 0.0, low_im)], 0),
        jnp.concatenate(
            [
                jnp.where(edge, half_im, top_h),
                jnp.where(last, jnp.where(edge, half_re, 0.0), low_h),
            ],
            0,
        ),
    ]
    main = right_dot(jnp.concatenate(mains, 1).T, dft_ref[0], dft_ref[1], NT)
    odd = jnp.concatenate([low_re, low_im, low_h], 1).T
    odd = jnp.concatenate([odd[128 * k + 96 : 128 * k + 128] for k in range(3)], 0)
    odd = right_dot(odd, dft_ref[0][:, :128], dft_ref[1][:, :128], NT)
    m_cos, m_sin, o_cos, o_sin = main[:, :256], main[:, 256:], odd[:, :256], odd[:, 256:]
    root = math.sqrt(0.5)

    def imag_rows(values):
        rows = values.shape[0]
        near_row = (lax.broadcasted_iota(jnp.int32, values.shape, 0) & 8) == 0
        return jnp.where(near_row, pltpu.roll(values, rows - 4, 0), pltpu.roll(values, 4, 0))

    for k in (0, 256):
        if k == 0:
            re, im = m_cos[0:128] - m_sin[128:256], m_cos[128:256] + m_sin[0:128]
            last_re, last_im = o_cos[0:32] - o_sin[32:64], o_cos[32:64] + o_sin[0:32]
        else:
            m_c, m_s, o_c, o_s = m_cos[256:384], m_sin[256:384], o_cos[64:96], o_sin[64:96]
            re, im = m_c - imag_rows(m_s), imag_rows(m_c) + m_s
            last_re, last_im = o_c - imag_rows(o_s), imag_rows(o_c) + o_s
        w4 = last_re * twist_ref[3:4, :] - last_im * twist_ref[7:8, :]
        w0 = re[96:128]
        ws = []
        for p in range(3):
            cos, sin = twist_ref[p : p + 1, :], twist_ref[4 + p : 5 + p, :]
            r_p, i_p = re[32 * p : 32 * p + 32], im[32 * p : 32 * p + 32]
            ws.append((r_p * cos - i_p * sin, i_p * cos + r_p * sin))
        for r in range(8):
            total = w0 + w4 if r % 2 == 0 else w0 - w4
            for p in range(3):
                turn_by = (r * (p + 1)) % 8
                cos_r = [1.0, root, 0.0, -root, -1.0, -root, 0.0, root][turn_by]
                sin_r = [0.0, root, 1.0, root, 0.0, -root, -1.0, -root][turn_by]
                if cos_r:
                    total = total + cos_r * ws[p][0]
                if sin_r:
                    total = total - sin_r * ws[p][1]
            total = total + total
            lanes = slice(256 * r, 256 * r + 256)
            for ch in range(2):
                if k == 0:
                    out_ref[ch, 2:18, lanes] = total[16 * ch : 16 * ch + 16]
                else:
                    out_ref[ch, 0:2, lanes] = total[16 * ch + 14 : 16 * ch + 16]
                    out_ref[ch, 18:20, lanes] = total[16 * ch : 16 * ch + 2]
                    if r == 0:
                        out_ref[ch, 20:24, :] = jnp.zeros((4, NX), f32)


def ahead_of(values):
    return pltpu.roll(values, NX - 1, 1)


def behind_of(values):
    return pltpu.roll(values, 1, 1)


def fill_taps(build_ref, target, fields, sign):
    for c in range(2):
        whole = fields[c]
        moves = (behind_of(whole), whole, ahead_of(whole))[::sign]
        for a in range(3):
            row = (2 * a + c) * WIDE
            build_ref[row : row + WIDE, :] = moves[a]
    build_ref[144:152, :] = jnp.ones((8, NX), f32)
    build_ref[152:160, :] = jnp.zeros((8, NX), f32)
    target[0:160, :] = build_ref[...].astype(bf16)


def bands_kernel(
    first_far, second_far, bias_far, pick_far,
    w1_out, w2_out, turn_ref,
    w1_ref, w2_ref, first_ref, second_ref, bias_ref, pick_ref, sems,
):
    copies = [
        pltpu.make_async_copy(source, target, sems.at[k])
        for k, (source, target) in enumerate(
            (
                (first_far, first_ref), (second_far, second_ref),
                (bias_far, bias_ref), (pick_far, pick_ref),
            )
        )
    ]
    for copy in copies:
        copy.start()
    for copy in copies:
        copy.wait()
    lane = lax.broadcasted_iota(jnp.int32, (FEATS, 256), 1)
    square = lax.broadcasted_iota(jnp.int32, (FEATS, FEATS), 0)
    own = square == lax.broadcasted_iota(jnp.int32, (FEATS, FEATS), 1)
    bias = jnp.sum(jnp.where(own, bias_ref[...], 0.0), 1, keepdims=True)
    bias_high = bias.astype(bf16).astype(f32)
    bias_part = jnp.where(
        lane == 6 * WIDE, bias_high, jnp.where(lane == 6 * WIDE + 1, bias - bias_high, 0.0)
    )
    base1 = dot(first_ref[...].astype(f32).T.astype(bf16), pick_ref[0])
    base2 = dot(second_ref[...].astype(f32).T.astype(bf16), pick_ref[1])
    for j in range(18):
        rows = slice(32 * j, 32 * j + 32)
        moved1 = pltpu.roll(base1, j, 1) if j else base1
        moved2 = pltpu.roll(base2, j, 1) if j else base2
        w1_ref[rows, :] = moved1 + bias_part
        w2_ref[rows, :] = moved2
    w1 = w1_ref[...]
    turn_ref[...] = w1.T[:160].astype(bf16)
    w1_out[...] = w1[:, :160].astype(bf16)
    w2_out[...] = w2_ref[:, :160].astype(bf16)


def closure_kernel(
    w1_ref, w2_ref, turn_ref, own_ref, before_ref, after_ref,
    dft_ref, twist_ref, take1_ref, take2_ref, in_ref,
    out_ref,
    field_ref, proj_ref, build_ref, state_low, scaled_low, grads, acts,
):
    for c in range(2):
        field_ref[c, 20:24, :] = jnp.zeros((4, NX), f32)
        for r in range(8):
            field_ref[c, 2:18, 256 * r : 256 * r + 256] = own_ref[
                r, 32 + 16 * c : 48 + 16 * c, :
            ]
        field_ref[c, 0:2, :] = before_ref[2 * c : 2 * c + 2, :]
        field_ref[c, 18:20, :] = after_ref[2 * c : 2 * c + 2, :]
    fill_taps(build_ref, state_low, (field_ref[0], field_ref[1]), 1)
    back_part(in_ref, dft_ref, twist_ref, proj_ref)
    state_low[160:256, :] = jnp.zeros((96, NX), bf16)
    scaled_low[160:256, :] = jnp.zeros((96, NX), bf16)
    fill_taps(build_ref, scaled_low, (STEP * proj_ref[0], STEP * proj_ref[1]), -1)
    active = jnp.tanh(dot(w1_ref[...], state_low[0:160, :]))
    acts[...] = active[32:544].astype(bf16)
    back = dot(w2_ref[...], scaled_low[0:160, :])
    grads[...] = (back * (1.0 - active * active)).astype(bf16)
    build_ref[...] = dot(turn_ref[...], grads[...])
    first_sums = dot(grads[32:544, :], state_low[...], NT)
    second_sums = dot(acts[...], scaled_low[...], NT)
    lane = lax.broadcasted_iota(jnp.int32, (FEATS, 256), 1)
    total1 = total2 = plain = jnp.zeros((FEATS, 256), f32)
    for j in range(16):
        rows = slice(32 * j, 32 * j + 32)
        total1 = total1 + pltpu.roll(first_sums[rows], 255 - j, 1)
        total2 = total2 + pltpu.roll(second_sums[rows], 255 - j, 1)
        plain = plain + first_sums[rows]
    total1 = jnp.where(lane >= 6 * WIDE, plain, total1)
    high1, low1 = split(total1)
    high2, low2 = split(total2)
    packed = (dot(high1, take1_ref[...]) + dot(low1, take1_ref[...])) + (
        dot(high2, take2_ref[...]) + dot(low2, take2_ref[...])
    )
    turned = jnp.concatenate([packed, jnp.zeros((96, 128), f32)], 0).T
    ten = turned[0:10]
    for g in range(1, 4):
        ten = ten + pltpu.roll(turned[10 * g : 10 * g + 10], 32 * g, 1)
    for r in range(8):
        out_ref[r, 32:40, 0:128] = ten[0:8]
        out_ref[r, 32:34, 128:256] = ten[8:10]
        out_ref[r, 34:40, 128:256] = jnp.zeros((6, 128), f32)

    inner, up, down = slice(2, 18), slice(3, 19), slice(1, 17)
    su = field_ref[0, inner, :]
    along_x, along_y = [], []
    for c in range(2):
        mine = field_ref[c, inner, :]
        along_x.append(0.5 * (ahead_of(mine) - behind_of(mine)))
        along_y.append(0.5 * (field_ref[c, up, :] - field_ref[c, down, :]))
    along = (along_x, along_y)
    centre = [STEP * proj_ref[c, inner, :] for c in range(2)]
    for c in range(2):
        mine = centre[c]
        above = STEP * proj_ref[c, up, :]
        below = STEP * proj_ref[c, down, :]
        carried = su * mine
        total = 0.5 * (ahead_of(carried) - behind_of(carried))
        total = total + 0.5 * (field_ref[1, up, :] * above - field_ref[1, down, :] * below)
        total = total - (centre[0] * along[c][0] + centre[1] * along[c][1])
        total = total + (ahead_of(mine) + behind_of(mine) + above + below - 4.0 * mine)
        total = total + proj_ref[c, inner, :]
        for a, move in enumerate((ahead_of, None, behind_of)):
            row = (2 * a + c) * WIDE
            part = build_ref[row + 2 : row + 18, :]
            total = total + (move(part) if move else part)
        for r in range(8):
            out_ref[r, 16 * c : 16 * c + 16, :] = total[:, 256 * r : 256 * r + 256]


def part_kernel(in_ref, part_ref):
    total = in_ref[0, 32:40, :]
    for r in range(1, 8):
        total = total + in_ref[r, 32:40, :]
    ten = jnp.concatenate([total[:, 0:128], total[0:2, 128:256]], 0)
    for d in range(COLS):
        part_ref[10 * d : 10 * d + 10, :] = ten


def final_kernel(result_ref, in_ref, out_ref, first_ref, second_ref, bias_ref):
    total = in_ref[0:10, :]
    for d in range(1, COLS):
        total = total + in_ref[10 * d : 10 * d + 10, :]
    total = total * (1.0 / math.sqrt(NX * NY))
    moved = [total] + [pltpu.roll(total, 128 - 32 * g, 1) for g in range(1, 4)]
    first_ref[0:10, :] = moved[0][:, 0:32]
    first_ref[10:18, :] = moved[1][0:8, 0:32]
    bias_ref[...] = moved[1][8:9, 0:32]
    second_ref[0:1, :] = moved[1][9:10, 0:32]
    second_ref[1:11, :] = moved[2][:, 0:32]
    second_ref[11:18, :] = moved[3][0:7, 0:32]
    for c in range(2):
        lines = jnp.concatenate([result_ref[r, 16 * c : 16 * c + 16, :] for r in range(8)], 0)
        out_ref[c] = lines.T


def call(kernel, outs, scratch=(), scalars=0, count=0, remote=0, mib=8):
    space = [pl.BlockSpec(memory_space=pltpu.SMEM)] * scalars
    space += [pl.BlockSpec(memory_space=pltpu.HBM)] * remote
    space += [pl.BlockSpec(memory_space=pltpu.VMEM)] * (count - scalars - remote)
    many = isinstance(outs, (list, tuple))
    out_space = pl.BlockSpec(memory_space=pltpu.VMEM)
    return pl.pallas_call(
        kernel,
        out_shape=outs,
        in_specs=space,
        out_specs=[out_space] * len(outs) if many else out_space,
        scratch_shapes=list(scratch),
        compiler_params=pltpu.CompilerParams(vmem_limit_bytes=mib * 2**20),
    )


def shape(*dims, dtype=f32):
    return jax.ShapeDtypeStruct(dims, dtype)


def shards(state, cotangent, first_kernel, first_bias, second_kernel):
    t = tables()
    first_pick, second_pick, first_take, second_take = picks()
    dft, group, twist_y, twist_x = (
        jnp.asarray(t[k]) for k in ("dft", "group", "twist_y", "twist_x")
    )
    every = ("col", "row")
    place = (lax.axis_index("col") * ROWS + lax.axis_index("row")).astype(jnp.int32).reshape(1)

    def exchange(values, axis):
        return lax.all_to_all(values, axis, 0, 0, tiled=True)

    space = [pltpu.VMEM((4, 256, 128), f32), pltpu.SemaphoreType.DMA((5,))]
    packed, twist_x = call(
        pack_kernel, [shape(8, 64, 256), shape(8, 256)], space, count=3, remote=3
    )(far(cotangent), far(state), far(twist_x))
    lines = exchange(packed, "row")
    modes, low, high = call(
        ahead_kernel, [shape(512, 128), shape(4, NX), shape(4, NX)],
        count=3,
    )(dft, twist_x, lines)
    order = [(i % ROWS) * COLS + i // ROWS for i in range(DEV)]
    up = [(order[i], order[(i + 1) % DEV]) for i in range(DEV)]
    before = lax.ppermute(high, ("row", "col"), up)
    after = lax.ppermute(low, ("row", "col"), [(j, i) for i, j in up])
    modes = exchange(modes.reshape(DEV, 1, 256), every).reshape(512, 128)
    prepared = call(
        bands_kernel,
        [
            shape(576, 160, dtype=bf16), shape(576, 160, dtype=bf16), shape(160, 576, dtype=bf16),
        ],
        [
            pltpu.VMEM((576, 256), f32), pltpu.VMEM((576, 256), f32),
            pltpu.VMEM((18, FEATS), bf16), pltpu.VMEM((18, FEATS), bf16),
            pltpu.VMEM((1, FEATS), f32), pltpu.VMEM((2, 18, 256), bf16),
            pltpu.SemaphoreType.DMA((4,)),
        ],
        count=4,
        remote=4,
    )(
        far(first_kernel), far(second_kernel.T), far(first_bias.reshape(1, FEATS)),
        far(jnp.asarray(np.stack([first_pick, second_pick]))),
    )
    modes, prepared = lax.optimization_barrier((modes, prepared))
    modes = call(middle_kernel, shape(768, 128), scalars=1, count=5)(place, dft, twist_y, group, modes)
    modes, before, after = lax.optimization_barrier((modes, before, after))
    modes = exchange(modes.reshape(DEV, 1, 384), every).reshape(768, 128)
    scratch = [
        pltpu.VMEM((2, WIDE, NX), f32),
        pltpu.VMEM((2, WIDE, NX), f32),
        pltpu.VMEM((160, NX), f32),
        pltpu.VMEM((256, NX), bf16),
        pltpu.VMEM((256, NX), bf16),
        pltpu.VMEM((576, NX), bf16),
        pltpu.VMEM((512, NX), bf16),
    ]
    result = call(
        closure_kernel, shape(8, 40, 256), scratch, count=11, mib=40
    )(*prepared, lines, before, after, dft, twist_x, first_take, second_take, modes)
    result = exchange(result, "row")
    part = call(part_kernel, shape(320, 128), count=1)(result)
    part = exchange(part.reshape(COLS, 1, 1280), "col").reshape(320, 128)
    grad_state, grad_first, grad_second, grad_bias = call(
        final_kernel, [shape(2, 256, 128), shape(18, 32), shape(18, 32), shape(1, 32)], count=2
    )(result, part)
    return grad_state, grad_first, grad_second.T, grad_bias.reshape(32)


def solution(mesh):
    placed = (P(None, "row", "col"), P(None, "row", "col"), P(), P(), P())
    return jax.shard_map(
        shards,
        mesh=mesh,
        in_specs=placed,
        out_specs=(P(None, "row", "col"), P(), P(), P()),
        check_vma=False,
    )
```
